32 devices in a mesh: dp: 8 (over z, x), seq: 4 (over y, core).
Axes of the slice: x: 2, y: 2, z: 4, core: 2. Of those that a mesh axis runs over, the one named last changes fastest.
Arguments:
- pixels: bfloat16 [16, 1024, 768], P('dp', 'seq'), may hold values from -6 to 6
- lengths: int32 [16, 3], P('dp'), may hold values from 66 to 578, as said below
- labels: int32 [16, 3], P('dp'), may hold values from 0 to 999
- teacher: float32 [16, 3, 1000], P('dp'), may hold values from -15 to 15
- embedder: float32 [768, 768], P(('dp', 'seq')), may hold values from -0.21875 to 0.21875
- embedder_mean: float32 [768, 768], P(('dp', 'seq')), may hold values from -1.1444092e-05 to 1.1444092e-05
- embedder_square: float32 [768, 768], P(('dp', 'seq')), may hold values from 2.7144834e-13 to 1.0857933e-12
- attend: float32 [1, 768, 2304], P(None, ('dp', 'seq')), may hold values from -0.21875 to 0.21875
- attend_mean: float32 [1, 768, 2304], P(None, ('dp', 'seq')), may hold values from -1.1444092e-05 to 1.1444092e-05
- attend_square: float32 [1, 768, 2304], P(None, ('dp', 'seq')), may hold values from 2.7144834e-13 to 1.0857933e-12
- merger: float32 [1, 768, 768], P(None, ('dp', 'seq')), may hold values from -0.875 to 0.875
- merger_mean: float32 [1, 768, 768], P(None, ('dp', 'seq')), may hold values from -1.1444092e-05 to 1.1444092e-05
- merger_square: float32 [1, 768, 768], P(None, ('dp', 'seq')), may hold values from 2.7144834e-13 to 1.0857933e-12
- expand: float32 [1, 768, 3072], P(None, ('dp', 'seq')), may hold values from -0.21875 to 0.21875
- expand_mean: float32 [1, 768, 3072], P(None, ('dp', 'seq')), may hold values from -1.1444092e-05 to 1.1444092e-05
- expand_square: float32 [1, 768, 3072], P(None, ('dp', 'seq')), may hold values from 2.7144834e-13 to 1.0857933e-12
- shrink: float32 [1, 3072, 768], P(None, ('dp', 'seq')), may hold values from -0.109375 to 0.109375
- shrink_mean: float32 [1, 3072, 768], P(None, ('dp', 'seq')), may hold values from -1.1444092e-05 to 1.1444092e-05
- shrink_square: float32 [1, 3072, 768], P(None, ('dp', 'seq')), may hold values from 2.7144834e-13 to 1.0857933e-12
- readout: float32 [2, 768, 1000], P(None, ('dp', 'seq')), may hold values from -0.21875 to 0.21875
- readout_mean: float32 [2, 768, 1000], P(None, ('dp', 'seq')), may hold values from -1.1444092e-05 to 1.1444092e-05
- readout_square: float32 [2, 768, 1000], P(None, ('dp', 'seq')), may hold values from 2.7144834e-13 to 1.0857933e-12
- vectors: float32 [8, 768], P(None, ('dp', 'seq')), may hold values from 0.5 to 1.5
- vectors_mean: float32 [8, 768], P(None, ('dp', 'seq')), may hold values from -4.5776367e-05 to 4.5776367e-05
- vectors_square: float32 [8, 768], P(None, ('dp', 'seq')), may hold values from 4.3431734e-12 to 1.7372694e-11
Outputs:
- embedder_next: float32 [768, 768], P(('dp', 'seq'))
- embedder_mean_next: float32 [768, 768], P(('dp', 'seq'))
- embedder_square_next: float32 [768, 768], P(('dp', 'seq'))
- attend_next: float32 [1, 768, 2304], P(None, ('dp', 'seq'))
- attend_mean_next: float32 [1, 768, 2304], P(None, ('dp', 'seq'))
- attend_square_next: float32 [1, 768, 2304], P(None, ('dp', 'seq'))
- merger_next: float32 [1, 768, 768], P(None, ('dp', 'seq'))
- merger_mean_next: float32 [1, 768, 768], P(None, ('dp', 'seq'))
- merger_square_next: float32 [1, 768, 768], P(None, ('dp', 'seq'))
- expand_next: float32 [1, 768, 3072], P(None, ('dp', 'seq'))
- expand_mean_next: float32 [1, 768, 3072], P(None, ('dp', 'seq'))
- expand_square_next: float32 [1, 768, 3072], P(None, ('dp', 'seq'))
- shrink_next: float32 [1, 3072, 768], P(None, ('dp', 'seq'))
- shrink_mean_next: float32 [1, 3072, 768], P(None, ('dp', 'seq'))
- shrink_square_next: float32 [1, 3072, 768], P(None, ('dp', 'seq'))
- readout_next: float32 [2, 768, 1000], P(None, ('dp', 'seq'))
- readout_mean_next: float32 [2, 768, 1000], P(None, ('dp', 'seq'))
- readout_square_next: float32 [2, 768, 1000], P(None, ('dp', 'seq'))
- vectors_mean_next: float32 [8, 768], P(None, ('dp', 'seq'))
- vectors_square_next: float32 [8, 768], P(None, ('dp', 'seq'))
- loss: float32 [], replicated
- grad_norm: float32 [], replicated
The draws below stay inside these ranges and needn't reach their ends.
Inputs may be any that keep to these rules, and one draw needn't show every extreme that they name: `lengths`: each row holds 3 images in order and then padding; in every row one image has exactly 578 tokens and the others at most (446) // 2.
All inputs are finite; a program needn't handle non-finite values.
Results may differ from the reference program's by a relative error of at most 0.006.
The reference program's roundings to bfloat16 on the way (of `weights`, `a`, `projected`, `mixed` and `class_norm`) count: a program that leaves them out, or rounds other values in their place, can miss the bound.
Values may be sent and summed in bfloat16 or wider, within the bound.
No kernel may reach another device: no remote copies, remote signals or barrier semaphores. Data moves between devices by JAX's collectives and lax.ppermute only.
A program may use at most 192 MiB of HBM per device.

```python
import math
import jax
import jax.numpy as jnp
from jax import lax

D = 768
HEADS = 12
HD = 64
FF = 3072
C = 1000
P_SIZE = 768
L = 1
ROW_LEN = 1024
IMGS = 3
MAXLEN = 578
MINLEN = 66
STEP_COUNT = 7
ROWS = 16
NIMG = 48
NVEC = 8
NPARAM = 9209856


def draw_lengths(key, part):
    first_key = jax.random.fold_in(key, 11)
    second_key = jax.random.fold_in(key, 12)
    others = jax.random.randint(first_key, (ROWS, IMGS), MINLEN, (ROW_LEN - MAXLEN) // (IMGS - 1) + 1)
    longest = jax.random.randint(second_key, (ROWS,), 0, IMGS)
    column = jnp.arange(IMGS)[None, :]
    result = jnp.where(column == longest[:, None], MAXLEN, others)
    spare_column = jnp.where(longest[0] == 0, 1, 0)
    row_index = jnp.arange(ROWS)[:, None]
    result = jnp.where((row_index == 0) & (column == spare_column), MINLEN, result)
    return result.astype(jnp.int32)


def set_ends(values, key, low, top_value):
    shape = values.shape
    spot = [jax.random.randint(jax.random.fold_in(key, axis), (), 0, shape[axis]) for axis in range(len(shape))]
    values = values.at[tuple(spot)].set(low)
    longest = shape.index(max(shape))
    spot[longest] = (spot[longest] + 1) % shape[longest]
    return values.at[tuple(spot)].set(top_value)


def block_scale(stream_key, dims, pieces, smallest, largest):
    factor_of, own = 1.0, jax.random.fold_in(stream_key, 6)
    for axis_at, shards_of in pieces:
        heights = jnp.exp(jax.random.uniform(jax.random.fold_in(own, axis_at), (shards_of,), jnp.float32, smallest / len(pieces), largest / len(pieces)))
        factor_of = factor_of * jnp.repeat(heights, dims[axis_at] // shards_of).reshape([-1 if axis == axis_at else 1 for axis in range(len(dims))])
    return factor_of


def bell_draw(rng, extent, scale, reach, pieces=(), kind=jnp.bfloat16):
    level = block_scale(rng, extent, pieces, -0.22, 0.18) if pieces else 1.0
    values = jax.random.normal(rng, extent, jnp.float32) * scale * level
    return jnp.minimum(jnp.maximum(values, -reach), reach).astype(kind)


def setup_inputs(seed: int = 0) -> dict:
    streams_of = jax.random.split(jax.random.key(seed), 26)
    return {
        "pixels": bell_draw(streams_of[0], (ROWS, ROW_LEN, P_SIZE), 1.0, 6.0, ((0, 8), (1, 4))),
        "lengths": draw_lengths(jax.random.fold_in(streams_of[25], 71), 0),
        "labels": set_ends(jax.random.randint(streams_of[2], (ROWS, IMGS), 0, C), jax.random.fold_in(streams_of[2], 1), 0, C - 1).astype(jnp.int32),
        "teacher": bell_draw(streams_of[3], (ROWS, IMGS, C), 3.0, 15.0, ((0, 8),), jnp.float32),
        "embedder": bell_draw(streams_of[4], (P_SIZE, D), P_SIZE ** -0.5, 0.21875, ((0, 32),), jnp.float32),
        "embedder_mean": bell_draw(streams_of[5], (P_SIZE, D), (0.0055 * NPARAM ** -0.5), 1.1444091796875e-05, ((0, 32),), jnp.float32),
        "embedder_square": jnp.clip(jnp.exp(math.log(1.0857933475938442e-12) - 1.3862944 * jax.random.uniform(streams_of[6], (P_SIZE, D), jnp.float32) ** block_scale(streams_of[6], (P_SIZE, D), ((0, 32),), -0.2, 0.2)), 2.7144833689846104e-13, 1.0857933475938442e-12),
        "attend": bell_draw(streams_of[7], (L, D, 3 * D), D ** -0.5, 0.21875, ((1, 32),), jnp.float32),
        "attend_mean": bell_draw(streams_of[8], (L, D, 3 * D), (0.0055 * NPARAM ** -0.5), 1.1444091796875e-05, ((1, 32),), jnp.float32),
        "attend_square": jnp.clip(jnp.exp(math.log(1.0857933475938442e-12) - 1.3862944 * jax.random.uniform(streams_of[9], (L, D, 3 * D), jnp.float32) ** block_scale(streams_of[9], (L, D, 3 * D), ((1, 32),), -0.2, 0.2)), 2.7144833689846104e-13, 1.0857933475938442e-12),
        "merger": bell_draw(streams_of[10], (L, D, D), (D // 16) ** -0.5, 0.875, ((1, 32),), jnp.float32),
        "merger_mean": bell_draw(streams_of[11], (L, D, D), (0.0055 * NPARAM ** -0.5), 1.1444091796875e-05, ((1, 32),), jnp.float32),
        "merger_square": jnp.clip(jnp.exp(math.log(1.0857933475938442e-12) - 1.3862944 * jax.random.uniform(streams_of[12], (L, D, D), jnp.float32) ** block_scale(streams_of[12], (L, D, D), ((1, 32),), -0.2, 0.2)), 2.7144833689846104e-13, 1.0857933475938442e-12),
        "expand": bell_draw(streams_of[13], (L, D, FF), D ** -0.5, 0.21875, ((1, 32),), jnp.float32),
        "expand_mean": bell_draw(streams_of[14], (L, D, FF), (0.0055 * NPARAM ** -0.5), 1.1444091796875e-05, ((1, 32),), jnp.float32),
        "expand_square": jnp.clip(jnp.exp(math.log(1.0857933475938442e-12) - 1.3862944 * jax.random.uniform(streams_of[15], (L, D, FF), jnp.float32) ** block_scale(streams_of[15], (L, D, FF), ((1, 32),), -0.2, 0.2)), 2.7144833689846104e-13, 1.0857933475938442e-12),
        "shrink": bell_draw(streams_of[16], (L, FF, D), FF ** -0.5, 0.109375, ((1, 32),), jnp.float32),
        "shrink_mean": bell_draw(streams_of[17], (L, FF, D), (0.0055 * NPARAM ** -0.5), 1.1444091796875e-05, ((1, 32),), jnp.float32),
        "shrink_square": jnp.clip(jnp.exp(math.log(1.0857933475938442e-12) - 1.3862944 * jax.random.uniform(streams_of[18], (L, FF, D), jnp.float32) ** block_scale(streams_of[18], (L, FF, D), ((1, 32),), -0.2, 0.2)), 2.7144833689846104e-13, 1.0857933475938442e-12),
        "readout": bell_draw(streams_of[19], (2, D, C), D ** -0.5, 0.21875, ((1, 32),), jnp.float32),
        "readout_mean": bell_draw(streams_of[20], (2, D, C), (0.0055 * NPARAM ** -0.5), 1.1444091796875e-05, ((1, 32),), jnp.float32),
        "readout_square": jnp.clip(jnp.exp(math.log(1.0857933475938442e-12) - 1.3862944 * jax.random.uniform(streams_of[21], (2, D, C), jnp.float32) ** block_scale(streams_of[21], (2, D, C), ((1, 32),), -0.2, 0.2)), 2.7144833689846104e-13, 1.0857933475938442e-12),
        "vectors": jnp.clip(1.0 + 0.1 * jax.random.normal(streams_of[22], (NVEC, D), jnp.float32), 0.5, 1.5),
        "vectors_mean": bell_draw(streams_of[23], (NVEC, D), (0.022 * NPARAM ** -0.5), 4.57763671875e-05, ((1, 32),), jnp.float32),
        "vectors_square": jnp.clip(jnp.exp(math.log(1.7372693561501507e-11) - 1.3862944 * jax.random.uniform(streams_of[24], (NVEC, D), jnp.float32) ** block_scale(streams_of[24], (NVEC, D), ((1, 32),), -0.2, 0.2)), 4.343173390375377e-12, 1.7372693561501507e-11),
    }


@jax.custom_vjp
def low(v):
    return lax.optimization_barrier(v.astype(jnp.bfloat16)).astype(jnp.float32)

@jax.custom_vjp
def low_back(v):
    return v

def low_keep(v):
    return (low(v), None)

def low_pass(kept, grad):
    return (grad,)

def back_keep(v):
    return (v, None)

def back_low(kept, grad):
    return (low(grad),)
low.defvjp(low_keep, low_pass)
low_back.defvjp(back_keep, back_low)
NORM_EPS = 1e-06
MASKED = -1000000000.0
SCALE = 0.125
BETA_ONE = 0.9
BETA_TWO = 0.999
ADAM_EPS = 1e-08
DECAY = 0.05
BASE_RATE = 0.05
LAYER_RATE = 0.75
CLIP_AT = 0.05
HIGH = lax.Precision.HIGHEST

def layer_norm(x, gain, shift):
    centre = x - lax.optimization_barrier(jnp.mean(x, -1, keepdims=True))
    spread = lax.optimization_barrier(jnp.mean(centre * centre, -1, keepdims=True))
    return centre * lax.rsqrt(spread + NORM_EPS) * gain + shift

def token_kinds(lengths):
    ends = jnp.cumsum(lengths).astype(jnp.int32)
    starts = (ends - lengths).astype(jnp.int32)
    places = jnp.arange(ROW_LEN, dtype=jnp.int32)
    segment = lax.optimization_barrier(jnp.sum((places[:, None] >= ends[None, :]).astype(jnp.int32), 1))
    is_cls = lax.optimization_barrier(jnp.sum((places[:, None] == starts[None, :]).astype(jnp.float32), 1))
    is_dist = lax.optimization_barrier(jnp.sum((places[:, None] == starts[None, :] + 1).astype(jnp.float32), 1))
    is_patch = (segment < IMGS).astype(jnp.float32) - is_cls - is_dist
    return (segment, is_cls, is_dist, is_patch, starts)

def attention(query, keys, values, segment):
    query_h = query.reshape(ROW_LEN, HEADS, HD)
    keys_h = keys.reshape(ROW_LEN, HEADS, HD)
    values_h = values.reshape(ROW_LEN, HEADS, HD)
    scores = low_back(jnp.einsum('qhd,khd->hqk', query_h, keys_h, precision=HIGH) * SCALE)
    scores = jnp.where((segment[:, None] == segment[None, :])[None], scores, MASKED)
    shares = jax.nn.softmax(scores, axis=-1)
    mixed = jnp.einsum('hqk,khd->qhd', low(shares), values_h, precision=HIGH)
    return mixed.reshape(ROW_LEN, D)

def row_loss(weights, pixels, lengths, labels, teacher):
    embedder, attend, merger, expand, shrink, readout, vectors = weights
    segment, is_cls, is_dist, is_patch, starts = token_kinds(lengths)
    patches = low_back(jnp.dot(pixels, embedder, precision=HIGH))
    x = is_patch[:, None] * patches + is_cls[:, None] * vectors[4 * L + 2] + is_dist[:, None] * vectors[4 * L + 3]
    for layer in range(L):
        base = 4 * layer
        a = low(layer_norm(x, vectors[base], vectors[base + 1]))
        projected = low_back(low(jnp.dot(a, attend[layer], precision=HIGH)))
        mixed = low_back(low(attention(projected[:, :D], projected[:, D:2 * D], projected[:, 2 * D:], segment)))
        x = x + low_back(jnp.dot(mixed, merger[layer], precision=HIGH))
        normed = low(layer_norm(x, vectors[base + 2], vectors[base + 3]))
        hidden_in = low_back(jnp.dot(normed, expand[layer], precision=HIGH))
        hidden = low(jax.nn.gelu(hidden_in, approximate=False))
        x = x + low_back(jnp.dot(hidden, shrink[layer], precision=HIGH))
    class_norm = low(layer_norm(x[starts], vectors[4 * L], vectors[4 * L + 1]))
    distill_norm = low(layer_norm(x[starts + 1], vectors[4 * L], vectors[4 * L + 1]))
    class_logits = jnp.dot(class_norm, readout[0], precision=HIGH)
    distill_logits = jnp.dot(distill_norm, readout[1], precision=HIGH)
    label_hot = (labels[:, None] == jnp.arange(C, dtype=jnp.int32)[None, :]).astype(jnp.float32)
    cross = jax.scipy.special.logsumexp(class_logits, axis=-1) - lax.optimization_barrier(jnp.sum(class_logits * label_hot, -1))
    teach_log = jax.nn.log_softmax(teacher, -1)
    diverge = lax.optimization_barrier(jnp.sum(jnp.exp(teach_log) * (teach_log - jax.nn.log_softmax(distill_logits, -1)), -1))
    return jnp.sum(0.5 * cross + 0.5 * diverge)

def total_loss(masters, pixels, lengths, labels, teacher):
    weights = tuple((low(w) for w in masters))

    def one_row(items):
        return row_loss(weights, items[0], items[1], items[2], items[3])
    losses = lax.map(jax.checkpoint(one_row), (pixels, lengths, labels, teacher))
    return jnp.sum(losses) / NIMG

def rates():
    layer_scale = jnp.power(LAYER_RATE, (L - jnp.arange(L)).astype(jnp.float32))[:, None, None]
    return (LAYER_RATE ** (L + 1), layer_scale, layer_scale, layer_scale, layer_scale, 1.0)

def adamw(weight, mean, square, grad, scale, decay):
    mean_next = BETA_ONE * mean + (1.0 - BETA_ONE) * grad
    square_next = BETA_TWO * square + (1.0 - BETA_TWO) * grad * grad
    mean_hat = mean_next / (1.0 - BETA_ONE ** STEP_COUNT)
    square_hat = square_next / (1.0 - BETA_TWO ** STEP_COUNT)
    weight_next = weight - BASE_RATE * scale * (mean_hat / (jnp.sqrt(square_hat) + ADAM_EPS) + decay * weight)
    return (weight_next, mean_next, square_next)

def moments(mean, square, grad):
    return (BETA_ONE * mean + (1.0 - BETA_ONE) * grad, BETA_TWO * square + (1.0 - BETA_TWO) * grad * grad)

def reference(pixels, lengths, labels, teacher, embedder, embedder_mean, embedder_square, attend, attend_mean, attend_square, merger, merger_mean, merger_square, expand, expand_mean, expand_square, shrink, shrink_mean, shrink_square, readout, readout_mean, readout_square, vectors, vectors_mean, vectors_square):
    masters = (embedder, attend, merger, expand, shrink, readout, vectors)
    means = (embedder_mean, attend_mean, merger_mean, expand_mean, shrink_mean, readout_mean, vectors_mean)
    squares = (embedder_square, attend_square, merger_square, expand_square, shrink_square, readout_square, vectors_square)
    pixel_values = pixels.astype(jnp.float32)

    def objective(params):
        return total_loss(params, pixel_values, lengths, labels, teacher)
    loss, puller = jax.vjp(objective, masters)
    grads = puller(jnp.ones_like(loss))[0]
    grad_norm = jnp.sqrt(sum((jnp.sum(g * g) for g in grads)))
    factor = jnp.minimum(1.0, CLIP_AT / (grad_norm + 1e-06))
    scales = rates()
    fresh = [adamw(masters[j], means[j], squares[j], grads[j] * factor, scales[j], DECAY) for j in range(6)]
    vec_mean, vec_square = moments(vectors_mean, vectors_square, grads[6] * factor)
    return (fresh[0][0], fresh[0][1], fresh[0][2], fresh[1][0], fresh[1][1], fresh[1][2], fresh[2][0], fresh[2][1], fresh[2][2], fresh[3][0], fresh[3][1], fresh[3][2], fresh[4][0], fresh[4][1], fresh[4][2], fresh[5][0], fresh[5][1], fresh[5][2], vec_mean, vec_square, loss, grad_norm)
```

```python
from functools import partial

import jax
import jax.numpy as jnp
from jax import lax
from jax.experimental import pallas as pl
from jax.experimental.pallas import tpu as pltpu
from jax.sharding import PartitionSpec as P

HEADS = 12
HD = 64
L = 1
IMGS = 3
STEP_COUNT = 7

NORM_EPS = 1e-06
MASKED = -1000000000.0
SCALE = 0.125
BETA_ONE = 0.9
BETA_TWO = 0.999
ADAM_EPS = 1e-08
DECAY = 0.05
BASE_RATE = 0.05
LAYER_RATE = 0.75
CLIP_AT = 0.05
HIGH = lax.Precision.HIGHEST
BF = jnp.bfloat16
F32 = jnp.float32
AXES = ("dp", "seq")
PANEL = 768
RATES = (LAYER_RATE ** (L + 1), LAYER_RATE, LAYER_RATE, LAYER_RATE, LAYER_RATE, 1.0)


def pairs(dp_size, seq_size, move):
    return [
        (d * seq_size + s, move(d, s)[0] * seq_size + move(d, s)[1])
        for d in range(dp_size)
        for s in range(seq_size)
    ]


def exchange(value, move):
    return lax.ppermute(value, AXES, pairs(lax.axis_size("dp"), lax.axis_size("seq"), move))


def along_z(step):
    return lambda d, s: (d ^ (2 * step), s)


def across_core(d, s):
    return (d, s ^ 1)


def across_first(d, s):
    return (d ^ 1, s) if s % 2 == 0 else (d, s ^ 2)


def across_second(d, s):
    return (d, s ^ 2) if s % 2 == 0 else (d ^ 1, s)


def spot():
    dp, seq = lax.axis_index("dp"), lax.axis_index("seq")
    return (dp // 2, dp % 2, seq // 2, seq % 2)


def total_of(value):
    for bit in range((lax.axis_size("seq") - 1).bit_length()):
        value = value + exchange(value, lambda d, s, bit=bit: (d, s ^ (1 << bit)))
    for bit in range((lax.axis_size("dp") - 1).bit_length()):
        value = value + exchange(value, lambda d, s, bit=bit: (d ^ (1 << bit), s))
    return value


def assemble(pieces, places, z, plan, shapes):
    count, outs = len(pieces), len(shapes)
    leads = [len(s) - 6 for s in shapes]

    def body(where, *refs):
        ins, out_refs = refs[:count], refs[count:]
        for i in range(count):
            x, y, c = where[3 * i + 1], where[3 * i + 2], where[3 * i + 3]
            for row, rows, o, lead, lo, hi, at in plan:
                out_refs[o][lead + (0, x, y, c, slice(None), slice(at, at + hi - lo))] = ins[i][
                    0, row : row + rows, lo:hi
                ]

    def out_spec(shape, lead):
        block = shape[:lead] + (1,) + shape[lead + 1 :]
        rest = len(shape) - lead - 1
        return pl.BlockSpec(block, lambda j, where: (0,) * lead + (where[0] ^ j,) + (0,) * rest)

    slab = (1,) + pieces[0].shape[1:]
    return pl.pallas_call(
        body,
        out_shape=[jax.ShapeDtypeStruct(s, BF) for s in shapes],
        grid_spec=pltpu.PrefetchScalarGridSpec(
            num_scalar_prefetch=1,
            grid=(pieces[0].shape[0],),
            in_specs=[pl.BlockSpec(slab, lambda j, where: (j, 0, 0))] * count,
            out_specs=[out_spec(s, n) for s, n in zip(shapes, leads)],
        ),
        name="assemble",
    )(jnp.concatenate([jnp.stack([z]), places]).astype(jnp.int32), *pieces)


def gather_group(packed, plan, shapes):
    z, x, y, c = spot()
    depth = lax.axis_size("dp") // 2
    parts = [packed] + [exchange(packed, along_z(j)) for j in range(1, depth)]
    own = jnp.stack(parts)
    near = exchange(own, across_first)
    side = exchange(own, across_second)
    far = exchange(near, across_second)
    pieces = [own, near, side, far]
    pieces = pieces + [exchange(p, across_core) for p in pieces]
    one = jnp.int32(1)
    places = []
    for k in (c, 1 - c):
        fx, fy = 1 - k, k
        places += [x, y, k, x ^ fx, y ^ fy, k, x ^ fy, y ^ fx, k, x ^ one, y ^ one, k]
    places = jnp.stack(places).astype(jnp.int32)
    return assemble(pieces, places, z, plan, shapes)


def at(value, index, axis):
    return lax.dynamic_index_in_dim(value, index, axis, keepdims=False)


def scatter_group(panels):
    z, x, y, c = spot()
    depth = lax.axis_size("dp") // 2
    first = c == 0

    def pick_core(k):
        return jnp.concatenate([at(p, k, 3) for p in panels], 3)

    got = exchange(pick_core(1 - c), across_core)
    total = pick_core(c).astype(F32) + got.astype(F32)
    give = jnp.where(first, at(total, 1 - y, 2), at(total, 1 - x, 1)).astype(BF)
    keep = jnp.where(first, at(total, y, 2), at(total, x, 1))
    total = keep + exchange(give, across_second).astype(F32)
    here = jnp.where(first, x, y)
    give = at(total, 1 - here, 1).astype(BF)
    total = at(total, here, 1) + exchange(give, across_first).astype(F32)
    result = at(total, z, 0)
    for j in range(1, depth):
        result = result + exchange(at(total, z ^ j, 0).astype(BF), along_z(j)).astype(F32)
    return result


def blocks(grad):
    shards = lax.axis_size("dp") * lax.axis_size("seq")
    return grad.reshape(shards // 8, 2, 2, 2, grad.shape[0] // shards, PANEL)


def attend_forward(q_ref, k_ref, v_ref, sq_ref, sk_ref, out_ref, lse_ref):
    step = 256 if q_ref.shape[0] % 256 == 0 else q_ref.shape[0]
    lane = lax.broadcasted_iota(jnp.int32, (1, 2 * HD), 1)
    keys, values = k_ref[...], v_ref[...]
    seg_keys = sk_ref[...]
    for start in range(0, q_ref.shape[0], step):
        rows = slice(start, start + step)
        query = q_ref[rows, :] * jnp.asarray(SCALE, BF)
        same = seg_keys == sq_ref[:, rows]
        mixed = None
        for h in range(2):
            mine = (lane // HD) == h
            raw = lax.dot_general(
                keys,
                jnp.where(mine, query, jnp.zeros_like(query)),
                (((1,), (1,)), ((), ())),
                preferred_element_type=F32,
            )
            raw = jnp.where(same, raw, MASKED)
            top = jnp.max(raw, 0, keepdims=True)
            heavy = jnp.exp(raw - top)
            mass = jnp.sum(heavy, 0, keepdims=True)
            shares = (heavy * (1.0 / mass)).astype(BF)
            part = lax.dot_general(
                jnp.where(mine, values, jnp.zeros_like(values)),
                shares,
                (((0,), (0,)), ((), ())),
                preferred_element_type=F32,
            )
            mixed = part if mixed is None else mixed + part
            lse_ref[0, h : h + 1, rows] = top + jnp.log(mass)
        out_ref[rows, :] = mixed.T.astype(BF)


def attend_backward(
    q_ref, k_ref, v_ref, do_ref, lse_ref, sq_ref, sk_ref, dq_ref, dk_ref, dv_ref
):
    step = 256 if q_ref.shape[0] % 256 == 0 else q_ref.shape[0]
    lane = lax.broadcasted_iota(jnp.int32, (1, 2 * HD), 1)
    keys, values = k_ref[...], v_ref[...]
    seg_keys = sk_ref[...]
    for start in range(0, q_ref.shape[0], step):
        rows = slice(start, start + step)
        query = q_ref[rows, :] * jnp.asarray(SCALE, BF)
        grad = do_ref[rows, :]
        same = seg_keys == sq_ref[:, rows]
        grad_query = None
        grad_keys = None
        grad_values = None
        for h in range(2):
            mine = (lane // HD) == h
            query_h = jnp.where(mine, query, jnp.zeros_like(query))
            grad_h = jnp.where(mine, grad, jnp.zeros_like(grad))
            raw = lax.dot_general(
                keys, query_h, (((1,), (1,)), ((), ())), preferred_element_type=F32
            )
            shares = jnp.exp(jnp.where(same, raw, MASKED) - lse_ref[0, h : h + 1, rows])
            grad_shares = lax.dot_general(
                values, grad_h, (((1,), (1,)), ((), ())), preferred_element_type=F32
            )
            spread = jnp.sum(grad_shares * shares, 0, keepdims=True)
            grad_raw = (shares * (grad_shares - spread)).astype(BF)
            part = lax.dot_general(
                jnp.where(mine, keys, jnp.zeros_like(keys)),
                grad_raw,
                (((0,), (0,)), ((), ())),
                preferred_element_type=F32,
            )
            part_k = jnp.dot(grad_raw, query_h, preferred_element_type=F32)
            part_v = jnp.dot(shares.astype(BF), grad_h, preferred_element_type=F32)
            grad_query = part if grad_query is None else grad_query + part
            grad_keys = part_k if grad_keys is None else grad_keys + part_k
            grad_values = part_v if grad_values is None else grad_values + part_v
        dq_ref[rows, :] = (grad_query.T * SCALE).astype(BF)
        if start == 0:
            dk_ref[...] = grad_keys
            dv_ref[...] = grad_values
        else:
            dk_ref[...] += grad_keys
            dv_ref[...] += grad_values


def head_pair(rows):
    return pl.BlockSpec((rows, 2 * HD), lambda i: (0, i))


def whole(shape):
    return pl.BlockSpec(shape, lambda i: (0,) * len(shape))


def mix_tokens(query, keys, values, seg_q, seg_k):
    nq, nk = query.shape[0], keys.shape[0]
    return pl.pallas_call(
        attend_forward,
        grid=(HEADS // 2,),
        in_specs=[head_pair(nq), head_pair(nk), head_pair(nk), whole((1, nq)), whole((nk, 1))],
        out_specs=[head_pair(nq), pl.BlockSpec((1, 2, nq), lambda i: (i, 0, 0))],
        out_shape=[
            jax.ShapeDtypeStruct((nq, HEADS * HD), BF),
            jax.ShapeDtypeStruct((HEADS // 2, 2, nq), F32),
        ],
        name="attend_forward",
    )(query, keys, values, seg_q, seg_k)


def mix_back(query, keys, values, grad, lse, seg_q, seg_k):
    nq, nk = query.shape[0], keys.shape[0]
    return pl.pallas_call(
        attend_backward,
        grid=(HEADS // 2,),
        in_specs=[
            head_pair(nq),
            head_pair(nk),
            head_pair(nk),
            head_pair(nq),
            pl.BlockSpec((1, 2, nq), lambda i: (i, 0, 0)),
            whole((1, nq)),
            whole((nk, 1)),
        ],
        out_specs=[head_pair(nq), head_pair(nk), head_pair(nk)],
        out_shape=[
            jax.ShapeDtypeStruct((nq, HEADS * HD), BF),
            jax.ShapeDtypeStruct((nk, HEADS * HD), F32),
            jax.ShapeDtypeStruct((nk, HEADS * HD), F32),
        ],
        name="attend_backward",
    )(query, keys, values, grad, lse, seg_q, seg_k)


def norm_parts(x):
    centre = x - jnp.mean(x, -1, keepdims=True)
    rate = lax.rsqrt(jnp.mean(centre * centre, -1, keepdims=True) + NORM_EPS)
    return (centre * rate, rate)


def layer_norm(x, gain, shift):
    return norm_parts(x)[0] * gain + shift


def norm_back(x, gain, grad):
    unit, rate = norm_parts(x)
    inner_grad = grad * gain
    back = rate * (
        inner_grad
        - jnp.mean(inner_grad, -1, keepdims=True)
        - unit * jnp.mean(inner_grad * unit, -1, keepdims=True)
    )
    return (back, jnp.sum(grad * unit, 0), jnp.sum(grad, 0))


def matmul(left, right):
    return jnp.dot(left, right, preferred_element_type=F32)


def outer(left, right):
    return lax.dot_general(left, right, (((0,), (0,)), ((), ())), preferred_element_type=F32)


def inner(grad, weight):
    return lax.dot_general(grad, weight, (((1,), (1,)), ((), ())), preferred_element_type=F32)


def row_swap(seq_size):
    return [(s, s ^ (seq_size // 2)) for s in range(seq_size)]


def rel_bits(seq_size):
    return [1 << b for b in range((seq_size // 2 - 1).bit_length())]


def share_rows(value):
    size = lax.axis_size("seq")
    for bit in rel_bits(size):
        other = lax.ppermute(value, "seq", [(s, s ^ bit) for s in range(size)])
        value = jnp.concatenate([value, other], 0)
    return value


def return_rows(value):
    size = lax.axis_size("seq")
    for bit in reversed(rel_bits(size)):
        half = value.shape[0] // 2
        other = lax.ppermute(value[half:].astype(BF), "seq", [(s, s ^ bit) for s in range(size)])
        value = value[:half] + other.astype(F32)
    return value


def head_terms(rows, inside, readout_w, gain, shift, target, classes, image_count):
    unit, rate = norm_parts(rows)
    low = (unit * gain + shift).astype(BF)
    logits = matmul(low, readout_w)[:, :classes]
    log_share = jax.nn.log_softmax(logits, -1)
    grad = 0.5 * (jnp.exp(log_share) - target) * (inside / image_count)[:, None]
    grad = jnp.pad(grad, ((0, 0), (0, readout_w.shape[1] - classes)))
    grad_readout = lax.dot_general(
        low.astype(F32), grad, (((0,), (0,)), ((), ())), precision=HIGH
    )
    grad_norm = lax.dot_general(
        grad, readout_w.astype(F32), (((1,), (1,)), ((), ())), precision=HIGH
    )
    back, gain_grad, shift_grad = norm_back(rows, gain, grad_norm)
    return (log_share, grad_readout, back, gain_grad, shift_grad)


def adamw(weight, mean, square, grad, scale, decay):
    mean_next = BETA_ONE * mean + (1.0 - BETA_ONE) * grad
    square_next = BETA_TWO * square + (1.0 - BETA_TWO) * grad * grad
    mean_hat = mean_next / (1.0 - BETA_ONE**STEP_COUNT)
    square_hat = square_next / (1.0 - BETA_TWO**STEP_COUNT)
    weight_next = weight - BASE_RATE * scale * (
        mean_hat / (jnp.sqrt(square_hat) + ADAM_EPS) + decay * weight
    )
    return (weight_next, mean_next, square_next)


def moments(mean, square, grad):
    return (
        BETA_ONE * mean + (1.0 - BETA_ONE) * grad,
        BETA_TWO * square + (1.0 - BETA_TWO) * grad * grad,
    )


def side_by_side(shard):
    return [shard[:, k : k + PANEL] for k in range(0, shard.shape[1], PANEL)]


def gather_weights(embedder, attend, merger, expand, shrink, readout, vectors, fast):
    low = [w.astype(BF) for w in (embedder, attend, merger, expand, shrink, readout, vectors)]
    if not fast:
        full = [
            lax.all_gather(w, AXES, axis=0 if n == 0 else 1, tiled=True) for n, w in enumerate(low)
        ]
        return (full[0], full[1][0], full[2][0], full[3][0], full[4][0], full[5], full[6])
    embedder, attend, merger, expand, shrink, readout, vectors = low
    depth = lax.axis_size("dp") // 2
    front = (depth, 2, 2, 2)
    rows, long = embedder.shape[0], shrink.shape[1]
    tall = vectors.shape[0]
    width = PANEL * (-(-readout.shape[2] // 256) * 256 // PANEL) + 256
    readout = jnp.pad(readout, ((0, 0), (0, 0), (0, width - readout.shape[2])))

    wide = jnp.pad(vectors, ((0, 0), (0, PANEL - vectors.shape[1])))
    pack = jnp.concatenate([wide, embedder] + side_by_side(attend[0]), 0)
    plan = [(0, tall, 0, (), 0, 128, 0), (tall, rows, 1, (), 0, PANEL, 0)]
    plan += [(tall + rows * (n + 1), rows, 2, (), 0, PANEL, PANEL * n) for n in range(3)]
    vec, emb, att = gather_group(
        pack, plan, [front + (tall, 128), front + (rows, PANEL), front + (rows, attend.shape[2])]
    )
    vec = vec.reshape(-1, tall, 128)[:, :, : vectors.shape[1]].transpose(1, 0, 2)

    count = expand.shape[2] // PANEL
    pack = jnp.concatenate([merger[0]] + side_by_side(expand[0]), 0)
    plan = [(0, rows, 0, (), 0, PANEL, 0)]
    plan += [(rows * (n + 1), rows, 1, (), 0, PANEL, PANEL * n) for n in range(count)]
    mer, exp = gather_group(
        pack, plan, [front + (rows, PANEL), front + (rows, expand.shape[2])]
    )

    rest = jnp.concatenate([readout[0][:, PANEL:], readout[1][:, PANEL:]], 1)
    rest = jnp.pad(rest, ((0, 0), (0, PANEL - rest.shape[1])))
    pack = jnp.concatenate([shrink[0], readout[0][:, :PANEL], readout[1][:, :PANEL], rest], 0)
    plan = [(0, long, 0, (), 0, PANEL, 0)]
    for head in range(2):
        plan += [
            (long + rows * head, rows, 1, (head,), 0, PANEL, 0),
            (long + rows * 2, rows, 1, (head,), 256 * head, 256 * head + 256, PANEL),
        ]
    shr, rea = gather_group(pack, plan, [front + (long, PANEL), (2,) + front + (rows, width)])
    return (
        emb.reshape(-1, PANEL),
        att.reshape(-1, attend.shape[2]),
        mer.reshape(-1, PANEL),
        exp.reshape(-1, expand.shape[2]),
        shr.reshape(-1, PANEL),
        rea.reshape(2, -1, width),
        vec.reshape(tall, -1),
    )


def scatter_early(merger, expand, shrink, readout, classes, fast):
    if not fast:
        reduced = [
            lax.psum_scatter(g.astype(BF), AXES, scatter_dimension=n, tiled=True).astype(F32)
            for g, n in ((merger, 0), (expand, 0), (shrink, 0), (readout, 1))
        ]
        return (reduced[0], reduced[1], reduced[2], reduced[3][:, :, :classes])
    merger, expand, shrink, readout = [g.astype(BF) for g in (merger, expand, shrink, readout)]
    rest = jnp.concatenate([readout[0][:, PANEL:], readout[1][:, PANEL:]], 1)
    rest = jnp.pad(rest, ((0, 0), (0, PANEL - rest.shape[1])))
    panels = [merger] + side_by_side(expand) + [shrink]
    panels += [readout[0][:, :PANEL], readout[1][:, :PANEL], rest]
    mine = scatter_group([blocks(p) for p in panels])
    parts, row = [], 0
    for p in panels:
        count = p.shape[0] // (lax.axis_size("dp") * lax.axis_size("seq"))
        parts.append(mine[row : row + count])
        row += count
    count = len(parts) - 5
    tails = [parts[-1][:, :256], parts[-1][:, 256:512]]
    reads = [jnp.concatenate([parts[-3 + n], tails[n]], 1)[:, :classes] for n in range(2)]
    return (parts[0], jnp.concatenate(parts[1 : 1 + count], 1), parts[-4], jnp.stack(reads))


def scatter_late(embedder, attend, vectors, fast):
    shards = lax.axis_size("dp") * lax.axis_size("seq")
    if not fast:
        return tuple(
            lax.psum_scatter(g.astype(BF), AXES, scatter_dimension=n, tiled=True).astype(F32)
            for g, n in ((embedder, 0), (attend, 0), (vectors, 1))
        )
    tall, width = vectors.shape[0], vectors.shape[1] // shards
    wide = vectors.astype(BF).reshape(tall, shards, width).transpose(1, 0, 2)
    wide = jnp.pad(wide, ((0, 0), (0, 0), (0, PANEL - width)))
    panels = [wide.reshape(-1, PANEL), embedder.astype(BF)] + side_by_side(attend.astype(BF))
    mine = scatter_group([blocks(p) for p in panels])
    rows = embedder.shape[0] // shards
    parts = [mine[tall + rows * n : tall + rows * (n + 1)] for n in range(4)]
    return (parts[0], jnp.concatenate(parts[1:], 1), mine[:tall, :width])


def on_device(
    pixels,
    lengths,
    labels,
    teacher,
    embedder,
    embedder_mean,
    embedder_square,
    attend,
    attend_mean,
    attend_square,
    merger,
    merger_mean,
    merger_square,
    expand,
    expand_mean,
    expand_square,
    shrink,
    shrink_mean,
    shrink_square,
    readout,
    readout_mean,
    readout_square,
    vectors,
    vectors_mean,
    vectors_square,
):
    seq_size, dp_size = lax.axis_size("seq"), lax.axis_size("dp")
    fast = seq_size == 4 and dp_size % 2 == 0 and embedder.shape[0] % 8 == 0
    seq = lax.axis_index("seq")
    local = pixels.shape[1]
    classes = readout.shape[2]
    image_count = lengths.shape[0] * dp_size * IMGS

    side = seq // (seq_size // 2)
    pixels_mine = lax.dynamic_index_in_dim(pixels, side, 0, False)
    pixels_give = lax.dynamic_index_in_dim(pixels, 1 - side, 0, False)
    pixels_got = lax.ppermute(pixels_give, "seq", row_swap(seq_size))
    tokens = jnp.concatenate([pixels_mine, pixels_got], 0)
    row_lengths = lax.dynamic_index_in_dim(lengths, side, 0, False)
    row_labels = lax.dynamic_index_in_dim(labels, side, 0, False)
    row_teacher = lax.dynamic_index_in_dim(teacher, side, 0, False)

    def places_of(where):
        span = jnp.arange(local, dtype=jnp.int32)
        return jnp.concatenate([where * local + span, (where ^ (seq_size // 2)) * local + span])

    places = places_of(seq)
    all_places = jnp.concatenate([places_of(seq ^ j) for j in range(seq_size // 2)])
    ends = jnp.cumsum(row_lengths)
    starts = ends - row_lengths
    seg_q = jnp.sum((places[:, None] >= ends[None, :]).astype(jnp.int32), 1)
    seg_k = jnp.sum((all_places[:, None] >= ends[None, :]).astype(jnp.int32), 1)
    class_hit = (starts[:, None] == places[None, :]).astype(F32)
    distill_hit = (starts[:, None] + 1 == places[None, :]).astype(F32)
    is_cls, is_dist = jnp.sum(class_hit, 0), jnp.sum(distill_hit, 0)
    is_patch = (seg_q < IMGS).astype(F32) - is_cls - is_dist

    embed_w, attend_w, merger_w, expand_w, shrink_w, readout_w, vector_w = gather_weights(
        embedder, attend, merger, expand, shrink, readout, vectors, fast
    )
    vector_f = vector_w.astype(F32)

    patches = matmul(tokens, embed_w)
    x = (
        is_patch[:, None] * patches
        + is_cls[:, None] * vector_f[4 * L + 2]
        + is_dist[:, None] * vector_f[4 * L + 3]
    )
    a = layer_norm(x, vector_f[0], vector_f[1]).astype(BF)
    projected = matmul(a, attend_w).astype(BF)
    query = projected[:, :PANEL]
    shared = share_rows(projected[:, PANEL:])
    keys, values = shared[:, :PANEL], shared[:, PANEL:]
    mixed, lse = mix_tokens(query, keys, values, seg_q[None, :], seg_k[:, None])
    x_mid = x + matmul(mixed, merger_w)
    normed = layer_norm(x_mid, vector_f[2], vector_f[3]).astype(BF)
    hidden_in = matmul(normed, expand_w)
    cdf = 0.5 * (1.0 + lax.erf(hidden_in * (0.5**0.5)))
    hidden = (hidden_in * cdf).astype(BF)
    slope = cdf + hidden_in * jnp.exp(-0.5 * hidden_in * hidden_in) * ((0.5 / jnp.pi) ** 0.5)
    x_last = x_mid + matmul(hidden, shrink_w)

    class_in, distill_in = jnp.sum(class_hit, 1), jnp.sum(distill_hit, 1)
    class_rows = jnp.dot(class_hit, x_last, precision=HIGH)
    distill_rows = jnp.dot(distill_hit, x_last, precision=HIGH)
    label_hot = (row_labels[:, None] == jnp.arange(classes, dtype=jnp.int32)).astype(F32)
    teach_log = jax.nn.log_softmax(row_teacher, -1)
    teach = jnp.exp(teach_log)
    gain, shift = vector_f[4 * L], vector_f[4 * L + 1]
    class_log, read_a, class_back, gain_a, shift_a = head_terms(
        class_rows, class_in, readout_w[0], gain, shift, label_hot, classes, image_count
    )
    distill_log, read_b, distill_back, gain_b, shift_b = head_terms(
        distill_rows, distill_in, readout_w[1], gain, shift, teach, classes, image_count
    )
    cross = -jnp.sum(class_log * label_hot, -1)
    diverge = jnp.sum(teach * (teach_log - distill_log), -1)
    loss_local = jnp.sum(0.5 * cross * class_in + 0.5 * diverge * distill_in)

    hits = jnp.concatenate([class_hit, distill_hit], 0)
    grad_out = lax.dot_general(
        hits,
        jnp.concatenate([class_back, distill_back], 0),
        (((0,), (0,)), ((), ())),
        precision=HIGH,
    )
    grad_branch = grad_out.astype(BF)
    grad_shrink = outer(hidden, grad_branch)
    grad_pre = (inner(grad_branch, shrink_w) * slope).astype(BF)
    grad_expand = outer(normed, grad_pre)
    grad_normed, gain_two, shift_two = norm_back(x_mid, vector_f[2], inner(grad_pre, expand_w))
    grad_mid = grad_out + grad_normed
    grad_attn = grad_mid.astype(BF)
    grad_merger = outer(mixed, grad_attn)
    early = scatter_early(
        grad_merger, grad_expand, grad_shrink, jnp.stack([read_a, read_b]), classes, fast
    )
    grad_mixed = inner(grad_attn, merger_w).astype(BF)
    grad_query, part_keys, part_values = mix_back(
        query, keys, values, grad_mixed, lse, seg_q[None, :], seg_k[:, None]
    )
    grad_shared = return_rows(jnp.concatenate([part_keys, part_values], 1))
    grad_proj = jnp.concatenate([grad_query, grad_shared.astype(BF)], 1)
    grad_attend = outer(a, grad_proj)
    grad_input, gain_one, shift_one = norm_back(x, vector_f[0], inner(grad_proj, attend_w))
    grad_x = grad_mid + grad_input
    grad_patch = (grad_x * is_patch[:, None]).astype(BF)
    grad_embed = outer(tokens, grad_patch)
    class_token = jnp.sum(grad_x * is_cls[:, None], 0)
    distill_token = jnp.sum(grad_x * is_dist[:, None], 0)
    grad_vectors = jnp.stack(
        [
            gain_one,
            shift_one,
            gain_two,
            shift_two,
            gain_a + gain_b,
            shift_a + shift_b,
            class_token,
            distill_token,
        ]
    )
    late = scatter_late(grad_embed, grad_attend, grad_vectors, fast)
    reduced = (late[0], late[1][None], early[0][None], early[1][None], early[2][None], early[3])
    square_sum = sum((jnp.sum(g * g) for g in reduced)) + jnp.sum(late[2] * late[2])
    both = total_of(jnp.stack([square_sum, loss_local])[None, :])
    grad_norm = jnp.sqrt(both[0, 0])
    factor = jnp.minimum(1.0, CLIP_AT / (grad_norm + 1e-06))

    masters = (embedder, attend, merger, expand, shrink, readout)
    means = (embedder_mean, attend_mean, merger_mean, expand_mean, shrink_mean, readout_mean)
    squares = (
        embedder_square,
        attend_square,
        merger_square,
        expand_square,
        shrink_square,
        readout_square,
    )
    outs = []
    for j in range(6):
        outs += adamw(masters[j], means[j], squares[j], reduced[j] * factor, RATES[j], DECAY)
    outs += moments(vectors_mean, vectors_square, late[2] * factor)
    return tuple(outs) + (both[0, 1] / image_count, grad_norm)


def solution(mesh):
    return jax.shard_map(
        on_device,
        mesh=mesh,
        in_specs=(
            P("dp", "seq", None),
            P("dp", None),
            P("dp", None),
            P("dp", None, None),
            P(("dp", "seq"), None),
            P(("dp", "seq"), None),
            P(("dp", "seq"), None),
            P(None, ("dp", "seq"), None),
            P(None, ("dp", "seq"), None),
            P(None, ("dp", "seq"), None),
            P(None, ("dp", "seq"), None),
            P(None, ("dp", "seq"), None),
            P(None, ("dp", "seq"), None),
            P(None, ("dp", "seq"), None),
            P(None, ("dp", "seq"), None),
            P(None, ("dp", "seq"), None),
            P(None, ("dp", "seq"), None),
            P(None, ("dp", "seq"), None),
            P(None, ("dp", "seq"), None),
            P(None, ("dp", "seq"), None),
            P(None, ("dp", "seq"), None),
            P(None, ("dp", "seq"), None),
            P(None, ("dp", "seq")),
            P(None, ("dp", "seq")),
            P(None, ("dp", "seq")),
        ),
        out_specs=(
            P(("dp", "seq"), None),
            P(("dp", "seq"), None),
            P(("dp", "seq"), None),
            P(None, ("dp", "seq"), None),
            P(None, ("dp", "seq"), None),
            P(None, ("dp", "seq"), None),
            P(None, ("dp", "seq"), None),
            P(None, ("dp", "seq"), None),
            P(None, ("dp", "seq"), None),
            P(None, ("dp", "seq"), None),
            P(None, ("dp", "seq"), None),
            P(None, ("dp", "seq"), None),
            P(None, ("dp", "seq"), None),
            P(None, ("dp", "seq"), None),
            P(None, ("dp", "seq"), None),
            P(None, ("dp", "seq"), None),
            P(None, ("dp", "seq"), None),
            P(None, ("dp", "seq"), None),
            P(None, ("dp", "seq")),
            P(None, ("dp", "seq")),
            P(),
            P(),
        ),
        check_vma=False,
    )
```

```python
from functools import partial

import jax
import jax.numpy as jnp
from jax import lax
from jax.experimental import pallas as pl
from jax.experimental.pallas import tpu as pltpu
from jax.sharding import PartitionSpec as P

HEADS = 12
HD = 64
L = 1
IMGS = 3
STEP_COUNT = 7

NORM_EPS = 1e-06
MASKED = -1000000000.0
SCALE = 0.125
BETA_ONE = 0.9
BETA_TWO = 0.999
ADAM_EPS = 1e-08
DECAY = 0.05
BASE_RATE = 0.05
LAYER_RATE = 0.75
CLIP_AT = 0.05
HIGH = lax.Precision.HIGHEST
BF = jnp.bfloat16
F32 = jnp.float32
AXES = ("dp", "seq")
D = 768
HALF = 384
PAIRS = HEADS // 4
RATES = (LAYER_RATE ** (L + 1), LAYER_RATE, LAYER_RATE, LAYER_RATE, LAYER_RATE, 1.0)


def pairs(move):
    dp_size, seq_size = lax.axis_size("dp"), lax.axis_size("seq")
    return [
        (d * seq_size + s, move(d, s)[0] * seq_size + move(d, s)[1])
        for d in range(dp_size)
        for s in range(seq_size)
    ]


def exchange(value, move):
    return lax.ppermute(value, AXES, pairs(move))


def along_z(step):
    return lambda d, s: (d ^ (2 * step), s)


def across_core(d, s):
    return (d, s ^ 1)


def across_first(d, s):
    return (d ^ 1, s) if s % 2 == 0 else (d, s ^ 2)


def across_second(d, s):
    return (d, s ^ 2) if s % 2 == 0 else (d ^ 1, s)


def swap(value):
    return exchange(value, across_core)


def spot():
    dp, seq = lax.axis_index("dp"), lax.axis_index("seq")
    return (dp // 2, dp % 2, seq // 2, seq % 2)


def total_of(value):
    for bit in range((lax.axis_size("seq") - 1).bit_length()):
        value = value + exchange(value, lambda d, s, bit=bit: (d, s ^ (1 << bit)))
    for bit in range((lax.axis_size("dp") - 1).bit_length()):
        value = value + exchange(value, lambda d, s, bit=bit: (d ^ (1 << bit), s))
    return value


def after(value, *others):
    return lax.optimization_barrier((value,) + others)[0]


def at(value, index, axis):
    return lax.dynamic_index_in_dim(value, index, axis, keepdims=False)


def in_core_order(core, mine, other, axis):
    return jnp.where(
        core == 0,
        jnp.concatenate([mine, other], axis),
        jnp.concatenate([other, mine], axis),
    )


def both_tokens(value):
    return jnp.concatenate([value, swap(value)], 0)


def to_columns(core, value):
    halves = value.reshape(value.shape[0], 2, HALF)
    return jnp.concatenate([at(halves, core, 1), swap(at(halves, 1 - core, 1))], 0)


def to_tokens(core, value):
    count = value.shape[0] // 2
    return in_core_order(core, value[:count], swap(value[count:]), 1)


def reduce_tokens(value):
    count = value.shape[0] // 2
    return value[:count] + swap(value[count:])


def cost(flops, byte_count):
    return pl.CostEstimate(flops=int(flops), bytes_accessed=int(byte_count), transcendentals=0)


def half_of(shard, parts, which):
    rows, wide = shard.shape
    return at(shard.reshape(rows, parts, 2, wide // parts // 2), which, 2).reshape(rows, -1)


def join_halves(core, mine, other, parts):
    rows = mine.shape[0]
    shape = (rows, parts, 1, mine.shape[1] // parts)
    return in_core_order(core, mine.reshape(shape), other.reshape(shape), 2).reshape(rows, -1)


def pad_lanes(value, width):
    return jnp.pad(value, ((0, 0), (0, width - value.shape[1])))


def assemble(pieces, places, z, plan, shapes):
    count = len(pieces)

    def body(where, *refs):
        ins, outs = refs[:count], refs[count:]
        for i in range(count):
            x, y = where[2 * i + 1], where[2 * i + 2]
            rows = ins[i].shape[1]
            for j in range(2):
                for o, row, lane in plan:
                    outs[o][(where[0] % 2) ^ j, x, y, row : row + rows, :] = ins[i][
                        j, :, lane : lane + outs[o].shape[-1]
                    ]

    def out_spec(shape):
        return pl.BlockSpec((2,) + shape[1:], lambda j, where: ((where[0] // 2) ^ j, 0, 0, 0, 0))

    slab = (2,) + pieces[0].shape[1:]
    size = 4 * pieces[0].size
    return pl.pallas_call(
        body,
        out_shape=[jax.ShapeDtypeStruct(s, BF) for s in shapes],
        grid_spec=pltpu.PrefetchScalarGridSpec(
            num_scalar_prefetch=1,
            grid=(pieces[0].shape[0] // 2,),
            in_specs=[pl.BlockSpec(slab, lambda j, where: (j, 0, 0))] * count,
            out_specs=[out_spec(s) for s in shapes],
        ),
        cost_estimate=cost(0, 4 * size),
        name="assemble",
    )(jnp.concatenate([jnp.stack([z]), places]).astype(jnp.int32), *pieces)


def gather_column(unit):
    pair = jnp.stack([unit, exchange(unit, along_z(1))])
    return jnp.concatenate([pair, exchange(pair, along_z(2))], 0)


def gather_plane(own, plan, widths):
    z, x, y, c = spot()
    near = exchange(own, across_first)
    side = exchange(own, across_second)
    far = exchange(near, across_second)
    places = jnp.stack([x, y, x ^ (1 - c), y ^ c, x ^ c, y ^ (1 - c), x ^ 1, y ^ 1])
    shapes = [(own.shape[0], 2, 2) + w for w in widths]
    return assemble([own, near, side, far], places, z, plan, shapes), near


def gather_weights(embedder, attend, merger, expand, shrink, readout, vectors):
    _, _, _, c = spot()
    low = [w.astype(BF) for w in (embedder, attend[0], merger[0], expand[0], shrink[0], readout)]
    embedder, attend, merger, expand, shrink, readout = low
    vectors = vectors.astype(BF)
    rows, chips = embedder.shape[0], lax.axis_size("dp") * lax.axis_size("seq") // 2
    tall, thin = vectors.shape
    wide = -(-readout.shape[2] // 128) * 128

    def chip_rows(mine, other):
        return in_core_order(c, mine, other, 0)

    def of_core(k):
        vec = jnp.pad(vectors, ((0, rows - tall), (0, 128 - thin)))
        first = [half_of(embedder, 1, k), vec, half_of(attend, 3, k)]
        second = [half_of(merger, 1, k), half_of(expand, chips, k), pad_lanes(at(readout, k, 0), wide)]
        return jnp.concatenate(first, 1), jnp.concatenate(second, 1)

    mine, give = of_core(c), of_core(1 - c)
    got = swap(give[0])
    front = chip_rows(mine[0], got)
    vec = in_core_order(c, vectors, got[:tall, HALF : HALF + thin], 1)
    vec = jnp.pad(vec, ((0, 2 * rows - tall), (0, 128 - 2 * thin)))
    back = chip_rows(mine[1], swap(give[1]))
    tall_shrink = shrink.shape[0]
    shrink = jnp.concatenate([shrink[: 2 * rows], shrink[2 * rows :]], 1)

    tall_rows = 2 * rows
    unit = jnp.concatenate([front[:, :HALF], vec, front[:, HALF + 128 :]], 1)
    own = gather_column(unit)
    (emb, vec, att), near = gather_plane(
        own,
        [(0, 0, 0), (1, 0, HALF), (2, 0, HALF + 128)],
        [(tall_rows, HALF), (tall_rows, 128), (tall_rows, 3 * HALF)],
    )
    own = gather_column(after(back[:, : 5 * HALF], own))
    (mer, exp), _ = gather_plane(
        own, [(0, 0, 0), (1, 0, HALF)], [(tall_rows, HALF), (tall_rows, 4 * HALF)]
    )
    unit = jnp.concatenate([shrink, back[:, 5 * HALF :]], 1)
    own = gather_column(after(unit, own, near))
    (shr, rea), _ = gather_plane(
        own,
        [(0, 0, 0), (0, tall_rows, D), (1, 0, 2 * D)],
        [(tall_shrink, D), (tall_rows, wide)],
    )
    vec = vec.reshape(chips, 2 * rows, 128)[:, :tall, : 2 * thin].transpose(1, 0, 2)
    return (
        emb.reshape(-1, HALF),
        att.reshape(-1, 3 * HALF),
        mer.reshape(-1, HALF),
        exp.reshape(-1, 4 * HALF),
        shr.reshape(-1, D),
        rea.reshape(-1, wide),
        vec.reshape(tall, -1),
    )


def gather_plain(embedder, attend, merger, expand, shrink, readout, vectors):
    _, _, _, c = spot()
    chips = lax.axis_size("dp") * lax.axis_size("seq") // 2
    wide = -(-readout.shape[2] // 128) * 128

    def whole_of(shard, axis):
        return lax.all_gather(shard.astype(BF), AXES, axis=axis, tiled=True)

    shrink = whole_of(shrink[0], 0).reshape(chips, 2, -1, D)
    return (
        half_of(whole_of(embedder, 0), 1, c),
        half_of(whole_of(attend[0], 0), 3, c),
        half_of(whole_of(merger[0], 0), 1, c),
        half_of(whole_of(expand[0], 0), chips, c),
        at(shrink, c, 1).reshape(-1, D),
        pad_lanes(at(whole_of(readout, 1), c, 0), wide),
        whole_of(vectors, 1),
    )


def blocks(grad):
    chips = lax.axis_size("dp") * lax.axis_size("seq") // 2
    return grad.reshape(chips // 4, 2, 2, grad.shape[0] // chips, grad.shape[1])


def lane_plan(grads, rows):
    plan, lane = [], 0
    for n, g in enumerate(grads):
        for row in range(0, g.shape[3], rows):
            plan.append((n, row, lane))
            lane += g.shape[4]
    return plan, lane


def position():
    return jnp.stack(spot()).astype(jnp.int32)


def chosen(grads, keep):
    def spec(g):
        def index(t, w):
            px = jnp.where(w[3] == 0, t, w[1] if keep else 1 - w[1])
            py = jnp.where(w[3] == 0, w[2] if keep else 1 - w[2], t)
            return (0, px, py, 0, 0)

        return pl.BlockSpec((g.shape[0], 1, 1) + g.shape[3:], index)

    return [spec(g) for g in grads]


def scatter_give(grads, rows):
    depth, count = grads[0].shape[0], len(grads)
    plan, lanes = lane_plan(grads, rows)

    def body(w, *refs):
        for n, row, lane in plan:
            block = refs[n][:, 0, 0, row : row + rows, :]
            refs[count][:, 0, :, lane : lane + block.shape[2]] = block

    give = pl.pallas_call(
        body,
        out_shape=jax.ShapeDtypeStruct((depth, 2, rows, lanes), BF),
        grid_spec=pltpu.PrefetchScalarGridSpec(
            num_scalar_prefetch=1,
            grid=(2,),
            in_specs=chosen(grads, False),
            out_specs=pl.BlockSpec((depth, 1, rows, lanes), lambda t, w: (0, t, 0, 0)),
        ),
        cost_estimate=cost(0, 8 * depth * rows * lanes),
        name="scatter_give",
    )(position(), *grads)
    return grads, rows, exchange(give, across_second)


def scatter_near(state, *others):
    grads, rows, got = state
    depth, count = grads[0].shape[0], len(grads)
    plan, lanes = lane_plan(grads, rows)

    def body(w, *refs):
        ins, got_ref, give_ref, keep_ref = refs[:count], refs[count], refs[count + 1], refs[count + 2]
        here = jnp.where(w[3] == 0, w[1], w[2])
        for n, row, lane in plan:
            block = ins[n][:, 0, 0, row : row + rows, :]
            span = slice(lane, lane + block.shape[2])
            value = block.astype(F32) + got_ref[:, 0, :, span].astype(F32)

            @pl.when(pl.program_id(0) == here)
            def _():
                keep_ref[:, :, span] = value

            @pl.when(pl.program_id(0) != here)
            def _():
                give_ref[:, :, span] = value.astype(BF)

    out = pl.BlockSpec((depth, rows, lanes), lambda t, w: (0, 0, 0))
    slab = pl.BlockSpec((depth, 1, rows, lanes), lambda t, w: (0, t, 0, 0))
    give, keep = pl.pallas_call(
        body,
        out_shape=[jax.ShapeDtypeStruct((depth, rows, lanes), t) for t in (BF, F32)],
        grid_spec=pltpu.PrefetchScalarGridSpec(
            num_scalar_prefetch=1,
            grid=(2,),
            in_specs=chosen(grads, True) + [slab],
            out_specs=[out, out],
        ),
        cost_estimate=cost(0, 14 * depth * rows * lanes),
        name="scatter_near",
    )(position(), *grads, after(got, *others))
    return keep, exchange(give, across_first)


def scatter_column(state, *others):
    keep, got = state
    depth, rows, lanes = keep.shape

    def body(w, keep_in, got_ref, keep_ref, give_ref):
        for j in range(depth):
            value = keep_in[w[0] ^ j] + got_ref[w[0] ^ j].astype(F32)
            if j < 2:
                keep_ref[j] = value
            else:
                give_ref[j - 2] = value.astype(BF)

    block = pl.BlockSpec((depth, rows, lanes), lambda t, w: (0, 0, 0))
    out = pl.BlockSpec((2, rows, lanes), lambda t, w: (0, 0, 0))
    keep, give = pl.pallas_call(
        body,
        out_shape=[jax.ShapeDtypeStruct((2, rows, lanes), t) for t in (F32, BF)],
        grid_spec=pltpu.PrefetchScalarGridSpec(
            num_scalar_prefetch=1, grid=(1,), in_specs=[block, block], out_specs=[out, out]
        ),
        cost_estimate=cost(0, 9 * depth * rows * lanes),
        name="scatter_column",
    )(position(), keep, after(got, *others))
    return keep, exchange(give, along_z(2))


def scatter_pair(state, *others):
    keep, got = state
    total = keep + after(got, *others).astype(F32)
    return total[0], exchange(total[1].astype(BF), along_z(1))


def scatter_end(state):
    return state[0] + state[1].astype(F32)


def own_rows(core, unit):
    halves = unit.reshape(2, unit.shape[0] // 2, unit.shape[1])
    return at(halves, core, 0), swap(at(halves, 1 - core, 0))


def first_done(state, classes):
    core = lax.axis_index("seq") % 2
    unit = scatter_end(state)
    shrink = jnp.concatenate([unit[:, :D], unit[:, D : 2 * D]], 0)
    mine, other = own_rows(core, unit[:, 2 * D :])
    return shrink, in_core_order(core, mine[None], other[None], 0)[:, :, :classes]


def second_done(state, wide):
    core = lax.axis_index("seq") % 2
    chips = lax.axis_size("dp") * lax.axis_size("seq") // 2
    mine, other = own_rows(core, scatter_end(state))
    return (
        join_halves(core, mine[:, :wide], other[:, :wide], chips),
        join_halves(core, mine[:, wide:], other[:, wide:], 1),
    )


def vector_blocks(vectors, like):
    chips = lax.axis_size("dp") * lax.axis_size("seq") // 2
    tall, thin = vectors.shape[0], vectors.shape[1] // chips
    vec = vectors.astype(BF).reshape(tall, chips, thin).transpose(1, 0, 2)
    vec = jnp.pad(vec, ((0, 0), (0, like.shape[3] - tall), (0, 128 - thin)))
    return vec.reshape(like.shape[:4] + (128,))


def last_done(attend, embedder, tall, thin):
    core = lax.axis_index("seq") % 2
    attend, unit = scatter_end(attend), scatter_end(embedder)
    rows = attend.shape[0] // 2
    pieces = unit[:tall, HALF : HALF + 2 * thin].reshape(tall, 2, thin)
    halves = jnp.concatenate([unit[:, :HALF], attend], 1).reshape(2, rows, -1)
    mine = at(halves, core, 0)
    sent = jnp.pad(at(pieces, 1 - core, 1), ((0, rows - tall), (0, 128 - thin)))
    got = swap(jnp.concatenate([at(halves, 1 - core, 0), sent], 1))
    wide = mine.shape[1]
    return (
        join_halves(core, mine[:, :HALF], got[:, :HALF], 1),
        join_halves(core, mine[:, HALF:], got[:, HALF:wide], 3),
        at(pieces, core, 1) + got[:tall, wide : wide + thin],
    )


def scatter_plain(grads, classes):
    embedder, attend, merger, expand, shrink, readout, vectors = grads
    _, _, _, c = spot()
    chips = lax.axis_size("dp") * lax.axis_size("seq") // 2

    def reduced(value, axis):
        value = value.astype(F32)
        return lax.psum_scatter(value, AXES, scatter_dimension=axis, tiled=True)

    def spread(half, parts):
        return reduced(join_halves(c, half, jnp.zeros_like(half), parts), 0)

    tall = shrink.reshape(chips, 1, -1, D)
    tall = in_core_order(c, tall, jnp.zeros_like(tall), 1).reshape(-1, D)
    pair = in_core_order(c, readout[None], jnp.zeros_like(readout)[None], 0)
    return (
        spread(embedder, 1),
        spread(attend, 3),
        spread(merger, 1),
        spread(expand, chips),
        reduced(tall, 0),
        reduced(pair, 1)[:, :, :classes],
        reduced(vectors, 1),
    )


def dot_keys(left, right):
    return lax.dot_general(left, right, (((1,), (1,)), ((), ())), preferred_element_type=F32)


def turned(value):
    return value.astype(F32).T.astype(BF)


def attend_forward(q_ref, k_ref, v_ref, qm_ref, km_ref, out_ref, exact_ref, lse_ref, keys, values):
    lane = lax.broadcasted_iota(jnp.int32, (1, 2 * HD), 1) // HD

    @pl.when(pl.program_id(1) == 0)
    def _():
        for h in range(2):
            keys[h] = jnp.where(lane == h, k_ref[...], km_ref[...])
        values[...] = turned(v_ref[...])

    query = q_ref[...] * jnp.asarray(SCALE, BF)
    parts = []
    for h in range(2):
        raw = dot_keys(keys[h], jnp.where(lane == h, query, qm_ref[...]))
        top = jnp.max(raw, 0, keepdims=True)
        heavy = jnp.exp(raw - top)
        mass = jnp.sum(heavy, 0, keepdims=True)
        shares = (heavy * (1.0 / mass)).astype(BF)
        part = jnp.dot(values[...], shares, preferred_element_type=F32)
        parts.append(part[HD * h : HD * (h + 1)])
        lse_ref[0, h : h + 1, :] = top + jnp.log(mass)
    mixed = jnp.concatenate(parts, 0).T
    exact_ref[...] = mixed
    out_ref[...] = mixed.astype(BF)


def attend_backward(joined, q_ref, k_ref, v_ref, do_ref, exact_ref, lse_ref, qm_ref, km_ref, *refs):
    outs, (keys, turned_keys, grad_keys, grad_values) = refs[:-4], refs[-4:]
    lane = lax.broadcasted_iota(jnp.int32, (1, 2 * HD), 1) // HD
    pair, step = pl.program_id(0), pl.program_id(1)

    @pl.when(step == 0)
    def _():
        for h in range(2):
            keys[h] = jnp.where(lane == h, k_ref[...], km_ref[...])
        turned_keys[...] = turned(k_ref[...])
        grad_keys[...] = jnp.zeros_like(grad_keys)
        grad_values[...] = jnp.zeros_like(grad_values)

    query = q_ref[...] * jnp.asarray(SCALE, BF)
    grad = do_ref[...]
    spreads = (grad.astype(F32) * exact_ref[...]).T
    parts = []
    for h in range(2):
        own = slice(HD * h, HD * (h + 1))
        grad_h = jnp.where(lane == h, grad, jnp.zeros_like(grad))
        query_h = jnp.where(lane == h, query, jnp.zeros_like(query))
        raw = dot_keys(keys[h], jnp.where(lane == h, query, qm_ref[...]))
        shares = jnp.exp(raw - lse_ref[0, h : h + 1, :])
        spread = jnp.sum(spreads[own], 0, keepdims=True)
        grad_raw = (shares * (dot_keys(v_ref[...], grad_h) - spread)).astype(BF)
        parts.append(jnp.dot(turned_keys[...], grad_raw, preferred_element_type=F32)[own])
        grad_keys[...] += jnp.dot(grad_raw, query_h, preferred_element_type=F32)
        grad_values[...] += jnp.dot(shares.astype(BF), grad_h, preferred_element_type=F32)
    grad_query = (jnp.concatenate(parts, 0).T * SCALE).astype(BF)
    if joined:
        rows = grad_query.shape[0]
        down = pl.ds(pl.multiple_of(step * rows, rows), rows)
        outs[0][down, pl.ds(pl.multiple_of(pair * 128, 128), 128)] = grad_query
    else:
        outs[0][...] = grad_query

    @pl.when(step == pl.num_programs(1) - 1)
    def _():
        if joined:
            across = pl.num_programs(0)
            for n, total in enumerate((grad_keys, grad_values)):
                place = (pair + across * (n + 1)) * 128
                outs[0][:, pl.ds(pl.multiple_of(place, 128), 128)] = total[...].astype(BF)
        else:
            outs[1][...] = grad_keys[...]
            outs[2][...] = grad_values[...]


def tile_of(count):
    return 256 if count % 256 == 0 else count


def mix_tokens(projected, around, mask_q, mask_k):
    nq, nk = projected.shape[0], around.shape[0]
    tile = tile_of(nq)
    rows = lambda part: pl.BlockSpec((tile, 128), lambda i, j: (j, part * PAIRS + i))
    tall = lambda part: pl.BlockSpec((nk, 128), lambda i, j: (0, part * PAIRS + i))
    return pl.pallas_call(
        attend_forward,
        grid=(PAIRS, nq // tile),
        in_specs=[
            rows(0),
            tall(1),
            tall(2),
            pl.BlockSpec((tile, 128), lambda i, j: (j, 0)),
            pl.BlockSpec((nk, 128), lambda i, j: (0, 0)),
        ],
        out_specs=[rows(0), rows(0), pl.BlockSpec((1, 2, tile), lambda i, j: (i, 0, j))],
        out_shape=[
            jax.ShapeDtypeStruct((nq, HALF), BF),
            jax.ShapeDtypeStruct((nq, HALF), F32),
            jax.ShapeDtypeStruct((PAIRS, 2, nq), F32),
        ],
        scratch_shapes=[pltpu.VMEM((2, nk, 128), BF), pltpu.VMEM((128, nk), BF)],
        cost_estimate=cost(8 * nq * nk * HALF * 4, 12 * nq * HALF),
        name="attend_forward",
    )(projected, around, around, mask_q, mask_k)


def mix_back(projected, around, grad, exact, lse, mask_q, mask_k):
    nq, nk = projected.shape[0], around.shape[0]
    tile, joined = tile_of(nq), nq == nk
    rows = lambda part: pl.BlockSpec((tile, 128), lambda i, j: (j, part * PAIRS + i))
    tall = lambda part: pl.BlockSpec((nk, 128), lambda i, j: (0, part * PAIRS + i))
    if joined:
        out_specs = [pl.BlockSpec((nq, 3 * HALF), lambda i, j: (0, 0))]
        out_shape = [jax.ShapeDtypeStruct((nq, 3 * HALF), BF)]
    else:
        out_specs = [rows(0), tall(0), tall(0)]
        out_shape = [jax.ShapeDtypeStruct((nq, HALF), BF)]
        out_shape += [jax.ShapeDtypeStruct((nk, HALF), F32)] * 2
    return pl.pallas_call(
        partial(attend_backward, joined),
        grid=(PAIRS, nq // tile),
        in_specs=[
            rows(0),
            tall(1),
            tall(2),
            rows(0),
            rows(0),
            pl.BlockSpec((1, 2, tile), lambda i, j: (i, 0, j)),
            pl.BlockSpec((tile, 128), lambda i, j: (j, 0)),
            pl.BlockSpec((nk, 128), lambda i, j: (0, 0)),
        ],
        out_specs=out_specs,
        out_shape=out_shape,
        scratch_shapes=[
            pltpu.VMEM((2, nk, 128), BF),
            pltpu.VMEM((128, nk), BF),
            pltpu.VMEM((nk, 128), F32),
            pltpu.VMEM((nk, 128), F32),
        ],
        cost_estimate=cost(20 * nq * nk * HALF * 3, 12 * nq * HALF),
        name="attend_backward",
    )(projected, around, around, grad, exact, lse, mask_q, mask_k)


def norm_parts(x):
    centre = x - jnp.mean(x, -1, keepdims=True)
    rate = lax.rsqrt(jnp.mean(centre * centre, -1, keepdims=True) + NORM_EPS)
    return (centre * rate, rate)


def layer_norm(x, gain, shift):
    return norm_parts(x)[0] * gain + shift


def norm_back(x, gain, grad):
    unit, rate = norm_parts(x)
    inner_grad = grad * gain
    back = rate * (
        inner_grad
        - jnp.mean(inner_grad, -1, keepdims=True)
        - unit * jnp.mean(inner_grad * unit, -1, keepdims=True)
    )
    return (back, jnp.sum(grad * unit, 0), jnp.sum(grad, 0))


def matmul(left, right):
    return jnp.dot(left, right, preferred_element_type=F32)


def outer(left, right):
    return lax.dot_general(left, right, (((0,), (0,)), ((), ())), preferred_element_type=F32)


def inner(grad, weight):
    return lax.dot_general(grad, weight, (((1,), (1,)), ((), ())), preferred_element_type=F32)


def chip_bits():
    return [2 << b for b in range((lax.axis_size("seq") // 4 - 1).bit_length())]


def of_bit(value, bit):
    return exchange(value, lambda d, s: (d, s ^ bit))


def row_tokens(value):
    for bit in chip_bits():
        value = jnp.concatenate([value, of_bit(value, bit)], 0)
    return value


def row_return(value):
    for bit in reversed(chip_bits()):
        half = value.shape[0] // 2
        value = value[:half] + of_bit(value[half:].astype(BF), bit).astype(F32)
    return value


def row_sum(value):
    for bit in chip_bits():
        value = value + of_bit(value, bit)
    return value


def segment_lanes(segment, of_query):
    lane = jnp.arange(128, dtype=jnp.int32) % HD
    hit = segment[:, None] == lane[None, :]
    if of_query:
        return jnp.where(hit | (lane > IMGS)[None, :], 0.0, MASKED).astype(BF)
    return hit.astype(BF)


def adamw(weight, mean, square, grad, scale, decay):
    mean_next = BETA_ONE * mean + (1.0 - BETA_ONE) * grad
    square_next = BETA_TWO * square + (1.0 - BETA_TWO) * grad * grad
    mean_hat = mean_next / (1.0 - BETA_ONE**STEP_COUNT)
    square_hat = square_next / (1.0 - BETA_TWO**STEP_COUNT)
    weight_next = weight - BASE_RATE * scale * (
        mean_hat / (jnp.sqrt(square_hat) + ADAM_EPS) + decay * weight
    )
    return (weight_next, mean_next, square_next)


def moments(mean, square, grad):
    return (
        BETA_ONE * mean + (1.0 - BETA_ONE) * grad,
        BETA_TWO * square + (1.0 - BETA_TWO) * grad * grad,
    )


def on_device(
    pixels,
    lengths,
    labels,
    teacher,
    embedder,
    embedder_mean,
    embedder_square,
    attend,
    attend_mean,
    attend_square,
    merger,
    merger_mean,
    merger_square,
    expand,
    expand_mean,
    expand_square,
    shrink,
    shrink_mean,
    shrink_square,
    readout,
    readout_mean,
    readout_square,
    vectors,
    vectors_mean,
    vectors_square,
):
    seq_size, dp_size = lax.axis_size("seq"), lax.axis_size("dp")
    fast = seq_size == 4 and dp_size == 8 and embedder.shape[0] == 24
    seq, core = lax.axis_index("seq"), lax.axis_index("seq") % 2
    local, far = pixels.shape[1], seq_size // 2
    span = seq_size // 4
    classes = readout.shape[2]
    image_count = lengths.shape[0] * dp_size * IMGS

    side = seq // far
    pixels_got = of_bit(at(pixels, 1 - side, 0), far)
    tokens = jnp.concatenate([at(pixels, side, 0), pixels_got], 0)
    all_pixels = both_tokens(tokens)
    row_lengths = at(lengths, side, 0)
    row_labels = at(labels, side, 0)
    row_teacher = at(teacher, side, 0)

    def places_of(where):
        step = jnp.arange(local, dtype=jnp.int32)
        return jnp.concatenate([where * local + step, (where ^ far) * local + step])

    places = places_of(seq)
    ends = jnp.cumsum(row_lengths)
    starts = ends - row_lengths

    def segment_of(spots):
        return jnp.sum((spots[:, None] >= ends[None, :]).astype(jnp.int32), 1)

    seg_q = segment_of(jnp.concatenate([places, places_of(seq ^ 1)]))
    order = [0]
    for bit in chip_bits():
        order = order + [o ^ bit for o in order]
    seg_k = segment_of(jnp.concatenate([places_of(seq ^ o ^ k) for o in order for k in range(2)]))
    mask_q, mask_k = segment_lanes(seg_q, True), segment_lanes(seg_k, False)
    marks = jnp.concatenate([starts, starts + 1])
    hits = (marks[:, None] == places[None, :]).astype(F32)
    token_hits = (places[:, None] == marks[None, :]).astype(F32)
    is_cls, is_dist = jnp.sum(hits[:IMGS], 0), jnp.sum(hits[IMGS:], 0)
    is_patch = (seg_q[: 2 * local] < IMGS).astype(F32) - is_cls - is_dist

    gather = gather_weights if fast else gather_plain
    embed_w, attend_w, merger_half, expand_w, shrink_w, readout_w, vector_w = gather(
        embedder, attend, merger, expand, shrink, readout, vectors
    )
    merger_w = in_core_order(core, merger_half, swap(merger_half), 1)
    vector_f = vector_w.astype(F32)

    patches = to_tokens(core, matmul(all_pixels, embed_w))
    x = (
        is_patch[:, None] * patches
        + is_cls[:, None] * vector_f[4 * L + 2]
        + is_dist[:, None] * vector_f[4 * L + 3]
    )
    a = both_tokens(layer_norm(x, vector_f[0], vector_f[1]).astype(BF))
    projected = matmul(a, attend_w).astype(BF)
    around = row_tokens(projected)
    mixed_half, exact, lse = mix_tokens(projected, around, mask_q, mask_k)
    other = swap(mixed_half)
    count = 2 * local
    other = jnp.concatenate([other[count:], other[:count]], 0)
    mixed = in_core_order(core, mixed_half, other, 1)
    x_mid = x + matmul(mixed[:count], merger_w)
    normed = both_tokens(layer_norm(x_mid, vector_f[2], vector_f[3]).astype(BF))
    hidden_in = matmul(normed, expand_w)
    cdf = 0.5 * (1.0 + lax.erf(hidden_in * (0.5**0.5)))
    hidden = (hidden_in * cdf).astype(BF)
    slope = cdf + hidden_in * jnp.exp(-0.5 * hidden_in * hidden_in) * ((0.5 / jnp.pi) ** 0.5)
    x_last = x_mid + reduce_tokens(matmul(hidden, shrink_w))

    label_hot = (row_labels[:, None] == jnp.arange(classes, dtype=jnp.int32)).astype(F32)
    teach_log = jax.nn.log_softmax(row_teacher, -1)
    target = jnp.where(core == 0, label_hot, jnp.exp(teach_log))
    target_log = jnp.where(core == 0, 0.0, teach_log)
    gain, shift = vector_f[4 * L], vector_f[4 * L + 1]
    rows = row_sum(jnp.dot(hits, x_last, precision=HIGH)).reshape(2, IMGS, D)
    rows = at(rows, core, 0) + swap(at(rows, 1 - core, 0))
    unit, rate = norm_parts(rows)
    head_in = (unit * gain + shift).astype(BF)
    logits = matmul(head_in, readout_w)[:, :classes]
    log_share = jax.nn.log_softmax(logits, -1)
    loss_local = jnp.sum(0.5 * target * (target_log - log_share)) / span
    grad_logits = pad_lanes(
        0.5 * (jnp.exp(log_share) - target) / image_count, readout_w.shape[1]
    )
    grad_readout = lax.dot_general(
        head_in.astype(F32), grad_logits / span, (((0,), (0,)), ((), ())), precision=HIGH
    )
    grad_head = lax.dot_general(
        grad_logits, readout_w.astype(F32), (((1,), (1,)), ((), ())), precision=HIGH
    )
    head_back, gain_out, shift_out = norm_back(rows, gain, grad_head)
    back = in_core_order(core, head_back, swap(head_back), 0)

    grad_out = jnp.dot(token_hits, back, precision=HIGH)
    grad_branch = both_tokens(grad_out.astype(BF))
    grad_shrink = outer(hidden, grad_branch).astype(BF)
    grad_readout = grad_readout.astype(BF)
    if fast:
        parts = [blocks(grad_shrink), blocks(grad_readout)]
        unit_rows = parts[1].shape[3]
        first = scatter_give(parts, unit_rows)
    grad_pre = (inner(grad_branch, shrink_w) * slope).astype(BF)
    grad_expand = outer(normed, grad_pre).astype(BF)
    grad_normed, gain_two, shift_two = norm_back(
        x_mid, vector_f[2], reduce_tokens(inner(grad_pre, expand_w))
    )
    grad_mid = grad_out + grad_normed
    grad_attn = both_tokens(grad_mid.astype(BF))
    attn_half = at(grad_attn.reshape(-1, 2, HALF), core, 1)
    grad_merger = outer(mixed, attn_half).astype(BF)
    if fast:
        second = scatter_give([blocks(grad_expand), blocks(grad_merger)], unit_rows)
    grad_mixed = inner(grad_attn, at(merger_w.reshape(2, HALF, D), core, 0)).astype(BF)
    grads = mix_back(projected, around, grad_mixed, exact, lse, mask_q, mask_k)
    if len(grads) == 1:
        grad_proj = grads[0]
    else:
        grad_proj = jnp.concatenate([grads[0]] + [row_return(g).astype(BF) for g in grads[1:]], 1)
    if fast:
        first = scatter_near(first, grad_proj)
    grad_a = inner(grad_proj, attend_w)
    grad_attend = outer(a, grad_proj).astype(BF)
    if fast:
        third = scatter_give([blocks(grad_attend)], unit_rows)
        second = scatter_near(second, grad_attend)
    grad_input, gain_one, shift_one = norm_back(x, vector_f[0], reduce_tokens(grad_a))
    grad_x = grad_mid + grad_input
    grad_patch = (grad_x * is_patch[:, None]).astype(BF)
    grad_embed = outer(all_pixels, to_columns(core, grad_patch)).astype(BF)
    grad_vectors = jnp.stack(
        [
            gain_one,
            shift_one,
            gain_two,
            shift_two,
            gain_out / span,
            shift_out / span,
            jnp.sum(grad_x * is_cls[:, None], 0),
            jnp.sum(grad_x * is_dist[:, None], 0),
        ]
    )
    if fast:
        first = scatter_column(first, grad_patch)
        parts = [blocks(grad_embed)]
        fourth = scatter_give(parts + [vector_blocks(grad_vectors, parts[0])], unit_rows)
        third = scatter_near(third, grad_embed)
        second = scatter_column(second, grad_embed)
        fourth = scatter_near(fourth)
        first = scatter_pair(first, fourth[0])
        third = scatter_column(third)
        fourth = scatter_column(fourth)
        second = scatter_pair(second, fourth[0])
        third, fourth = scatter_pair(third), scatter_pair(fourth)
        sum_shrink, sum_readout = first_done(first, classes)
        sum_expand, sum_merger = second_done(second, grad_expand.shape[1])
        sum_embed, sum_attend, sum_vectors = last_done(third, fourth, *vectors.shape)
    else:
        sum_embed, sum_attend, sum_merger, sum_expand, sum_shrink, sum_readout, sum_vectors = (
            scatter_plain(
                (grad_embed, grad_attend, grad_merger, grad_expand)
                + (grad_shrink, grad_readout, grad_vectors),
                classes,
            )
        )
    reduced = (sum_embed, sum_attend, sum_merger, sum_expand, sum_shrink, sum_readout)
    square_sum = sum((jnp.sum(g * g) for g in reduced)) + jnp.sum(sum_vectors * sum_vectors)
    both = total_of(jnp.stack([square_sum, loss_local])[None, :])
    grad_norm = jnp.sqrt(both[0, 0])
    factor = jnp.minimum(1.0, CLIP_AT / (grad_norm + 1e-06))

    masters = (embedder, attend, merger, expand, shrink, readout)
    means = (embedder_mean, attend_mean, merger_mean, expand_mean, shrink_mean, readout_mean)
    squares = (
        embedder_square,
        attend_square,
        merger_square,
        expand_square,
        shrink_square,
        readout_square,
    )
    outs = []
    for j in range(6):
        grad = reduced[j].reshape(masters[j].shape) * factor
        outs += adamw(masters[j], means[j], squares[j], grad, RATES[j], DECAY)
    outs += moments(vectors_mean, vectors_square, sum_vectors * factor)
    return tuple(outs) + (both[0, 1] / image_count, grad_norm)


def solution(mesh):
    return jax.shard_map(
        on_device,
        mesh=mesh,
        in_specs=(
            P("dp", "seq", None),
            P("dp", None),
            P("dp", None),
            P("dp", None, None),
            P(("dp", "seq"), None),
            P(("dp", "seq"), None),
            P(("dp", "seq"), None),
            P(None, ("dp", "seq"), None),
            P(None, ("dp", "seq"), None),
            P(None, ("dp", "seq"), None),
            P(None, ("dp", "seq"), None),
            P(None, ("dp", "seq"), None),
            P(None, ("dp", "seq"), None),
            P(None, ("dp", "seq"), None),
            P(None, ("dp", "seq"), None),
            P(None, ("dp", "seq"), None),
            P(None, ("dp", "seq"), None),
            P(None, ("dp", "seq"), None),
            P(None, ("dp", "seq"), None),
            P(None, ("dp", "seq"), None),
            P(None, ("dp", "seq"), None),
            P(None, ("dp", "seq"), None),
            P(None, ("dp", "seq")),
            P(None, ("dp", "seq")),
            P(None, ("dp", "seq")),
        ),
        out_specs=(
            P(("dp", "seq"), None),
            P(("dp", "seq"), None),
            P(("dp", "seq"), None),
            P(None, ("dp", "seq"), None),
            P(None, ("dp", "seq"), None),
            P(None, ("dp", "seq"), None),
            P(None, ("dp", "seq"), None),
            P(None, ("dp", "seq"), None),
            P(None, ("dp", "seq"), None),
            P(None, ("dp", "seq"), None),
            P(None, ("dp", "seq"), None),
            P(None, ("dp", "seq"), None),
            P(None, ("dp", "seq"), None),
            P(None, ("dp", "seq"), None),
            P(None, ("dp", "seq"), None),
            P(None, ("dp", "seq"), None),
            P(None, ("dp", "seq"), None),
            P(None, ("dp", "seq"), None),
            P(None, ("dp", "seq")),
            P(None, ("dp", "seq")),
            P(),
            P(),
        ),
        check_vma=False,
    )
```

```python
from functools import partial

import jax
import jax.numpy as jnp
from jax import lax
from jax.experimental import pallas as pl
from jax.experimental.pallas import tpu as pltpu
from jax.sharding import PartitionSpec as P

HEADS = 12
HD = 64
L = 1
IMGS = 3
STEP_COUNT = 7

NORM_EPS = 1e-06
MASKED = -1000000000.0
SCALE = 0.125
BETA_ONE = 0.9
BETA_TWO = 0.999
ADAM_EPS = 1e-08
DECAY = 0.05
BASE_RATE = 0.05
LAYER_RATE = 0.75
CLIP_AT = 0.05
HIGH = lax.Precision.HIGHEST
BF = jnp.bfloat16
F32 = jnp.float32
AXES = ("dp", "seq")
D = 768
HALF = 384
PAIRS = HEADS // 4
RATES = (LAYER_RATE ** (L + 1), LAYER_RATE, LAYER_RATE, LAYER_RATE, LAYER_RATE, 1.0)


def pairs(move):
    dp_size, seq_size = lax.axis_size("dp"), lax.axis_size("seq")
    return [
        (d * seq_size + s, move(d, s)[0] * seq_size + move(d, s)[1])
        for d in range(dp_size)
        for s in range(seq_size)
    ]


def exchange(value, move):
    return lax.ppermute(value, AXES, pairs(move))


def along_z(step):
    return lambda d, s: (d ^ (2 * step), s)


def across_core(d, s):
    return (d, s ^ 1)


def across_first(d, s):
    return (d ^ 1, s) if s % 2 == 0 else (d, s ^ 2)


def across_second(d, s):
    return (d, s ^ 2) if s % 2 == 0 else (d ^ 1, s)


def swap(value):
    return exchange(value, across_core)


def spot():
    dp, seq = lax.axis_index("dp"), lax.axis_index("seq")
    return (dp // 2, dp % 2, seq // 2, seq % 2)


def total_of(value):
    for bit in range((lax.axis_size("seq") - 1).bit_length()):
        value = value + exchange(value, lambda d, s, bit=bit: (d, s ^ (1 << bit)))
    for bit in range((lax.axis_size("dp") - 1).bit_length()):
        value = value + exchange(value, lambda d, s, bit=bit: (d ^ (1 << bit), s))
    return value


def after(value, *others):
    return lax.optimization_barrier((value,) + others)[0]


def at(value, index, axis):
    return lax.dynamic_index_in_dim(value, index, axis, keepdims=False)


def in_core_order(core, mine, other, axis):
    return jnp.where(
        core == 0,
        jnp.concatenate([mine, other], axis),
        jnp.concatenate([other, mine], axis),
    )


def both_tokens(value):
    return jnp.concatenate([value, swap(value)], 0)


def to_columns(core, value):
    halves = value.reshape(value.shape[0], 2, HALF)
    return jnp.concatenate([at(halves, core, 1), swap(at(halves, 1 - core, 1))], 0)


def to_tokens(core, value):
    count = value.shape[0] // 2
    return in_core_order(core, value[:count], swap(value[count:]), 1)


def reduce_tokens(value):
    count = value.shape[0] // 2
    return value[:count] + swap(value[count:])


def cost(flops, byte_count):
    return pl.CostEstimate(flops=int(flops), bytes_accessed=int(byte_count), transcendentals=0)


def half_of(shard, parts, which):
    rows, wide = shard.shape
    return at(shard.reshape(rows, parts, 2, wide // parts // 2), which, 2).reshape(rows, -1)


def join_halves(core, mine, other, parts):
    rows = mine.shape[0]
    shape = (rows, parts, 1, mine.shape[1] // parts)
    return in_core_order(core, mine.reshape(shape), other.reshape(shape), 2).reshape(rows, -1)


def pad_lanes(value, width):
    return jnp.pad(value, ((0, 0), (0, width - value.shape[1])))


def assemble(pieces, places, z, plan, shapes):
    count = len(pieces)

    def body(where, *refs):
        ins, outs = refs[:count], refs[count:]
        for i in range(count):
            x, y = where[2 * i + 1], where[2 * i + 2]
            rows = ins[i].shape[1]
            for j in range(2):
                for o, row, lane in plan:
                    outs[o][(where[0] % 2) ^ j, x, y, row : row + rows, :] = ins[i][
                        j, :, lane : lane + outs[o].shape[-1]
                    ]

    def out_spec(shape):
        return pl.BlockSpec((2,) + shape[1:], lambda j, where: ((where[0] // 2) ^ j, 0, 0, 0, 0))

    slab = (2,) + pieces[0].shape[1:]
    size = 4 * pieces[0].size
    return pl.pallas_call(
        body,
        out_shape=[jax.ShapeDtypeStruct(s, BF) for s in shapes],
        grid_spec=pltpu.PrefetchScalarGridSpec(
            num_scalar_prefetch=1,
            grid=(pieces[0].shape[0] // 2,),
            in_specs=[pl.BlockSpec(slab, lambda j, where: (j, 0, 0))] * count,
            out_specs=[out_spec(s) for s in shapes],
        ),
        cost_estimate=cost(0, 4 * size),
        name="assemble",
    )(jnp.concatenate([jnp.stack([z]), places]).astype(jnp.int32), *pieces)


def gather_planes(units, plans):
    z, x, y, c = spot()
    places = jnp.stack([x, y, x ^ (1 - c), y ^ c, x ^ c, y ^ (1 - c), x ^ 1, y ^ 1])
    others = [exchange(units[0], along_z(1))]
    others += [exchange(after(u, others[0]), along_z(1)) for u in units[1:]]
    columns = [jnp.stack([u, o]) for u, o in zip(units, others)]

    def finish(n, own, near, *waits):
        side = exchange(own, across_second)
        far = exchange(after(near, *waits), across_second)
        plan, widths = plans[n]
        shapes = [(own.shape[0], 2, 2) + w for w in widths]
        return assemble([own, near, side, far], places, z, plan, shapes)

    owns, nears, last = [], [], ()
    for n in range(2):
        other = exchange(after(columns[n], *last), along_z(2))
        owns.append(jnp.concatenate([columns[n], after(other, *others)], 0))
        nears.append(exchange(owns[n], across_first))
        last = (owns[n],)
    weights = finish(0, owns[0], nears[0], owns[1]) + finish(1, owns[1], nears[1])
    third = exchange(after(columns[2], *last), along_z(2))

    def later(value):
        own = jnp.concatenate([columns[2], after(third, value)], 0)
        near = exchange(own, across_first)
        return finish(2, own, near), near

    return weights, others[0], (nears[1], third), later


def gather_weights(embedder, attend, merger, expand, shrink, readout, vectors):
    _, _, _, c = spot()
    low = [w.astype(BF) for w in (embedder, attend[0], merger[0], expand[0], shrink[0], readout)]
    embedder, attend, merger, expand, shrink, readout = low
    vectors = vectors.astype(BF)
    rows, chips = embedder.shape[0], lax.axis_size("dp") * lax.axis_size("seq") // 2
    tall, thin = vectors.shape
    wide = -(-readout.shape[2] // 128) * 128

    def chip_rows(mine, other):
        return in_core_order(c, mine, other, 0)

    def of_core(k):
        vec = jnp.pad(vectors, ((0, rows - tall), (0, 128 - thin)))
        first = [half_of(embedder, 1, k), vec, half_of(attend, 3, k)]
        second = [half_of(merger, 1, k), half_of(expand, chips, k), pad_lanes(at(readout, k, 0), wide)]
        return jnp.concatenate(first, 1), jnp.concatenate(second, 1)

    mine, give = of_core(c), of_core(1 - c)
    got = swap(give[0])
    front = chip_rows(mine[0], got)
    vec = in_core_order(c, vectors, got[:tall, HALF : HALF + thin], 1)
    vec = jnp.pad(vec, ((0, 2 * rows - tall), (0, 128 - 2 * thin)))
    back = chip_rows(mine[1], swap(give[1]))
    tall_shrink = shrink.shape[0]
    shrink = jnp.concatenate([shrink[: 2 * rows], shrink[2 * rows :]], 1)

    tall_rows = 2 * rows
    units = [
        jnp.concatenate([front[:, :HALF], vec, front[:, HALF + 128 :]], 1),
        back[:, : 5 * HALF],
        jnp.concatenate([shrink, back[:, 5 * HALF :]], 1),
    ]
    plans = [
        (
            [(0, 0, 0), (1, 0, HALF), (2, 0, HALF + 128)],
            [(tall_rows, HALF), (tall_rows, 128), (tall_rows, 3 * HALF)],
        ),
        ([(0, 0, 0), (1, 0, HALF)], [(tall_rows, HALF), (tall_rows, 4 * HALF)]),
        ([(0, 0, 0), (0, tall_rows, D), (1, 0, 2 * D)], [(tall_shrink, D), (tall_rows, wide)]),
    ]
    (emb, vec, att, mer, exp), first, cover, later = gather_planes(units, plans)

    def later_weights(value):
        (shr, rea), near = later(value)
        return shr.reshape(-1, D), rea.reshape(-1, wide), near

    vec = vec.reshape(chips, tall_rows, 128)[:, :tall, : 2 * thin].transpose(1, 0, 2)
    return (
        emb.reshape(-1, HALF),
        att.reshape(-1, 3 * HALF),
        mer.reshape(-1, HALF),
        exp.reshape(-1, 4 * HALF),
        vec.reshape(tall, -1),
        first,
        cover,
        later_weights,
    )


def gather_plain(embedder, attend, merger, expand, shrink, readout, vectors):
    _, _, _, c = spot()
    chips = lax.axis_size("dp") * lax.axis_size("seq") // 2
    wide = -(-readout.shape[2] // 128) * 128

    def whole_of(shard, axis):
        return lax.all_gather(shard.astype(BF), AXES, axis=axis, tiled=True)

    shrink = whole_of(shrink[0], 0).reshape(chips, 2, -1, D)
    return (
        half_of(whole_of(embedder, 0), 1, c),
        half_of(whole_of(attend[0], 0), 3, c),
        half_of(whole_of(merger[0], 0), 1, c),
        half_of(whole_of(expand[0], 0), chips, c),
        whole_of(vectors, 1),
        c,
        (c,),
        lambda value: (
            at(shrink, c, 1).reshape(-1, D),
            pad_lanes(at(whole_of(readout, 1), c, 0), wide),
            c,
        ),
    )


def blocks(grad):
    chips = lax.axis_size("dp") * lax.axis_size("seq") // 2
    return grad.reshape(chips // 4, 2, 2, grad.shape[0] // chips, grad.shape[1])


def lane_plan(grads, rows):
    plan, lane = [], 0
    for n, g in enumerate(grads):
        for row in range(0, g.shape[3], rows):
            plan.append((n, row, lane))
            lane += g.shape[4]
    return plan, lane


def position():
    return jnp.stack(spot()).astype(jnp.int32)


def chosen(grads, keep):
    def spec(g):
        def index(t, w):
            px = jnp.where(w[3] == 0, t, w[1] if keep else 1 - w[1])
            py = jnp.where(w[3] == 0, w[2] if keep else 1 - w[2], t)
            return (0, px, py, 0, 0)

        return pl.BlockSpec((g.shape[0], 1, 1) + g.shape[3:], index)

    return [spec(g) for g in grads]


def scatter_give(grads, rows):
    depth, count = grads[0].shape[0], len(grads)
    plan, lanes = lane_plan(grads, rows)

    def body(w, *refs):
        for n, row, lane in plan:
            block = refs[n][:, 0, 0, row : row + rows, :]
            refs[count][:, 0, :, lane : lane + block.shape[2]] = block

    give = pl.pallas_call(
        body,
        out_shape=jax.ShapeDtypeStruct((depth, 2, rows, lanes), BF),
        grid_spec=pltpu.PrefetchScalarGridSpec(
            num_scalar_prefetch=1,
            grid=(2,),
            in_specs=chosen(grads, False),
            out_specs=pl.BlockSpec((depth, 1, rows, lanes), lambda t, w: (0, t, 0, 0)),
        ),
        cost_estimate=cost(0, 8 * depth * rows * lanes),
        name="scatter_give",
    )(position(), *grads)
    return grads, rows, exchange(give, across_second), give


def scatter_near(state, *others):
    grads, rows, got, _ = state
    depth, count = grads[0].shape[0], len(grads)
    plan, lanes = lane_plan(grads, rows)

    def body(w, *refs):
        ins, got_ref, give_ref, keep_ref = refs[:count], refs[count], refs[count + 1], refs[count + 2]
        here = jnp.where(w[3] == 0, w[1], w[2])
        for n, row, lane in plan:
            block = ins[n][:, 0, 0, row : row + rows, :]
            span = slice(lane, lane + block.shape[2])
            value = block.astype(F32) + got_ref[:, 0, :, span].astype(F32)

            @pl.when(pl.program_id(0) == here)
            def _():
                keep_ref[:, :, span] = value

            @pl.when(pl.program_id(0) != here)
            def _():
                give_ref[:, :, span] = value.astype(BF)

    out = pl.BlockSpec((depth, rows, lanes), lambda t, w: (0, 0, 0))
    slab = pl.BlockSpec((depth, 1, rows, lanes), lambda t, w: (0, t, 0, 0))
    give, keep = pl.pallas_call(
        body,
        out_shape=[jax.ShapeDtypeStruct((depth, rows, lanes), t) for t in (BF, F32)],
        grid_spec=pltpu.PrefetchScalarGridSpec(
            num_scalar_prefetch=1,
            grid=(2,),
            in_specs=chosen(grads, True) + [slab],
            out_specs=[out, out],
        ),
        cost_estimate=cost(0, 14 * depth * rows * lanes),
        name="scatter_near",
    )(position(), *grads, after(got, *others))
    return keep, exchange(give, across_first)


def scatter_column(state, *others):
    keep, got = state
    depth, rows, lanes = keep.shape

    def body(w, keep_in, got_ref, keep_ref, give_ref):
        for j in range(depth):
            value = keep_in[w[0] ^ j] + got_ref[w[0] ^ j].astype(F32)
            if j < 2:
                keep_ref[j] = value
            else:
                give_ref[j - 2] = value.astype(BF)

    block = pl.BlockSpec((depth, rows, lanes), lambda t, w: (0, 0, 0))
    out = pl.BlockSpec((2, rows, lanes), lambda t, w: (0, 0, 0))
    keep, give = pl.pallas_call(
        body,
        out_shape=[jax.ShapeDtypeStruct((2, rows, lanes), t) for t in (F32, BF)],
        grid_spec=pltpu.PrefetchScalarGridSpec(
            num_scalar_prefetch=1, grid=(1,), in_specs=[block, block], out_specs=[out, out]
        ),
        cost_estimate=cost(0, 9 * depth * rows * lanes),
        name="scatter_column",
    )(position(), keep, after(got, *others))
    return keep, exchange(give, along_z(2))


def scatter_pair(state, *others):
    keep, got = state
    total = keep + after(got, *others).astype(F32)
    return total[0], exchange(total[1].astype(BF), along_z(1))


def scatter_end(state):
    return state[0] + state[1].astype(F32)


def own_rows(core, unit):
    halves = unit.reshape(2, unit.shape[0] // 2, unit.shape[1])
    return at(halves, core, 0), swap(at(halves, 1 - core, 0))


def first_done(state, classes):
    core = lax.axis_index("seq") % 2
    unit = scatter_end(state)
    shrink = jnp.concatenate([unit[:, :D], unit[:, D : 2 * D]], 0)
    mine, other = own_rows(core, unit[:, 2 * D :])
    return shrink, in_core_order(core, mine[None], other[None], 0)[:, :, :classes]


def second_done(state, wide):
    core = lax.axis_index("seq") % 2
    chips = lax.axis_size("dp") * lax.axis_size("seq") // 2
    mine, other = own_rows(core, scatter_end(state))
    return (
        join_halves(core, mine[:, :wide], other[:, :wide], chips),
        join_halves(core, mine[:, wide:], other[:, wide:], 1),
    )


def vector_blocks(vectors, like):
    chips = lax.axis_size("dp") * lax.axis_size("seq") // 2
    tall, thin = vectors.shape[0], vectors.shape[1] // chips
    vec = vectors.astype(BF).reshape(tall, chips, thin).transpose(1, 0, 2)
    vec = jnp.pad(vec, ((0, 0), (0, like.shape[3] - tall), (0, 128 - thin)))
    return vec.reshape(like.shape[:4] + (128,))


def last_done(attend, embedder, tall, thin):
    core = lax.axis_index("seq") % 2
    attend, unit = scatter_end(attend), scatter_end(embedder)
    rows = attend.shape[0] // 2
    pieces = unit[:tall, HALF : HALF + 2 * thin].reshape(tall, 2, thin)
    halves = jnp.concatenate([unit[:, :HALF], attend], 1).reshape(2, rows, -1)
    mine = at(halves, core, 0)
    sent = jnp.pad(at(pieces, 1 - core, 1), ((0, rows - tall), (0, 128 - thin)))
    got = swap(jnp.concatenate([at(halves, 1 - core, 0), sent], 1))
    wide = mine.shape[1]
    return (
        join_halves(core, mine[:, :HALF], got[:, :HALF], 1),
        join_halves(core, mine[:, HALF:], got[:, HALF:wide], 3),
        at(pieces, core, 1) + got[:tall, wide : wide + thin],
    )


def scatter_plain(grads, classes):
    embedder, attend, merger, expand, shrink, readout, vectors = grads
    _, _, _, c = spot()
    chips = lax.axis_size("dp") * lax.axis_size("seq") // 2

    def reduced(value, axis):
        value = value.astype(F32)
        return lax.psum_scatter(value, AXES, scatter_dimension=axis, tiled=True)

    def spread(half, parts):
        return reduced(join_halves(c, half, jnp.zeros_like(half), parts), 0)

    tall = shrink.reshape(chips, 1, -1, D)
    tall = in_core_order(c, tall, jnp.zeros_like(tall), 1).reshape(-1, D)
    pair = in_core_order(c, readout[None], jnp.zeros_like(readout)[None], 0)
    return (
        spread(embedder, 1),
        spread(attend, 3),
        spread(merger, 1),
        spread(expand, chips),
        reduced(tall, 0),
        reduced(pair, 1)[:, :, :classes],
        reduced(vectors, 1),
    )


def dot_keys(left, right):
    return lax.dot_general(left, right, (((1,), (1,)), ((), ())), preferred_element_type=F32)


def turned(value):
    return value.astype(F32).T.astype(BF)


def chunks_of(count):
    size = 256 if count % 256 == 0 else count
    return [slice(start, start + size) for start in range(0, count, size)]


def attend_forward(q_ref, k_ref, v_ref, qm_ref, km_ref, out_ref, exact_ref, lse_ref, keys, values, raws):
    lane = lax.broadcasted_iota(jnp.int32, (1, 2 * HD), 1) // HD
    chunks = chunks_of(k_ref.shape[0])

    @pl.when(pl.program_id(1) == 0)
    def _():
        for h in range(2):
            keys[h] = jnp.where(lane == h, k_ref[...], km_ref[...])
        values[...] = turned(v_ref[...])

    query = q_ref[...] * jnp.asarray(SCALE, BF)
    tops, parts = [], []
    for h in range(2):
        query_h = jnp.where(lane == h, query, qm_ref[...])
        top = None
        for chunk in chunks:
            raw = dot_keys(keys[h, chunk, :], query_h)
            raws[h, chunk, :] = raw
            high = jnp.max(raw, 0, keepdims=True)
            top = high if top is None else jnp.maximum(top, high)
        tops.append(top)
    for h in range(2):
        mass, part = 0.0, 0.0
        for chunk in chunks:
            heavy = jnp.exp(raws[h, chunk, :] - tops[h])
            mass = mass + jnp.sum(heavy, 0, keepdims=True)
            side = values[HD * h : HD * (h + 1), chunk]
            part = part + jnp.dot(side, heavy.astype(BF), preferred_element_type=F32)
        parts.append(part * (1.0 / mass))
        lse_ref[0, h : h + 1, :] = tops[h] + jnp.log(mass)
    mixed = jnp.concatenate(parts, 0).T
    exact_ref[...] = mixed
    out_ref[...] = mixed.astype(BF)


def attend_backward(joined, q_ref, k_ref, v_ref, do_ref, exact_ref, lse_ref, qm_ref, km_ref, *refs):
    outs, (keys, turned_keys, grad_keys, grad_values) = refs[:-4], refs[-4:]
    lane = lax.broadcasted_iota(jnp.int32, (1, 2 * HD), 1) // HD
    pair, step = pl.program_id(0), pl.program_id(1)

    @pl.when(step == 0)
    def _():
        for h in range(2):
            keys[h] = jnp.where(lane == h, k_ref[...], km_ref[...])
        turned_keys[...] = turned(k_ref[...])
        grad_keys[...] = jnp.zeros_like(grad_keys)
        grad_values[...] = jnp.zeros_like(grad_values)

    query = q_ref[...] * jnp.asarray(SCALE, BF)
    grad = do_ref[...]
    spreads = (grad.astype(F32) * exact_ref[...]).T
    of_head = []
    for h in range(2):
        zero = jnp.zeros_like(query)
        of_head.append(
            (
                jnp.where(lane == h, query, qm_ref[...]),
                jnp.where(lane == h, query, zero),
                jnp.where(lane == h, grad, zero),
                jnp.sum(spreads[HD * h : HD * (h + 1)], 0, keepdims=True),
                lse_ref[0, h : h + 1, :],
            )
        )
    parts = []
    for h, (query_m, query_h, grad_h, spread, lse) in enumerate(of_head):
        shares = jnp.exp(dot_keys(keys[h], query_m) - lse)
        grad_raw = (shares * (dot_keys(v_ref[...], grad_h) - spread)).astype(BF)
        side = turned_keys[HD * h : HD * (h + 1), :]
        parts.append(jnp.dot(side, grad_raw, preferred_element_type=F32))
        grad_keys[...] += jnp.dot(grad_raw, query_h, preferred_element_type=F32)
        grad_values[...] += jnp.dot(shares.astype(BF), grad_h, preferred_element_type=F32)
    grad_query = (jnp.concatenate(parts, 0).T * SCALE).astype(BF)
    if joined:
        rows = grad_query.shape[0]
        down = pl.ds(pl.multiple_of(step * rows, rows), rows)
        outs[0][down, pl.ds(pl.multiple_of(pair * 128, 128), 128)] = grad_query
    else:
        outs[0][...] = grad_query

    @pl.when(step == pl.num_programs(1) - 1)
    def _():
        if joined:
            across = pl.num_programs(0)
            for n, total in enumerate((grad_keys, grad_values)):
                place = (pair + across * (n + 1)) * 128
                outs[0][:, pl.ds(pl.multiple_of(place, 128), 128)] = total[...].astype(BF)
        else:
            outs[1][...] = grad_keys[...]
            outs[2][...] = grad_values[...]


def tile_of(count):
    return 256 if count % 256 == 0 else count


def mix_tokens(projected, around, mask_q, mask_k):
    nq, nk = projected.shape[0], around.shape[0]
    tile = tile_of(nq)
    rows = lambda part: pl.BlockSpec((tile, 128), lambda i, j: (j, part * PAIRS + i))
    tall = lambda part: pl.BlockSpec((nk, 128), lambda i, j: (0, part * PAIRS + i))
    return pl.pallas_call(
        attend_forward,
        grid=(PAIRS, nq // tile),
        in_specs=[
            rows(0),
            tall(1),
            tall(2),
            pl.BlockSpec((tile, 128), lambda i, j: (j, 0)),
            pl.BlockSpec((nk, 128), lambda i, j: (0, 0)),
        ],
        out_specs=[rows(0), rows(0), pl.BlockSpec((1, 2, tile), lambda i, j: (i, 0, j))],
        out_shape=[
            jax.ShapeDtypeStruct((nq, HALF), BF),
            jax.ShapeDtypeStruct((nq, HALF), F32),
            jax.ShapeDtypeStruct((PAIRS, 2, nq), F32),
        ],
        scratch_shapes=[
            pltpu.VMEM((2, nk, 128), BF),
            pltpu.VMEM((128, nk), BF),
            pltpu.VMEM((2, nk, tile), F32),
        ],
        cost_estimate=cost(nq * nk * HALF, nq * HALF),
        name="attend_forward",
    )(projected, around, around, mask_q, mask_k)


def mix_back(projected, around, grad, exact, lse, mask_q, mask_k):
    nq, nk = projected.shape[0], around.shape[0]
    tile, joined = tile_of(nq), nq == nk
    rows = lambda part: pl.BlockSpec((tile, 128), lambda i, j: (j, part * PAIRS + i))
    tall = lambda part: pl.BlockSpec((nk, 128), lambda i, j: (0, part * PAIRS + i))
    if joined:
        out_specs = [pl.BlockSpec((nq, 3 * HALF), lambda i, j: (0, 0))]
        out_shape = [jax.ShapeDtypeStruct((nq, 3 * HALF), BF)]
    else:
        out_specs = [rows(0), tall(0), tall(0)]
        out_shape = [jax.ShapeDtypeStruct((nq, HALF), BF)]
        out_shape += [jax.ShapeDtypeStruct((nk, HALF), F32)] * 2
    return pl.pallas_call(
        partial(attend_backward, joined),
        grid=(PAIRS, nq // tile),
        in_specs=[
            rows(0),
            tall(1),
            tall(2),
            rows(0),
            rows(0),
            pl.BlockSpec((1, 2, tile), lambda i, j: (i, 0, j)),
            pl.BlockSpec((tile, 128), lambda i, j: (j, 0)),
            pl.BlockSpec((nk, 128), lambda i, j: (0, 0)),
        ],
        out_specs=out_specs,
        out_shape=out_shape,
        scratch_shapes=[
            pltpu.VMEM((2, nk, 128), BF),
            pltpu.VMEM((128, nk), BF),
            pltpu.VMEM((nk, 128), F32),
            pltpu.VMEM((nk, 128), F32),
        ],
        cost_estimate=cost(nq * nk * HALF, nq * HALF),
        name="attend_backward",
    )(projected, around, around, grad, exact, lse, mask_q, mask_k)


def norm_parts(x):
    centre = x - jnp.mean(x, -1, keepdims=True)
    rate = lax.rsqrt(jnp.mean(centre * centre, -1, keepdims=True) + NORM_EPS)
    return (centre * rate, rate)


def layer_norm(x, gain, shift):
    return norm_parts(x)[0] * gain + shift


def norm_back(x, gain, grad):
    unit, rate = norm_parts(x)
    inner_grad = grad * gain
    back = rate * (
        inner_grad
        - jnp.mean(inner_grad, -1, keepdims=True)
        - unit * jnp.mean(inner_grad * unit, -1, keepdims=True)
    )
    return (back, jnp.sum(grad * unit, 0), jnp.sum(grad, 0))


def matmul(left, right):
    return jnp.dot(left, right, preferred_element_type=F32)


def outer(left, right):
    return lax.dot_general(left, right, (((0,), (0,)), ((), ())), preferred_element_type=F32)


def inner(grad, weight):
    return lax.dot_general(grad, weight, (((1,), (1,)), ((), ())), preferred_element_type=F32)


def chip_bits():
    return [2 << b for b in range((lax.axis_size("seq") // 4 - 1).bit_length())]


def of_bit(value, bit):
    return exchange(value, lambda d, s: (d, s ^ bit))


def row_tokens(value):
    for bit in chip_bits():
        value = jnp.concatenate([value, of_bit(value, bit)], 0)
    return value


def row_return(value):
    for bit in reversed(chip_bits()):
        half = value.shape[0] // 2
        value = value[:half] + of_bit(value[half:].astype(BF), bit).astype(F32)
    return value


def row_sum(value):
    for bit in chip_bits():
        value = value + of_bit(value, bit)
    return value


def segment_lanes(segment, of_query):
    lane = jnp.arange(128, dtype=jnp.int32) % HD
    hit = segment[:, None] == lane[None, :]
    if of_query:
        return jnp.where(hit | (lane > IMGS)[None, :], 0.0, MASKED).astype(BF)
    return hit.astype(BF)


def adamw(weight, mean, square, grad, scale, decay):
    mean_next = BETA_ONE * mean + (1.0 - BETA_ONE) * grad
    square_next = BETA_TWO * square + (1.0 - BETA_TWO) * grad * grad
    mean_hat = mean_next / (1.0 - BETA_ONE**STEP_COUNT)
    square_hat = square_next / (1.0 - BETA_TWO**STEP_COUNT)
    weight_next = weight - BASE_RATE * scale * (
        mean_hat / (jnp.sqrt(square_hat) + ADAM_EPS) + decay * weight
    )
    return (weight_next, mean_next, square_next)


def moments(mean, square, grad):
    return (
        BETA_ONE * mean + (1.0 - BETA_ONE) * grad,
        BETA_TWO * square + (1.0 - BETA_TWO) * grad * grad,
    )


def on_device(
    pixels,
    lengths,
    labels,
    teacher,
    embedder,
    embedder_mean,
    embedder_square,
    attend,
    attend_mean,
    attend_square,
    merger,
    merger_mean,
    merger_square,
    expand,
    expand_mean,
    expand_square,
    shrink,
    shrink_mean,
    shrink_square,
    readout,
    readout_mean,
    readout_square,
    vectors,
    vectors_mean,
    vectors_square,
):
    seq_size, dp_size = lax.axis_size("seq"), lax.axis_size("dp")
    fast = seq_size == 4 and dp_size == 8 and embedder.shape[0] == 24
    seq, core = lax.axis_index("seq"), lax.axis_index("seq") % 2
    local, far = pixels.shape[1], seq_size // 2
    span = seq_size // 4
    classes = readout.shape[2]
    image_count = lengths.shape[0] * dp_size * IMGS

    gather = gather_weights if fast else gather_plain
    embed_w, attend_w, merger_half, expand_w, vector_w, first, cover, later_weights = gather(
        embedder, attend, merger, expand, shrink, readout, vectors
    )

    side = seq // far
    pixels = after(pixels, first)
    pixels_got = of_bit(at(pixels, 1 - side, 0), far)
    tokens = jnp.concatenate([at(pixels, side, 0), pixels_got], 0)
    all_pixels = both_tokens(tokens)
    row_lengths = at(lengths, side, 0)
    row_labels = at(labels, side, 0)
    row_teacher = at(teacher, side, 0)

    def places_of(where):
        step = jnp.arange(local, dtype=jnp.int32)
        return jnp.concatenate([where * local + step, (where ^ far) * local + step])

    places = places_of(seq)
    ends = jnp.cumsum(row_lengths)
    starts = ends - row_lengths

    def segment_of(spots):
        return jnp.sum((spots[:, None] >= ends[None, :]).astype(jnp.int32), 1)

    seg_q = segment_of(jnp.concatenate([places, places_of(seq ^ 1)]))
    order = [0]
    for bit in chip_bits():
        order = order + [o ^ bit for o in order]
    seg_k = segment_of(jnp.concatenate([places_of(seq ^ o ^ k) for o in order for k in range(2)]))
    mask_q, mask_k = segment_lanes(seg_q, True), segment_lanes(seg_k, False)
    marks = jnp.concatenate([starts, starts + 1])
    hits = (marks[:, None] == places[None, :]).astype(F32)
    token_hits = (places[:, None] == marks[None, :]).astype(F32)
    is_cls, is_dist = jnp.sum(hits[:IMGS], 0), jnp.sum(hits[IMGS:], 0)
    is_patch = (seg_q[: 2 * local] < IMGS).astype(F32) - is_cls - is_dist

    merger_w = in_core_order(core, merger_half, swap(merger_half), 1)
    vector_f = vector_w.astype(F32)

    patches = to_tokens(core, matmul(all_pixels, embed_w))
    x = (
        is_patch[:, None] * patches
        + is_cls[:, None] * vector_f[4 * L + 2]
        + is_dist[:, None] * vector_f[4 * L + 3]
    )
    a = both_tokens(layer_norm(x, vector_f[0], vector_f[1]).astype(BF))
    projected = matmul(a, attend_w).astype(BF)
    around = row_tokens(projected)
    mixed_half, exact, lse = mix_tokens(projected, around, mask_q, mask_k)
    mixed_half = after(mixed_half, *cover)
    shrink_w, readout_w, near = later_weights(mixed_half)
    other = swap(mixed_half)
    count = 2 * local
    other = jnp.concatenate([other[count:], other[:count]], 0)
    mixed = in_core_order(core, mixed_half, other, 1)
    x_mid = x + matmul(mixed[:count], merger_w)
    normed = both_tokens(layer_norm(x_mid, vector_f[2], vector_f[3]).astype(BF))
    hidden_in = matmul(after(normed, near), expand_w)
    cdf = 0.5 * (1.0 + lax.erf(hidden_in * (0.5**0.5)))
    hidden = (hidden_in * cdf).astype(BF)
    slope = cdf + hidden_in * jnp.exp(-0.5 * hidden_in * hidden_in) * ((0.5 / jnp.pi) ** 0.5)
    x_last = x_mid + reduce_tokens(matmul(hidden, shrink_w))

    label_hot = (row_labels[:, None] == jnp.arange(classes, dtype=jnp.int32)).astype(F32)
    teach_log = jax.nn.log_softmax(row_teacher, -1)
    target = jnp.where(core == 0, label_hot, jnp.exp(teach_log))
    target_log = jnp.where(core == 0, 0.0, teach_log)
    gain, shift = vector_f[4 * L], vector_f[4 * L + 1]
    rows = row_sum(jnp.dot(hits, x_last, precision=HIGH)).reshape(2, IMGS, D)
    rows = at(rows, core, 0) + swap(at(rows, 1 - core, 0))
    unit, rate = norm_parts(rows)
    head_in = (unit * gain + shift).astype(BF)
    logits = matmul(head_in, readout_w)[:, :classes]
    log_share = jax.nn.log_softmax(logits, -1)
    loss_local = jnp.sum(0.5 * target * (target_log - log_share)) / span
    grad_logits = pad_lanes(
        0.5 * (jnp.exp(log_share) - target) / image_count, readout_w.shape[1]
    )
    grad_readout = lax.dot_general(
        head_in.astype(F32), grad_logits / span, (((0,), (0,)), ((), ())), precision=HIGH
    )
    grad_head = lax.dot_general(
        grad_logits, readout_w.astype(F32), (((1,), (1,)), ((), ())), precision=HIGH
    )
    head_back, gain_out, shift_out = norm_back(rows, gain, grad_head)
    back = in_core_order(core, head_back, swap(head_back), 0)

    grad_out = jnp.dot(token_hits, back, precision=HIGH)
    grad_branch = both_tokens(grad_out.astype(BF))
    grad_shrink = outer(hidden, grad_branch).astype(BF)
    grad_readout = grad_readout.astype(BF)
    if fast:
        parts = [blocks(grad_shrink), blocks(grad_readout)]
        unit_rows = parts[1].shape[3]
        first = scatter_give(parts, unit_rows)
    grad_pre = (inner(grad_branch, shrink_w) * slope).astype(BF)
    grad_expand = outer(normed, grad_pre).astype(BF)
    grad_normed, gain_two, shift_two = norm_back(
        x_mid, vector_f[2], reduce_tokens(inner(grad_pre, expand_w))
    )
    grad_mid = grad_out + grad_normed
    grad_attn = both_tokens(grad_mid.astype(BF))
    attn_half = at(grad_attn.reshape(-1, 2, HALF), core, 1)
    grad_merger = outer(mixed, attn_half).astype(BF)
    if fast:
        second = scatter_give([blocks(grad_expand), blocks(grad_merger)], unit_rows)
    grad_mixed = inner(grad_attn, at(merger_w.reshape(2, HALF, D), core, 0)).astype(BF)
    if fast:
        grad_mixed = after(grad_mixed, second[3])
    grads = mix_back(projected, around, grad_mixed, exact, lse, mask_q, mask_k)
    if len(grads) == 1:
        grad_proj = grads[0]
    else:
        grad_proj = jnp.concatenate([grads[0]] + [row_return(g).astype(BF) for g in grads[1:]], 1)
    if fast:
        first = scatter_near(first, grad_proj)
        grad_proj = after(grad_proj, first[0], second[2])
    grad_a = inner(grad_proj, attend_w)
    grad_attend = outer(a, grad_proj).astype(BF)
    if fast:
        third = scatter_give([blocks(grad_attend)], unit_rows)
        first = scatter_column(first, third[3])
        second = scatter_near(second, first[0])
    grad_input, gain_one, shift_one = norm_back(x, vector_f[0], reduce_tokens(grad_a))
    grad_x = grad_mid + grad_input
    grad_patch = (grad_x * is_patch[:, None]).astype(BF)
    grad_embed = outer(all_pixels, to_columns(core, grad_patch)).astype(BF)
    grad_vectors = jnp.stack(
        [
            gain_one,
            shift_one,
            gain_two,
            shift_two,
            gain_out / span,
            shift_out / span,
            jnp.sum(grad_x * is_cls[:, None], 0),
            jnp.sum(grad_x * is_dist[:, None], 0),
        ]
    )
    if fast:
        parts = [blocks(grad_embed)]
        fourth = scatter_give(parts + [vector_blocks(grad_vectors, parts[0])], unit_rows)
        third = scatter_near(third, grad_embed)
        second = scatter_column(second, grad_embed)
        fourth = scatter_near(fourth)
        first = scatter_pair(first, fourth[0])
        third = scatter_column(third)
        fourth = scatter_column(fourth)
        second = scatter_pair(second, fourth[0])
        third, fourth = scatter_pair(third), scatter_pair(fourth)
        sum_shrink, sum_readout = first_done(first, classes)
        sum_expand, sum_merger = second_done(second, grad_expand.shape[1])
        sum_embed, sum_attend, sum_vectors = last_done(third, fourth, *vectors.shape)
    else:
        sum_embed, sum_attend, sum_merger, sum_expand, sum_shrink, sum_readout, sum_vectors = (
            scatter_plain(
                (grad_embed, grad_attend, grad_merger, grad_expand)
                + (grad_shrink, grad_readout, grad_vectors),
                classes,
            )
        )
    reduced = (sum_embed, sum_attend, sum_merger, sum_expand, sum_shrink, sum_readout)
    square_sum = sum((jnp.sum(g * g) for g in reduced)) + jnp.sum(sum_vectors * sum_vectors)
    both = total_of(jnp.stack([square_sum, loss_local])[None, :])
    grad_norm = jnp.sqrt(both[0, 0])
    factor = jnp.minimum(1.0, CLIP_AT / (grad_norm + 1e-06))

    masters = (embedder, attend, merger, expand, shrink, readout)
    means = (embedder_mean, attend_mean, merger_mean, expand_mean, shrink_mean, readout_mean)
    squares = (
        embedder_square,
        attend_square,
        merger_square,
        expand_square,
        shrink_square,
        readout_square,
    )
    outs = []
    for j in range(6):
        grad = reduced[j].reshape(masters[j].shape) * factor
        outs += adamw(masters[j], means[j], squares[j], grad, RATES[j], DECAY)
    outs += moments(vectors_mean, vectors_square, sum_vectors * factor)
    return tuple(outs) + (both[0, 1] / image_count, grad_norm)


def solution(mesh):
    return jax.shard_map(
        on_device,
        mesh=mesh,
        in_specs=(
            P("dp", "seq", None),
            P("dp", None),
            P("dp", None),
            P("dp", None, None),
            P(("dp", "seq"), None),
            P(("dp", "seq"), None),
            P(("dp", "seq"), None),
            P(None, ("dp", "seq"), None),
            P(None, ("dp", "seq"), None),
            P(None, ("dp", "seq"), None),
            P(None, ("dp", "seq"), None),
            P(None, ("dp", "seq"), None),
            P(None, ("dp", "seq"), None),
            P(None, ("dp", "seq"), None),
            P(None, ("dp", "seq"), None),
            P(None, ("dp", "seq"), None),
            P(None, ("dp", "seq"), None),
            P(None, ("dp", "seq"), None),
            P(None, ("dp", "seq"), None),
            P(None, ("dp", "seq"), None),
            P(None, ("dp", "seq"), None),
            P(None, ("dp", "seq"), None),
            P(None, ("dp", "seq")),
            P(None, ("dp", "seq")),
            P(None, ("dp", "seq")),
        ),
        out_specs=(
            P(("dp", "seq"), None),
            P(("dp", "seq"), None),
            P(("dp", "seq"), None),
            P(None, ("dp", "seq"), None),
            P(None, ("dp", "seq"), None),
            P(None, ("dp", "seq"), None),
            P(None, ("dp", "seq"), None),
            P(None, ("dp", "seq"), None),
            P(None, ("dp", "seq"), None),
            P(None, ("dp", "seq"), None),
            P(None, ("dp", "seq"), None),
            P(None, ("dp", "seq"), None),
            P(None, ("dp", "seq"), None),
            P(None, ("dp", "seq"), None),
            P(None, ("dp", "seq"), None),
            P(None, ("dp", "seq"), None),
            P(None, ("dp", "seq"), None),
            P(None, ("dp", "seq"), None),
            P(None, ("dp", "seq")),
            P(None, ("dp", "seq")),
            P(),
            P(),
        ),
        check_vma=False,
    )
```

```python
from functools import partial

import jax
import jax.numpy as jnp
from jax import lax
from jax.experimental import pallas as pl
from jax.experimental.pallas import tpu as pltpu
from jax.sharding import PartitionSpec as P

HEADS = 12
HD = 64
L = 1
IMGS = 3
STEP_COUNT = 7

NORM_EPS = 1e-06
MASKED = -1000000000.0
SCALE = 0.125
BETA_ONE = 0.9
BETA_TWO = 0.999
ADAM_EPS = 1e-08
DECAY = 0.05
BASE_RATE = 0.05
LAYER_RATE = 0.75
CLIP_AT = 0.05
HIGH = lax.Precision.HIGHEST
BF = jnp.bfloat16
F32 = jnp.float32
AXES = ("dp", "seq")
D = 768
HALF = 384
PAIRS = HEADS // 4
RATES = (LAYER_RATE ** (L + 1), LAYER_RATE, LAYER_RATE, LAYER_RATE, LAYER_RATE, 1.0)


def pairs(move):
    dp_size, seq_size = lax.axis_size("dp"), lax.axis_size("seq")
    return [
        (d * seq_size + s, move(d, s)[0] * seq_size + move(d, s)[1])
        for d in range(dp_size)
        for s in range(seq_size)
    ]


def exchange(value, move):
    return lax.ppermute(value, AXES, pairs(move))


def along_z(step):
    return lambda d, s: (d ^ (2 * step), s)


def across_core(d, s):
    return (d, s ^ 1)


def across_first(d, s):
    return (d ^ 1, s) if s % 2 == 0 else (d, s ^ 2)


def across_second(d, s):
    return (d, s ^ 2) if s % 2 == 0 else (d ^ 1, s)


def swap(value):
    return exchange(value, across_core)


def spot():
    dp, seq = lax.axis_index("dp"), lax.axis_index("seq")
    return (dp // 2, dp % 2, seq // 2, seq % 2)


def total_of(value, beside=()):
    hops = [(0, 1 << b) for b in range((lax.axis_size("seq") - 1).bit_length())]
    hops += [(1 << b, 0) for b in range((lax.axis_size("dp") - 1).bit_length())]
    for n, (of_dp, of_seq) in enumerate(hops):
        got = exchange(value, lambda d, s: (d ^ of_dp, s ^ of_seq))
        value = value + after(got, *beside[n : n + 1])
    return value


def after(value, *others):
    return lax.optimization_barrier((value,) + others)[0]


def at(value, index, axis):
    return lax.dynamic_index_in_dim(value, index, axis, keepdims=False)


def in_core_order(core, mine, other, axis):
    return jnp.where(
        core == 0,
        jnp.concatenate([mine, other], axis),
        jnp.concatenate([other, mine], axis),
    )


def both_tokens(value):
    return jnp.concatenate([value, swap(value)], 0)


def to_columns(core, value):
    halves = value.reshape(value.shape[0], 2, HALF)
    return jnp.concatenate([at(halves, core, 1), swap(at(halves, 1 - core, 1))], 0)


def to_tokens(core, value):
    count = value.shape[0] // 2
    return in_core_order(core, value[:count], swap(value[count:]), 1)


def with_other(product):
    return product, swap(product[product.shape[0] // 2 :])


def cost(flops, byte_count):
    return pl.CostEstimate(flops=int(flops), bytes_accessed=int(byte_count), transcendentals=0)


def half_of(shard, parts, which):
    rows, wide = shard.shape
    return at(shard.reshape(rows, parts, 2, wide // parts // 2), which, 2).reshape(rows, -1)


def join_halves(core, mine, other, parts):
    rows = mine.shape[0]
    shape = (rows, parts, 1, mine.shape[1] // parts)
    return in_core_order(core, mine.reshape(shape), other.reshape(shape), 2).reshape(rows, -1)


def pad_lanes(value, width):
    return jnp.pad(value, ((0, 0), (0, width - value.shape[1])))


def assemble(pieces, places, z, plan, shapes):
    count = len(pieces)

    def body(where, *refs):
        ins, outs = refs[:count], refs[count:]
        for i in range(count):
            x, y = where[2 * i + 1], where[2 * i + 2]
            rows = ins[i].shape[1]
            for j in range(2):
                for o, row, lane in plan:
                    outs[o][(where[0] % 2) ^ j, x, y, row : row + rows, :] = ins[i][
                        j, :, lane : lane + outs[o].shape[-1]
                    ]

    def out_spec(shape):
        return pl.BlockSpec((2,) + shape[1:], lambda j, where: ((where[0] // 2) ^ j, 0, 0, 0, 0))

    slab = (2,) + pieces[0].shape[1:]
    size = 4 * pieces[0].size
    return pl.pallas_call(
        body,
        out_shape=[jax.ShapeDtypeStruct(s, BF) for s in shapes],
        grid_spec=pltpu.PrefetchScalarGridSpec(
            num_scalar_prefetch=1,
            grid=(pieces[0].shape[0] // 2,),
            in_specs=[pl.BlockSpec(slab, lambda j, where: (j, 0, 0))] * count,
            out_specs=[out_spec(s) for s in shapes],
        ),
        cost_estimate=cost(0, 4 * size),
        name="assemble",
    )(jnp.concatenate([jnp.stack([z]), places]).astype(jnp.int32), *pieces)


def gather_planes(units, plans):
    z, x, y, c = spot()
    places = jnp.stack([x, y, x ^ (1 - c), y ^ c, x ^ c, y ^ (1 - c), x ^ 1, y ^ 1])
    others = [exchange(units[0], along_z(1))]
    others += [exchange(after(u, others[0]), along_z(1)) for u in units[1:]]
    columns = [jnp.stack([u, o]) for u, o in zip(units, others)]

    def finish(n, own, near, *waits):
        side = exchange(own, across_second)
        far = exchange(after(near, *waits), across_second)
        plan, widths = plans[n]
        shapes = [(own.shape[0], 2, 2) + w for w in widths]
        return assemble([own, near, side, far], places, z, plan, shapes)

    owns, nears, last = [], [], ()
    for n in range(2):
        other = exchange(after(columns[n], *last), along_z(2))
        owns.append(jnp.concatenate([columns[n], after(other, *others)], 0))
        nears.append(exchange(owns[n], across_first))
        last = (owns[n],)
    weights = finish(0, owns[0], nears[0], owns[1]) + finish(1, owns[1], nears[1])
    third = exchange(after(columns[2], *last), along_z(2))

    def later(value):
        own = jnp.concatenate([columns[2], after(third, value)], 0)
        near = exchange(own, across_first)
        return finish(2, own, near), near

    return weights, others[0], (nears[1], third), later


def gather_weights(embedder, attend, merger, expand, shrink, readout, vectors):
    _, _, _, c = spot()
    low = [w.astype(BF) for w in (embedder, attend[0], merger[0], expand[0], shrink[0], readout)]
    embedder, attend, merger, expand, shrink, readout = low
    vectors = vectors.astype(BF)
    rows, chips = embedder.shape[0], lax.axis_size("dp") * lax.axis_size("seq") // 2
    tall, thin = vectors.shape
    wide = -(-readout.shape[2] // 128) * 128

    def chip_rows(mine, other):
        return in_core_order(c, mine, other, 0)

    def of_core(k):
        vec = jnp.pad(vectors, ((0, rows - tall), (0, 128 - thin)))
        first = [half_of(embedder, 1, k), vec, half_of(attend, 3, k)]
        second = [half_of(merger, 1, k), half_of(expand, chips, k), pad_lanes(at(readout, k, 0), wide)]
        return jnp.concatenate(first, 1), jnp.concatenate(second, 1)

    mine, give = of_core(c), of_core(1 - c)
    got = swap(give[0])
    front = chip_rows(mine[0], got)
    vec = in_core_order(c, vectors, got[:tall, HALF : HALF + thin], 1)
    vec = jnp.pad(vec, ((0, 2 * rows - tall), (0, 128 - 2 * thin)))
    back = chip_rows(mine[1], swap(give[1]))
    tall_shrink = shrink.shape[0]
    shrink = jnp.concatenate([shrink[: 2 * rows], shrink[2 * rows :]], 1)

    tall_rows = 2 * rows
    units = [
        jnp.concatenate([front[:, :HALF], vec, front[:, HALF + 128 :]], 1),
        back[:, : 5 * HALF],
        jnp.concatenate([shrink, back[:, 5 * HALF :]], 1),
    ]
    plans = [
        (
            [(0, 0, 0), (1, 0, HALF), (2, 0, HALF + 128)],
            [(tall_rows, HALF), (tall_rows, 128), (tall_rows, 3 * HALF)],
        ),
        ([(0, 0, 0), (1, 0, HALF)], [(tall_rows, HALF), (tall_rows, 4 * HALF)]),
        ([(0, 0, 0), (0, tall_rows, D), (1, 0, 2 * D)], [(tall_shrink, D), (tall_rows, wide)]),
    ]
    (emb, vec, att, mer, exp), first, cover, later = gather_planes(units, plans)

    def later_weights(value):
        (shr, rea), near = later(value)
        return shr.reshape(-1, D), rea.reshape(-1, wide), near

    vec = vec.reshape(chips, tall_rows, 128)[:, :tall, : 2 * thin].transpose(1, 0, 2)
    return (
        emb.reshape(-1, HALF),
        att.reshape(-1, 3 * HALF),
        mer.reshape(-1, HALF),
        exp.reshape(-1, 4 * HALF),
        vec.reshape(tall, -1),
        first,
        cover,
        later_weights,
    )


def gather_plain(embedder, attend, merger, expand, shrink, readout, vectors):
    _, _, _, c = spot()
    chips = lax.axis_size("dp") * lax.axis_size("seq") // 2
    wide = -(-readout.shape[2] // 128) * 128

    def whole_of(shard, axis):
        return lax.all_gather(shard.astype(BF), AXES, axis=axis, tiled=True)

    shrink = whole_of(shrink[0], 0).reshape(chips, 2, -1, D)
    return (
        half_of(whole_of(embedder, 0), 1, c),
        half_of(whole_of(attend[0], 0), 3, c),
        half_of(whole_of(merger[0], 0), 1, c),
        half_of(whole_of(expand[0], 0), chips, c),
        whole_of(vectors, 1),
        c,
        (c,),
        lambda value: (
            at(shrink, c, 1).reshape(-1, D),
            pad_lanes(at(whole_of(readout, 1), c, 0), wide),
            c,
        ),
    )


def blocks(grad):
    chips = lax.axis_size("dp") * lax.axis_size("seq") // 2
    return grad.reshape(chips // 4, 2, 2, grad.shape[0] // chips, grad.shape[1])


def lane_plan(grads, rows):
    plan, lane = [], 0
    for n, g in enumerate(grads):
        for row in range(0, g.shape[3], rows):
            plan.append((n, row, lane))
            lane += g.shape[4]
    return plan, lane


def position():
    return jnp.stack(spot()).astype(jnp.int32)


def chosen(grads, keep):
    def spec(g):
        def index(t, w):
            px = jnp.where(w[3] == 0, t, w[1] if keep else 1 - w[1])
            py = jnp.where(w[3] == 0, w[2] if keep else 1 - w[2], t)
            return (0, px, py, 0, 0)

        return pl.BlockSpec((g.shape[0], 1, 1) + g.shape[3:], index)

    return [spec(g) for g in grads]


def scatter_give(grads, rows):
    depth, count = grads[0].shape[0], len(grads)
    plan, lanes = lane_plan(grads, rows)

    def body(w, *refs):
        for n, row, lane in plan:
            block = refs[n][:, 0, 0, row : row + rows, :]
            refs[count][:, 0, :, lane : lane + block.shape[2]] = block

    give = pl.pallas_call(
        body,
        out_shape=jax.ShapeDtypeStruct((depth, 2, rows, lanes), BF),
        grid_spec=pltpu.PrefetchScalarGridSpec(
            num_scalar_prefetch=1,
            grid=(2,),
            in_specs=chosen(grads, False),
            out_specs=pl.BlockSpec((depth, 1, rows, lanes), lambda t, w: (0, t, 0, 0)),
        ),
        cost_estimate=cost(0, 8 * depth * rows * lanes),
        name="scatter_give",
    )(position(), *grads)
    return grads, rows, exchange(give, across_second), give


def scatter_near(state, *others):
    grads, rows, got, _ = state
    depth, count = grads[0].shape[0], len(grads)
    plan, lanes = lane_plan(grads, rows)

    def body(w, *refs):
        ins, got_ref, give_ref, keep_ref = refs[:count], refs[count], refs[count + 1], refs[count + 2]
        here = jnp.where(w[3] == 0, w[1], w[2])
        for n, row, lane in plan:
            block = ins[n][:, 0, 0, row : row + rows, :]
            span = slice(lane, lane + block.shape[2])
            value = block.astype(F32) + got_ref[:, 0, :, span].astype(F32)

            @pl.when(pl.program_id(0) == here)
            def _():
                keep_ref[:, :, span] = value

            @pl.when(pl.program_id(0) != here)
            def _():
                give_ref[:, :, span] = value.astype(BF)

    out = pl.BlockSpec((depth, rows, lanes), lambda t, w: (0, 0, 0))
    slab = pl.BlockSpec((depth, 1, rows, lanes), lambda t, w: (0, t, 0, 0))
    give, keep = pl.pallas_call(
        body,
        out_shape=[jax.ShapeDtypeStruct((depth, rows, lanes), t) for t in (BF, F32)],
        grid_spec=pltpu.PrefetchScalarGridSpec(
            num_scalar_prefetch=1,
            grid=(2,),
            in_specs=chosen(grads, True) + [slab],
            out_specs=[out, out],
        ),
        cost_estimate=cost(0, 14 * depth * rows * lanes),
        name="scatter_near",
    )(position(), *grads, after(got, *others))
    return keep, exchange(give, across_first)


def scatter_column(state, *others):
    keep, got = state
    depth, rows, lanes = keep.shape

    def body(w, keep_in, got_ref, keep_ref, give_ref):
        for j in range(depth):
            value = keep_in[w[0] ^ j] + got_ref[w[0] ^ j].astype(F32)
            if j < 2:
                keep_ref[j] = value
            else:
                give_ref[j - 2] = value.astype(BF)

    block = pl.BlockSpec((depth, rows, lanes), lambda t, w: (0, 0, 0))
    out = pl.BlockSpec((2, rows, lanes), lambda t, w: (0, 0, 0))
    keep, give = pl.pallas_call(
        body,
        out_shape=[jax.ShapeDtypeStruct((2, rows, lanes), t) for t in (F32, BF)],
        grid_spec=pltpu.PrefetchScalarGridSpec(
            num_scalar_prefetch=1, grid=(1,), in_specs=[block, block], out_specs=[out, out]
        ),
        cost_estimate=cost(0, 9 * depth * rows * lanes),
        name="scatter_column",
    )(position(), keep, after(got, *others))
    return keep, exchange(give, along_z(2))


def scatter_pair(state, *others):
    keep, got = state
    total = keep + after(got, *others).astype(F32)
    return total[0], exchange(total[1].astype(BF), along_z(1))


def scatter_end(state):
    return state[0] + state[1].astype(F32)


def own_rows(core, unit):
    halves = unit.reshape(2, unit.shape[0] // 2, unit.shape[1])
    return at(halves, core, 0), swap(at(halves, 1 - core, 0))


def first_done(unit, classes):
    core = lax.axis_index("seq") % 2
    shrink = jnp.concatenate([unit[:, :D], unit[:, D : 2 * D]], 0)
    mine, other = own_rows(core, unit[:, 2 * D :])
    return shrink, in_core_order(core, mine[None], other[None], 0)[:, :, :classes]


def second_done(unit, wide):
    core = lax.axis_index("seq") % 2
    chips = lax.axis_size("dp") * lax.axis_size("seq") // 2
    mine, other = own_rows(core, unit)
    return (
        join_halves(core, mine[:, :wide], other[:, :wide], chips),
        join_halves(core, mine[:, wide:], other[:, wide:], 1),
    )


def vector_blocks(vectors, like):
    chips = lax.axis_size("dp") * lax.axis_size("seq") // 2
    tall, thin = vectors.shape[0], vectors.shape[1] // chips
    vec = vectors.astype(BF).reshape(tall, chips, thin).transpose(1, 0, 2)
    vec = jnp.pad(vec, ((0, 0), (0, like.shape[3] - tall), (0, 128 - thin)))
    return vec.reshape(like.shape[:4] + (128,))


def last_done(attend, embedder):
    core = lax.axis_index("seq") % 2
    mine, other = own_rows(core, jnp.concatenate([embedder[:, :HALF], attend], 1))
    return (
        join_halves(core, mine[:, :HALF], other[:, :HALF], 1),
        join_halves(core, mine[:, HALF:], other[:, HALF:], 3),
    )


def scatter_plain(grads, classes):
    embedder, attend, merger, expand, shrink, readout, vectors = grads
    _, _, _, c = spot()
    chips = lax.axis_size("dp") * lax.axis_size("seq") // 2

    def reduced(value, axis):
        value = value.astype(F32)
        return lax.psum_scatter(value, AXES, scatter_dimension=axis, tiled=True)

    def spread(half, parts):
        return reduced(join_halves(c, half, jnp.zeros_like(half), parts), 0)

    tall = shrink.reshape(chips, 1, -1, D)
    tall = in_core_order(c, tall, jnp.zeros_like(tall), 1).reshape(-1, D)
    pair = in_core_order(c, readout[None], jnp.zeros_like(readout)[None], 0)
    return (
        spread(embedder, 1),
        spread(attend, 3),
        spread(merger, 1),
        spread(expand, chips),
        reduced(tall, 0),
        reduced(pair, 1)[:, :, :classes],
        reduced(vectors * 0.5, 1),
    )


def dot_keys(left, right):
    return lax.dot_general(left, right, (((1,), (1,)), ((), ())), preferred_element_type=F32)


def turned(value):
    return value.astype(F32).T.astype(BF)


def chunks_of(count):
    size = 256 if count % 256 == 0 else count
    return [slice(start, start + size) for start in range(0, count, size)]


def attend_forward(q_ref, k_ref, v_ref, qm_ref, km_ref, out_ref, exact_ref, lse_ref, keys, values, raws):
    lane = lax.broadcasted_iota(jnp.int32, (1, 2 * HD), 1) // HD
    chunks = chunks_of(k_ref.shape[0])

    @pl.when(pl.program_id(1) == 0)
    def _():
        for h in range(2):
            keys[h] = jnp.where(lane == h, k_ref[...], km_ref[...])
        values[...] = turned(v_ref[...])

    query = q_ref[...] * jnp.asarray(SCALE, BF)
    tops, parts = [], []
    for h in range(2):
        query_h = jnp.where(lane == h, query, qm_ref[...])
        top = None
        for chunk in chunks:
            raw = dot_keys(keys[h, chunk, :], query_h)
            raws[h, chunk, :] = raw
            high = jnp.max(raw, 0, keepdims=True)
            top = high if top is None else jnp.maximum(top, high)
        tops.append(top)
    for h in range(2):
        mass, part = 0.0, 0.0
        for chunk in chunks:
            heavy = jnp.exp(raws[h, chunk, :] - tops[h])
            mass = mass + jnp.sum(heavy, 0, keepdims=True)
            side = values[HD * h : HD * (h + 1), chunk]
            part = part + jnp.dot(side, heavy.astype(BF), preferred_element_type=F32)
        parts.append(part * (1.0 / mass))
        lse_ref[0, h : h + 1, :] = tops[h] + jnp.log(mass)
    mixed = jnp.concatenate(parts, 0).T
    exact_ref[...] = mixed
    out_ref[...] = mixed.astype(BF)


def attend_backward(joined, q_ref, k_ref, v_ref, do_ref, exact_ref, lse_ref, qm_ref, km_ref, *refs):
    outs, (keys, turned_keys, grad_keys, grad_values) = refs[:-4], refs[-4:]
    lane = lax.broadcasted_iota(jnp.int32, (1, 2 * HD), 1) // HD
    pair, step = pl.program_id(0), pl.program_id(1)

    @pl.when(step == 0)
    def _():
        for h in range(2):
            keys[h] = jnp.where(lane == h, k_ref[...], km_ref[...])
        turned_keys[...] = turned(k_ref[...])
        grad_keys[...] = jnp.zeros_like(grad_keys)
        grad_values[...] = jnp.zeros_like(grad_values)

    query = q_ref[...] * jnp.asarray(SCALE, BF)
    grad = do_ref[...]
    spreads = (grad.astype(F32) * exact_ref[...]).T
    of_head = []
    for h in range(2):
        zero = jnp.zeros_like(query)
        of_head.append(
            (
                jnp.where(lane == h, query, qm_ref[...]),
                jnp.where(lane == h, query, zero),
                jnp.where(lane == h, grad, zero),
                jnp.sum(spreads[HD * h : HD * (h + 1)], 0, keepdims=True),
                lse_ref[0, h : h + 1, :],
            )
        )
    parts = []
    for h, (query_m, query_h, grad_h, spread, lse) in enumerate(of_head):
        shares = jnp.exp(dot_keys(keys[h], query_m) - lse)
        grad_raw = (shares * (dot_keys(v_ref[...], grad_h) - spread)).astype(BF)
        side = turned_keys[HD * h : HD * (h + 1), :]
        parts.append(jnp.dot(side, grad_raw, preferred_element_type=F32))
        grad_keys[...] += jnp.dot(grad_raw, query_h, preferred_element_type=F32)
        grad_values[...] += jnp.dot(shares.astype(BF), grad_h, preferred_element_type=F32)
    grad_query = (jnp.concatenate(parts, 0).T * SCALE).astype(BF)
    if joined:
        rows = grad_query.shape[0]
        down = pl.ds(pl.multiple_of(step * rows, rows), rows)
        outs[0][down, pl.ds(pl.multiple_of(pair * 128, 128), 128)] = grad_query
    else:
        outs[0][...] = grad_query

    @pl.when(step == pl.num_programs(1) - 1)
    def _():
        if joined:
            across = pl.num_programs(0)
            for n, total in enumerate((grad_keys, grad_values)):
                place = (pair + across * (n + 1)) * 128
                outs[0][:, pl.ds(pl.multiple_of(place, 128), 128)] = total[...].astype(BF)
        else:
            outs[1][...] = grad_keys[...]
            outs[2][...] = grad_values[...]


def queries_of(count):
    return 512 if count % 512 == 0 else tile_of(count)


def tile_of(count):
    return 256 if count % 256 == 0 else count


def mix_tokens(projected, around, mask_q, mask_k):
    nq, nk = projected.shape[0], around.shape[0]
    tile = queries_of(nq)
    rows = lambda part: pl.BlockSpec((tile, 128), lambda i, j: (j, part * PAIRS + i))
    tall = lambda part: pl.BlockSpec((nk, 128), lambda i, j: (0, part * PAIRS + i))
    return pl.pallas_call(
        attend_forward,
        grid=(PAIRS, nq // tile),
        in_specs=[
            rows(0),
            tall(1),
            tall(2),
            pl.BlockSpec((tile, 128), lambda i, j: (j, 0)),
            pl.BlockSpec((nk, 128), lambda i, j: (0, 0)),
        ],
        out_specs=[rows(0), rows(0), pl.BlockSpec((1, 2, tile), lambda i, j: (i, 0, j))],
        out_shape=[
            jax.ShapeDtypeStruct((nq, HALF), BF),
            jax.ShapeDtypeStruct((nq, HALF), F32),
            jax.ShapeDtypeStruct((PAIRS, 2, nq), F32),
        ],
        scratch_shapes=[
            pltpu.VMEM((2, nk, 128), BF),
            pltpu.VMEM((128, nk), BF),
            pltpu.VMEM((2, nk, tile), F32),
        ],
        cost_estimate=cost(nq * nk * HALF, nq * HALF),
        name="attend_forward",
    )(projected, around, around, mask_q, mask_k)


def mix_back(projected, around, grad, exact, lse, mask_q, mask_k):
    nq, nk = projected.shape[0], around.shape[0]
    tile, joined = queries_of(nq), nq == nk
    rows = lambda part: pl.BlockSpec((tile, 128), lambda i, j: (j, part * PAIRS + i))
    tall = lambda part: pl.BlockSpec((nk, 128), lambda i, j: (0, part * PAIRS + i))
    if joined:
        out_specs = [pl.BlockSpec((nq, 3 * HALF), lambda i, j: (0, 0))]
        out_shape = [jax.ShapeDtypeStruct((nq, 3 * HALF), BF)]
    else:
        out_specs = [rows(0), tall(0), tall(0)]
        out_shape = [jax.ShapeDtypeStruct((nq, HALF), BF)]
        out_shape += [jax.ShapeDtypeStruct((nk, HALF), F32)] * 2
    return pl.pallas_call(
        partial(attend_backward, joined),
        grid=(PAIRS, nq // tile),
        in_specs=[
            rows(0),
            tall(1),
            tall(2),
            rows(0),
            rows(0),
            pl.BlockSpec((1, 2, tile), lambda i, j: (i, 0, j)),
            pl.BlockSpec((tile, 128), lambda i, j: (j, 0)),
            pl.BlockSpec((nk, 128), lambda i, j: (0, 0)),
        ],
        out_specs=out_specs,
        out_shape=out_shape,
        scratch_shapes=[
            pltpu.VMEM((2, nk, 128), BF),
            pltpu.VMEM((128, nk), BF),
            pltpu.VMEM((nk, 128), F32),
            pltpu.VMEM((nk, 128), F32),
        ],
        cost_estimate=cost(nq * nk * HALF, nq * HALF),
        name="attend_backward",
    )(projected, around, around, grad, exact, lse, mask_q, mask_k)


def norm_parts(x):
    centre = x - jnp.mean(x, -1, keepdims=True)
    rate = lax.rsqrt(jnp.mean(centre * centre, -1, keepdims=True) + NORM_EPS)
    return (centre * rate, rate)


def layer_norm(x, gain, shift):
    return norm_parts(x)[0] * gain + shift


def norm_back(x, gain, grad):
    unit, rate = norm_parts(x)
    inner_grad = grad * gain
    back = rate * (
        inner_grad
        - jnp.mean(inner_grad, -1, keepdims=True)
        - unit * jnp.mean(inner_grad * unit, -1, keepdims=True)
    )
    return (back, jnp.sum(grad * unit, 0), jnp.sum(grad, 0))


def norm_back_body(x_ref, gain_ref, mine_ref, got_ref, more_ref, kind_ref, out_ref, low_ref, sum_ref):
    grad = mine_ref[...] + got_ref[...]
    back, _, _ = norm_back(x_ref[...], gain_ref[...], grad)
    unit, _ = norm_parts(x_ref[...])
    total = more_ref[...] + back
    out_ref[...] = total
    low_ref[...] = (total * kind_ref[:, :1]).astype(BF)

    @pl.when(pl.program_id(0) == 0)
    def _():
        sum_ref[...] = jnp.zeros_like(sum_ref)

    rows = (grad * unit, grad, total * kind_ref[:, 1:2], total * kind_ref[:, 2:3])
    for n, row in enumerate(rows):
        sum_ref[n : n + 1, :] += jnp.sum(row, 0, keepdims=True)


def norm_back_sum(x, gain, mine, got, more, kinds):
    count = x.shape[0]
    tile = tile_of(count)
    rows = pl.BlockSpec((tile, D), lambda i: (i, 0))
    return pl.pallas_call(
        norm_back_body,
        grid=(count // tile,),
        in_specs=[rows, pl.BlockSpec((1, D), lambda i: (0, 0)), rows, rows, rows]
        + [pl.BlockSpec((tile, 128), lambda i: (i, 0))],
        out_specs=[rows, rows, pl.BlockSpec((8, D), lambda i: (0, 0))],
        out_shape=[
            jax.ShapeDtypeStruct((count, D), F32),
            jax.ShapeDtypeStruct((count, D), BF),
            jax.ShapeDtypeStruct((8, D), F32),
        ],
        cost_estimate=cost(0, count * D),
        name="norm_back",
    )(x, gain[None, :], mine, got, more, kinds)


def matmul(left, right):
    return jnp.dot(left, right, preferred_element_type=F32)


def outer(left, right):
    return lax.dot_general(left, right, (((0,), (0,)), ((), ())), preferred_element_type=F32)


def inner(grad, weight):
    return lax.dot_general(grad, weight, (((1,), (1,)), ((), ())), preferred_element_type=F32)


def chip_bits():
    return [2 << b for b in range((lax.axis_size("seq") // 4 - 1).bit_length())]


def of_bit(value, bit):
    return exchange(value, lambda d, s: (d, s ^ bit))


def row_tokens(value):
    for bit in chip_bits():
        value = jnp.concatenate([value, of_bit(value, bit)], 0)
    return value


def row_return(value):
    for bit in reversed(chip_bits()):
        half = value.shape[0] // 2
        value = value[:half] + of_bit(value[half:].astype(BF), bit).astype(F32)
    return value


def row_sum(value):
    for bit in chip_bits():
        value = value + of_bit(value, bit)
    return value


def segment_lanes(segment, of_query):
    lane = jnp.arange(128, dtype=jnp.int32) % HD
    hit = segment[:, None] == lane[None, :]
    if of_query:
        return jnp.where(hit | (lane > IMGS)[None, :], 0.0, MASKED).astype(BF)
    return hit.astype(BF)


def adamw(weight, mean, square, grad, scale, decay):
    mean_next = BETA_ONE * mean + (1.0 - BETA_ONE) * grad
    square_next = BETA_TWO * square + (1.0 - BETA_TWO) * grad * grad
    mean_hat = mean_next / (1.0 - BETA_ONE**STEP_COUNT)
    square_hat = square_next / (1.0 - BETA_TWO**STEP_COUNT)
    weight_next = weight - BASE_RATE * scale * (
        mean_hat / (jnp.sqrt(square_hat) + ADAM_EPS) + decay * weight
    )
    return (weight_next, mean_next, square_next)


def moments(mean, square, grad):
    return (
        BETA_ONE * mean + (1.0 - BETA_ONE) * grad,
        BETA_TWO * square + (1.0 - BETA_TWO) * grad * grad,
    )


def on_device(
    pixels,
    lengths,
    labels,
    teacher,
    embedder,
    embedder_mean,
    embedder_square,
    attend,
    attend_mean,
    attend_square,
    merger,
    merger_mean,
    merger_square,
    expand,
    expand_mean,
    expand_square,
    shrink,
    shrink_mean,
    shrink_square,
    readout,
    readout_mean,
    readout_square,
    vectors,
    vectors_mean,
    vectors_square,
):
    seq_size, dp_size = lax.axis_size("seq"), lax.axis_size("dp")
    fast = seq_size == 4 and dp_size == 8 and embedder.shape[0] == 24
    seq, core = lax.axis_index("seq"), lax.axis_index("seq") % 2
    local, far = pixels.shape[1], seq_size // 2
    span = seq_size // 4
    classes = readout.shape[2]
    image_count = lengths.shape[0] * dp_size * IMGS

    gather = gather_weights if fast else gather_plain
    embed_w, attend_w, merger_half, expand_w, vector_w, first, cover, later_weights = gather(
        embedder, attend, merger, expand, shrink, readout, vectors
    )

    side = seq // far
    pixels = after(pixels, first)
    pixels_got = of_bit(at(pixels, 1 - side, 0), far)
    tokens = jnp.concatenate([at(pixels, side, 0), pixels_got], 0)
    all_pixels = both_tokens(tokens)
    row_lengths = at(lengths, side, 0)
    row_labels = at(labels, side, 0)
    row_teacher = at(teacher, side, 0)

    def places_of(where):
        step = jnp.arange(local, dtype=jnp.int32)
        return jnp.concatenate([where * local + step, (where ^ far) * local + step])

    places = places_of(seq)
    ends = jnp.cumsum(row_lengths)
    starts = ends - row_lengths

    def segment_of(spots):
        return jnp.sum((spots[:, None] >= ends[None, :]).astype(jnp.int32), 1)

    seg_q = segment_of(jnp.concatenate([places, places_of(seq ^ 1)]))
    order = [0]
    for bit in chip_bits():
        order = order + [o ^ bit for o in order]
    seg_k = segment_of(jnp.concatenate([places_of(seq ^ o ^ k) for o in order for k in range(2)]))
    mask_q, mask_k = segment_lanes(seg_q, True), segment_lanes(seg_k, False)
    marks = jnp.concatenate([starts, starts + 1])
    hits = (marks[:, None] == places[None, :]).astype(F32)
    token_hits = (places[:, None] == marks[None, :]).astype(F32)
    is_cls, is_dist = jnp.sum(hits[:IMGS], 0), jnp.sum(hits[IMGS:], 0)
    is_patch = (seg_q[: 2 * local] < IMGS).astype(F32) - is_cls - is_dist

    merger_w = in_core_order(core, merger_half, swap(merger_half), 1)
    vector_f = vector_w.astype(F32)

    patches = to_tokens(core, matmul(all_pixels, embed_w))
    x = (
        is_patch[:, None] * patches
        + is_cls[:, None] * vector_f[4 * L + 2]
        + is_dist[:, None] * vector_f[4 * L + 3]
    )
    a = both_tokens(layer_norm(x, vector_f[0], vector_f[1]).astype(BF))
    projected = matmul(a, attend_w).astype(BF)
    around = row_tokens(projected)
    mixed_half, exact, lse = mix_tokens(projected, around, mask_q, mask_k)
    mixed_half = after(mixed_half, *cover)
    shrink_w, readout_w, near = later_weights(mixed_half)
    other = swap(mixed_half)
    count = 2 * local
    other = jnp.concatenate([other[count:], other[:count]], 0)
    mixed = in_core_order(core, mixed_half, other, 1)
    x_mid = x + matmul(mixed[:count], merger_w)
    normed = both_tokens(layer_norm(x_mid, vector_f[2], vector_f[3]).astype(BF))
    hidden_in = matmul(after(normed, near), expand_w)
    cdf = 0.5 * (1.0 + lax.erf(hidden_in * (0.5**0.5)))
    hidden = (hidden_in * cdf).astype(BF)
    slope = cdf + hidden_in * jnp.exp(-0.5 * hidden_in * hidden_in) * ((0.5 / jnp.pi) ** 0.5)
    mine, got = with_other(matmul(hidden, shrink_w))
    x_last = x_mid + (mine[:count] + got)

    label_hot = (row_labels[:, None] == jnp.arange(classes, dtype=jnp.int32)).astype(F32)
    teach_log = jax.nn.log_softmax(row_teacher, -1)
    target = jnp.where(core == 0, label_hot, jnp.exp(teach_log))
    target_log = jnp.where(core == 0, 0.0, teach_log)
    gain, shift = vector_f[4 * L], vector_f[4 * L + 1]
    rows = row_sum(jnp.dot(hits, x_last, precision=HIGH)).reshape(2, IMGS, D)
    rows = at(rows, core, 0) + swap(at(rows, 1 - core, 0))
    unit, rate = norm_parts(rows)
    head_in = (unit * gain + shift).astype(BF)
    logits = matmul(head_in, readout_w)[:, :classes]
    log_share = jax.nn.log_softmax(logits, -1)
    loss_local = jnp.sum(0.5 * target * (target_log - log_share)) / span
    grad_logits = pad_lanes(
        0.5 * (jnp.exp(log_share) - target) / image_count, readout_w.shape[1]
    )
    grad_readout = lax.dot_general(
        head_in.astype(F32), grad_logits / span, (((0,), (0,)), ((), ())), precision=HIGH
    )
    grad_head = lax.dot_general(
        grad_logits, readout_w.astype(F32), (((1,), (1,)), ((), ())), precision=HIGH
    )
    head_back, gain_out, shift_out = norm_back(rows, gain, grad_head)
    back = in_core_order(core, head_back, swap(head_back), 0)

    grad_out = jnp.dot(token_hits, back, precision=HIGH)
    grad_branch = both_tokens(grad_out.astype(BF))
    grad_shrink = outer(hidden, grad_branch).astype(BF)
    grad_readout = grad_readout.astype(BF)
    if fast:
        parts = [blocks(grad_shrink), blocks(grad_readout)]
        unit_rows = parts[1].shape[3]
        first = scatter_give(parts, unit_rows)
    grad_pre = (inner(grad_branch, shrink_w) * slope).astype(BF)
    grad_expand = outer(normed, grad_pre).astype(BF)
    mine, got = with_other(inner(grad_pre, expand_w))
    kinds = jnp.stack([is_patch, is_cls, is_dist], 1)
    kinds = jnp.pad(kinds, ((0, 0), (0, 125)))
    every = jnp.ones_like(kinds)
    grad_mid, low_mid, sums_two = norm_back_sum(x_mid, vector_f[2], mine, got, grad_out, every)
    grad_attn = both_tokens(low_mid)
    attn_half = at(grad_attn.reshape(-1, 2, HALF), core, 1)
    grad_merger = outer(mixed, attn_half).astype(BF)
    if fast:
        second = scatter_give([blocks(grad_expand), blocks(grad_merger)], unit_rows)
    grad_mixed = inner(grad_attn, at(merger_w.reshape(2, HALF, D), core, 0)).astype(BF)
    if fast:
        first = scatter_near(first, second[3])
        grad_mixed = after(grad_mixed, first[0])
    grads = mix_back(projected, around, grad_mixed, exact, lse, mask_q, mask_k)
    if len(grads) == 1:
        grad_proj = grads[0]
    else:
        grad_proj = jnp.concatenate([grads[0]] + [row_return(g).astype(BF) for g in grads[1:]], 1)
    if fast:
        grad_proj = after(grad_proj, first[1], second[2])
    mine, got = with_other(inner(grad_proj, attend_w))
    grad_attend = outer(a, grad_proj).astype(BF)
    if fast:
        third = scatter_give([blocks(grad_attend)], unit_rows)
        first = scatter_column(first, third[3])
        second = scatter_near(second, first[0])
    _, grad_patch, sums_one = norm_back_sum(x, vector_f[0], mine, got, grad_mid, kinds)
    grad_embed = outer(all_pixels, to_columns(core, grad_patch)).astype(BF)
    grad_vectors = jnp.concatenate(
        [sums_one[:2], sums_two[:2], jnp.stack([gain_out, shift_out]) / span, sums_one[2:4]], 0
    )
    grad_vectors = grad_vectors + swap(grad_vectors)
    if fast:
        parts = [blocks(grad_embed)]
        fourth = scatter_give(parts + [vector_blocks(grad_vectors, parts[0])], unit_rows)
        third = scatter_near(third, grad_embed)
        second = scatter_column(second, grad_embed)
        fourth = scatter_near(fourth)
        first = scatter_pair(first, fourth[0])
        third = scatter_column(third)
        fourth = scatter_column(fourth)
        second = scatter_pair(second, fourth[0])
        third, fourth = scatter_pair(third), scatter_pair(fourth)
        units = [scatter_end(state) for state in (first, second, third, fourth)]
        tall, thin = vectors.shape
        sum_vectors = at(units[3][:tall, HALF : HALF + 2 * thin].reshape(tall, 2, thin), core, 1)
        squares_of = units[:3] + [units[3][:, :HALF], sum_vectors]
        sum_shrink, sum_readout = first_done(units[0], classes)
        sum_expand, sum_merger = second_done(units[1], grad_expand.shape[1])
        sum_embed, sum_attend = last_done(units[2], units[3])
    else:
        sum_embed, sum_attend, sum_merger, sum_expand, sum_shrink, sum_readout, sum_vectors = (
            scatter_plain(
                (grad_embed, grad_attend, grad_merger, grad_expand)
                + (grad_shrink, grad_readout, grad_vectors),
                classes,
            )
        )
        squares_of = [sum_embed, sum_attend, sum_merger, sum_expand, sum_shrink, sum_readout]
        squares_of.append(sum_vectors)
    reduced = (sum_embed, sum_attend, sum_merger, sum_expand, sum_shrink, sum_readout)
    square_sum = sum((jnp.sum(g * g) for g in squares_of))
    beside = [(sum_shrink, sum_readout), (sum_expand,), (sum_merger, sum_embed), (sum_attend,)]
    both = total_of(jnp.stack([square_sum, loss_local])[None, :], beside)
    grad_norm = jnp.sqrt(both[0, 0])
    factor = jnp.minimum(1.0, CLIP_AT / (grad_norm + 1e-06))

    masters = (embedder, attend, merger, expand, shrink, readout)
    means = (embedder_mean, attend_mean, merger_mean, expand_mean, shrink_mean, readout_mean)
    squares = (
        embedder_square,
        attend_square,
        merger_square,
        expand_square,
        shrink_square,
        readout_square,
    )
    outs = []
    for j in range(6):
        grad = reduced[j].reshape(masters[j].shape) * factor
        outs += adamw(masters[j], means[j], squares[j], grad, RATES[j], DECAY)
    outs += moments(vectors_mean, vectors_square, sum_vectors * factor)
    return tuple(outs) + (both[0, 1] / image_count, grad_norm)


def solution(mesh):
    return jax.shard_map(
        on_device,
        mesh=mesh,
        in_specs=(
            P("dp", "seq", None),
            P("dp", None),
            P("dp", None),
            P("dp", None, None),
            P(("dp", "seq"), None),
            P(("dp", "seq"), None),
            P(("dp", "seq"), None),
            P(None, ("dp", "seq"), None),
            P(None, ("dp", "seq"), None),
            P(None, ("dp", "seq"), None),
            P(None, ("dp", "seq"), None),
            P(None, ("dp", "seq"), None),
            P(None, ("dp", "seq"), None),
            P(None, ("dp", "seq"), None),
            P(None, ("dp", "seq"), None),
            P(None, ("dp", "seq"), None),
            P(None, ("dp", "seq"), None),
            P(None, ("dp", "seq"), None),
            P(None, ("dp", "seq"), None),
            P(None, ("dp", "seq"), None),
            P(None, ("dp", "seq"), None),
            P(None, ("dp", "seq"), None),
            P(None, ("dp", "seq")),
            P(None, ("dp", "seq")),
            P(None, ("dp", "seq")),
        ),
        out_specs=(
            P(("dp", "seq"), None),
            P(("dp", "seq"), None),
            P(("dp", "seq"), None),
            P(None, ("dp", "seq"), None),
            P(None, ("dp", "seq"), None),
            P(None, ("dp", "seq"), None),
            P(None, ("dp", "seq"), None),
            P(None, ("dp", "seq"), None),
            P(None, ("dp", "seq"), None),
            P(None, ("dp", "seq"), None),
            P(None, ("dp", "seq"), None),
            P(None, ("dp", "seq"), None),
            P(None, ("dp", "seq"), None),
            P(None, ("dp", "seq"), None),
            P(None, ("dp", "seq"), None),
            P(None, ("dp", "seq"), None),
            P(None, ("dp", "seq"), None),
            P(None, ("dp", "seq"), None),
            P(None, ("dp", "seq")),
            P(None, ("dp", "seq")),
            P(),
            P(),
        ),
        check_vma=False,
    )
```

```python
from functools import partial

import jax
import jax.numpy as jnp
from jax import lax
from jax.experimental import pallas as pl
from jax.experimental.pallas import tpu as pltpu
from jax.sharding import PartitionSpec as P

HEADS = 12
HD = 64
L = 1
IMGS = 3
STEP_COUNT = 7

NORM_EPS = 1e-06
MASKED = -1000000000.0
SCALE = 0.125
BETA_ONE = 0.9
BETA_TWO = 0.999
ADAM_EPS = 1e-08
DECAY = 0.05
BASE_RATE = 0.05
LAYER_RATE = 0.75
CLIP_AT = 0.05
HIGH = lax.Precision.HIGHEST
BF = jnp.bfloat16
F32 = jnp.float32
AXES = ("dp", "seq")
D = 768
HALF = 384
PAIRS = HEADS // 4
RATES = (LAYER_RATE ** (L + 1), LAYER_RATE, LAYER_RATE, LAYER_RATE, LAYER_RATE, 1.0)


def pairs(move):
    dp_size, seq_size = lax.axis_size("dp"), lax.axis_size("seq")
    return [
        (d * seq_size + s, move(d, s)[0] * seq_size + move(d, s)[1])
        for d in range(dp_size)
        for s in range(seq_size)
    ]


def exchange(value, move):
    return lax.ppermute(value, AXES, pairs(move))


def along_z(step):
    return lambda d, s: (d ^ (2 * step), s)


def across_core(d, s):
    return (d, s ^ 1)


def across_first(d, s):
    return (d ^ 1, s) if s % 2 == 0 else (d, s ^ 2)


def across_second(d, s):
    return (d, s ^ 2) if s % 2 == 0 else (d ^ 1, s)


def swap(value):
    return exchange(value, across_core)


def spot():
    dp, seq = lax.axis_index("dp"), lax.axis_index("seq")
    return (dp // 2, dp % 2, seq // 2, seq % 2)


def total_of(value, beside=()):
    hops = [(0, 1 << b) for b in range((lax.axis_size("seq") - 1).bit_length())]
    hops += [(1 << b, 0) for b in range((lax.axis_size("dp") - 1).bit_length())]
    for n, (of_dp, of_seq) in enumerate(hops):
        got = exchange(value, lambda d, s: (d ^ of_dp, s ^ of_seq))
        value = value + after(got, *beside[n : n + 1])
    return value


def after(value, *others):
    return lax.optimization_barrier((value,) + others)[0]


def at(value, index, axis):
    return lax.dynamic_index_in_dim(value, index, axis, keepdims=False)


def in_core_order(core, mine, other, axis):
    return jnp.where(
        core == 0,
        jnp.concatenate([mine, other], axis),
        jnp.concatenate([other, mine], axis),
    )


def both_tokens(value):
    return jnp.concatenate([value, swap(value)], 0)


def to_columns(core, value):
    halves = value.reshape(value.shape[0], 2, HALF)
    return jnp.concatenate([at(halves, core, 1), swap(at(halves, 1 - core, 1))], 0)


def to_tokens(core, value):
    count = value.shape[0] // 2
    return in_core_order(core, value[:count], swap(value[count:]), 1)


def with_other(product):
    return product, swap(product[product.shape[0] // 2 :])


def cost(flops, byte_count):
    return pl.CostEstimate(flops=int(flops), bytes_accessed=int(byte_count), transcendentals=0)


def half_of(shard, parts, which):
    rows, wide = shard.shape
    return at(shard.reshape(rows, parts, 2, wide // parts // 2), which, 2).reshape(rows, -1)


def join_halves(core, mine, other, parts):
    rows = mine.shape[0]
    shape = (rows, parts, 1, mine.shape[1] // parts)
    return in_core_order(core, mine.reshape(shape), other.reshape(shape), 2).reshape(rows, -1)


def pad_lanes(value, width):
    return jnp.pad(value, ((0, 0), (0, width - value.shape[1])))


def assemble(pieces, places, z, plan, shapes):
    count = len(pieces)

    def body(where, *refs):
        ins, outs = refs[:count], refs[count:]
        for i in range(count):
            x, y = where[2 * i + 1], where[2 * i + 2]
            rows = ins[i].shape[1]
            for j in range(2):
                for o, row, lane in plan:
                    outs[o][(where[0] % 2) ^ j, x, y, row : row + rows, :] = ins[i][
                        j, :, lane : lane + outs[o].shape[-1]
                    ]

    def out_spec(shape):
        return pl.BlockSpec((2,) + shape[1:], lambda j, where: ((where[0] // 2) ^ j, 0, 0, 0, 0))

    slab = (2,) + pieces[0].shape[1:]
    size = 4 * pieces[0].size
    return pl.pallas_call(
        body,
        out_shape=[jax.ShapeDtypeStruct(s, BF) for s in shapes],
        grid_spec=pltpu.PrefetchScalarGridSpec(
            num_scalar_prefetch=1,
            grid=(pieces[0].shape[0] // 2,),
            in_specs=[pl.BlockSpec(slab, lambda j, where: (j, 0, 0))] * count,
            out_specs=[out_spec(s) for s in shapes],
        ),
        cost_estimate=cost(0, 4 * size),
        name="assemble",
    )(jnp.concatenate([jnp.stack([z]), places]).astype(jnp.int32), *pieces)


def gather_planes(units, plans):
    z, x, y, c = spot()
    places = jnp.stack([x, y, x ^ (1 - c), y ^ c, x ^ c, y ^ (1 - c), x ^ 1, y ^ 1])
    others = [exchange(units[0], along_z(1))]
    others += [exchange(after(u, others[0]), along_z(1)) for u in units[1:]]
    columns = [jnp.stack([u, o]) for u, o in zip(units, others)]

    def finish(n, own, near, *waits):
        side = exchange(own, across_second)
        far = exchange(after(near, *waits), across_second)
        plan, widths = plans[n]
        shapes = [(own.shape[0], 2, 2) + w for w in widths]
        return assemble([own, near, side, far], places, z, plan, shapes)

    owns, nears, last = [], [], ()
    for n in range(2):
        other = exchange(after(columns[n], *last), along_z(2))
        owns.append(jnp.concatenate([columns[n], after(other, *others)], 0))
        nears.append(exchange(owns[n], across_first))
        last = (owns[n],)
    weights = finish(0, owns[0], nears[0], owns[1]) + finish(1, owns[1], nears[1])
    third = exchange(after(columns[2], *last), along_z(2))

    def later(value):
        own = jnp.concatenate([columns[2], after(third, value)], 0)
        near = exchange(own, across_first)
        return finish(2, own, near), near

    return weights, others[0], (nears[1], third), later


def gather_weights(embedder, attend, merger, expand, shrink, readout, vectors):
    _, _, _, c = spot()
    low = [w.astype(BF) for w in (embedder, attend[0], merger[0], expand[0], shrink[0], readout)]
    embedder, attend, merger, expand, shrink, readout = low
    vectors = vectors.astype(BF)
    rows, chips = embedder.shape[0], lax.axis_size("dp") * lax.axis_size("seq") // 2
    tall, thin = vectors.shape
    wide = -(-readout.shape[2] // 128) * 128

    def chip_rows(mine, other):
        return in_core_order(c, mine, other, 0)

    def of_core(k):
        vec = jnp.pad(vectors, ((0, rows - tall), (0, 128 - thin)))
        first = [half_of(embedder, 1, k), vec, half_of(attend, 3, k)]
        second = [half_of(merger, 1, k), half_of(expand, chips, k), pad_lanes(at(readout, k, 0), wide)]
        return jnp.concatenate(first, 1), jnp.concatenate(second, 1)

    mine, give = of_core(c), of_core(1 - c)
    got = swap(give[0])
    front = chip_rows(mine[0], got)
    vec = in_core_order(c, vectors, got[:tall, HALF : HALF + thin], 1)
    vec = jnp.pad(vec, ((0, 2 * rows - tall), (0, 128 - 2 * thin)))
    back = chip_rows(mine[1], swap(give[1]))
    tall_shrink = shrink.shape[0]
    shrink = jnp.concatenate([shrink[: 2 * rows], shrink[2 * rows :]], 1)

    tall_rows = 2 * rows
    units = [
        jnp.concatenate([front[:, :HALF], vec, front[:, HALF + 128 :]], 1),
        back[:, : 5 * HALF],
        jnp.concatenate([shrink, back[:, 5 * HALF :]], 1),
    ]
    plans = [
        (
            [(0, 0, 0), (1, 0, HALF), (2, 0, HALF + 128)],
            [(tall_rows, HALF), (tall_rows, 128), (tall_rows, 3 * HALF)],
        ),
        ([(0, 0, 0), (1, 0, HALF)], [(tall_rows, HALF), (tall_rows, 4 * HALF)]),
        ([(0, 0, 0), (0, tall_rows, D), (1, 0, 2 * D)], [(tall_shrink, D), (tall_rows, wide)]),
    ]
    (emb, vec, att, mer, exp), first, cover, later = gather_planes(units, plans)

    def later_weights(value):
        (shr, rea), near = later(value)
        return shr.reshape(-1, D), rea.reshape(-1, wide), near

    vec = vec.reshape(chips, tall_rows, 128)[:, :tall, : 2 * thin].transpose(1, 0, 2)
    return (
        emb.reshape(-1, HALF),
        att.reshape(-1, 3 * HALF),
        mer.reshape(-1, HALF),
        exp.reshape(-1, 4 * HALF),
        vec.reshape(tall, -1),
        first,
        cover,
        later_weights,
    )


def gather_plain(embedder, attend, merger, expand, shrink, readout, vectors):
    _, _, _, c = spot()
    chips = lax.axis_size("dp") * lax.axis_size("seq") // 2
    wide = -(-readout.shape[2] // 128) * 128

    def whole_of(shard, axis):
        return lax.all_gather(shard.astype(BF), AXES, axis=axis, tiled=True)

    shrink = whole_of(shrink[0], 0).reshape(chips, 2, -1, D)
    return (
        half_of(whole_of(embedder, 0), 1, c),
        half_of(whole_of(attend[0], 0), 3, c),
        half_of(whole_of(merger[0], 0), 1, c),
        half_of(whole_of(expand[0], 0), chips, c),
        whole_of(vectors, 1),
        c,
        (c,),
        lambda value: (
            at(shrink, c, 1).reshape(-1, D),
            pad_lanes(at(whole_of(readout, 1), c, 0), wide),
            c,
        ),
    )


def blocks(grad):
    chips = lax.axis_size("dp") * lax.axis_size("seq") // 2
    return grad.reshape(chips // 4, 2, 2, grad.shape[0] // chips, grad.shape[1])


def lane_plan(grads, rows):
    plan, lane = [], 0
    for n, g in enumerate(grads):
        for row in range(0, g.shape[3], rows):
            plan.append((n, row, lane))
            lane += g.shape[4]
    return plan, lane


def position():
    return jnp.stack(spot()).astype(jnp.int32)


def chosen(grads, keep):
    def spec(g):
        def index(t, w):
            px = jnp.where(w[3] == 0, t, w[1] if keep else 1 - w[1])
            py = jnp.where(w[3] == 0, w[2] if keep else 1 - w[2], t)
            return (0, px, py, 0, 0)

        return pl.BlockSpec((g.shape[0], 1, 1) + g.shape[3:], index)

    return [spec(g) for g in grads]


def scatter_give(grads, rows):
    depth, count = grads[0].shape[0], len(grads)
    plan, lanes = lane_plan(grads, rows)

    def body(w, *refs):
        for n, row, lane in plan:
            block = refs[n][:, 0, 0, row : row + rows, :]
            refs[count][:, 0, :, lane : lane + block.shape[2]] = block

    give = pl.pallas_call(
        body,
        out_shape=jax.ShapeDtypeStruct((depth, 2, rows, lanes), BF),
        grid_spec=pltpu.PrefetchScalarGridSpec(
            num_scalar_prefetch=1,
            grid=(2,),
            in_specs=chosen(grads, False),
            out_specs=pl.BlockSpec((depth, 1, rows, lanes), lambda t, w: (0, t, 0, 0)),
        ),
        cost_estimate=cost(0, 8 * depth * rows * lanes),
        name="scatter_give",
    )(position(), *grads)
    return grads, rows, exchange(give, across_second), give


def scatter_near(state, *others):
    grads, rows, got, _ = state
    depth, count = grads[0].shape[0], len(grads)
    plan, lanes = lane_plan(grads, rows)

    def body(w, *refs):
        ins, got_ref, give_ref, keep_ref = refs[:count], refs[count], refs[count + 1], refs[count + 2]
        here = jnp.where(w[3] == 0, w[1], w[2])
        for n, row, lane in plan:
            block = ins[n][:, 0, 0, row : row + rows, :]
            span = slice(lane, lane + block.shape[2])
            value = block.astype(F32) + got_ref[:, 0, :, span].astype(F32)

            @pl.when(pl.program_id(0) == here)
            def _():
                keep_ref[:, :, span] = value

            @pl.when(pl.program_id(0) != here)
            def _():
                give_ref[:, :, span] = value.astype(BF)

    out = pl.BlockSpec((depth, rows, lanes), lambda t, w: (0, 0, 0))
    slab = pl.BlockSpec((depth, 1, rows, lanes), lambda t, w: (0, t, 0, 0))
    give, keep = pl.pallas_call(
        body,
        out_shape=[jax.ShapeDtypeStruct((depth, rows, lanes), t) for t in (BF, F32)],
        grid_spec=pltpu.PrefetchScalarGridSpec(
            num_scalar_prefetch=1,
            grid=(2,),
            in_specs=chosen(grads, True) + [slab],
            out_specs=[out, out],
        ),
        cost_estimate=cost(0, 14 * depth * rows * lanes),
        name="scatter_near",
    )(position(), *grads, after(got, *others))
    return keep, exchange(give, across_first)


def scatter_column(state, *others):
    keep, got = state
    depth, rows, lanes = keep.shape

    def body(w, keep_in, got_ref, keep_ref, give_ref):
        for j in range(depth):
            value = keep_in[w[0] ^ j] + got_ref[w[0] ^ j].astype(F32)
            if j < 2:
                keep_ref[j] = value
            else:
                give_ref[j - 2] = value.astype(BF)

    block = pl.BlockSpec((depth, rows, lanes), lambda t, w: (0, 0, 0))
    out = pl.BlockSpec((2, rows, lanes), lambda t, w: (0, 0, 0))
    keep, give = pl.pallas_call(
        body,
        out_shape=[jax.ShapeDtypeStruct((2, rows, lanes), t) for t in (F32, BF)],
        grid_spec=pltpu.PrefetchScalarGridSpec(
            num_scalar_prefetch=1, grid=(1,), in_specs=[block, block], out_specs=[out, out]
        ),
        cost_estimate=cost(0, 9 * depth * rows * lanes),
        name="scatter_column",
    )(position(), keep, after(got, *others))
    return keep, exchange(give, along_z(2))


def scatter_pair(state, *others):
    keep, got = state
    total = keep + after(got, *others).astype(F32)
    return total[0], exchange(total[1].astype(BF), along_z(1))


def scatter_end(state):
    return state[0] + state[1].astype(F32)


def own_rows(core, unit):
    halves = unit.reshape(2, unit.shape[0] // 2, unit.shape[1])
    return at(halves, core, 0), swap(at(halves, 1 - core, 0))


def first_done(unit, classes):
    core = lax.axis_index("seq") % 2
    shrink = jnp.concatenate([unit[:, :D], unit[:, D : 2 * D]], 0)
    mine, other = own_rows(core, unit[:, 2 * D :])
    return shrink, in_core_order(core, mine[None], other[None], 0)[:, :, :classes]


def second_done(unit, wide):
    core = lax.axis_index("seq") % 2
    chips = lax.axis_size("dp") * lax.axis_size("seq") // 2
    mine, other = own_rows(core, unit)
    return (
        join_halves(core, mine[:, :wide], other[:, :wide], chips),
        join_halves(core, mine[:, wide:], other[:, wide:], 1),
    )


def vector_blocks(vectors, like):
    chips = lax.axis_size("dp") * lax.axis_size("seq") // 2
    tall, thin = vectors.shape[0], vectors.shape[1] // chips
    vec = vectors.astype(BF).reshape(tall, chips, thin).transpose(1, 0, 2)
    vec = jnp.pad(vec, ((0, 0), (0, like.shape[3] - tall), (0, 128 - thin)))
    return vec.reshape(like.shape[:4] + (128,))


def last_done(attend, embedder):
    core = lax.axis_index("seq") % 2
    mine, other = own_rows(core, jnp.concatenate([embedder[:, :HALF], attend], 1))
    return (
        join_halves(core, mine[:, :HALF], other[:, :HALF], 1),
        join_halves(core, mine[:, HALF:], other[:, HALF:], 3),
    )


def scatter_plain(grads, classes):
    embedder, attend, merger, expand, shrink, readout, vectors = grads
    _, _, _, c = spot()
    chips = lax.axis_size("dp") * lax.axis_size("seq") // 2

    def reduced(value, axis):
        value = value.astype(F32)
        return lax.psum_scatter(value, AXES, scatter_dimension=axis, tiled=True)

    def spread(half, parts):
        return reduced(join_halves(c, half, jnp.zeros_like(half), parts), 0)

    tall = shrink.reshape(chips, 1, -1, D)
    tall = in_core_order(c, tall, jnp.zeros_like(tall), 1).reshape(-1, D)
    pair = in_core_order(c, readout[None], jnp.zeros_like(readout)[None], 0)
    return (
        spread(embedder, 1),
        spread(attend, 3),
        spread(merger, 1),
        spread(expand, chips),
        reduced(tall, 0),
        reduced(pair, 1)[:, :, :classes],
        reduced(vectors * 0.5, 1),
    )


def dot_keys(left, right):
    return lax.dot_general(left, right, (((1,), (1,)), ((), ())), preferred_element_type=F32)


def turned(value):
    return value.astype(F32).T.astype(BF)


def chunks_of(count):
    size = 256 if count % 256 == 0 else count
    return [slice(start, start + size) for start in range(0, count, size)]


def attend_forward(q_ref, k_ref, v_ref, qm_ref, km_ref, out_ref, exact_ref, lse_ref, keys, values, raws):
    lane = lax.broadcasted_iota(jnp.int32, (1, 2 * HD), 1) // HD
    chunks = chunks_of(k_ref.shape[0])

    @pl.when(pl.program_id(1) == 0)
    def _():
        for h in range(2):
            keys[h] = jnp.where(lane == h, k_ref[...], km_ref[...])
        values[...] = turned(v_ref[...])

    query = q_ref[...] * jnp.asarray(SCALE, BF)
    tops, parts = [], []
    for h in range(2):
        query_h = jnp.where(lane == h, query, qm_ref[...])
        top = None
        for chunk in chunks:
            raw = dot_keys(keys[h, chunk, :], query_h)
            raws[h, chunk, :] = raw
            high = jnp.max(raw, 0, keepdims=True)
            top = high if top is None else jnp.maximum(top, high)
        tops.append(top)
    for h in range(2):
        mass, part = 0.0, 0.0
        for chunk in chunks:
            heavy = jnp.exp(raws[h, chunk, :] - tops[h])
            mass = mass + jnp.sum(heavy, 0, keepdims=True)
            side = values[HD * h : HD * (h + 1), chunk]
            part = part + jnp.dot(side, heavy.astype(BF), preferred_element_type=F32)
        parts.append(part * (1.0 / mass))
        lse_ref[0, h : h + 1, :] = tops[h] + jnp.log(mass)
    mixed = jnp.concatenate(parts, 0).T
    exact_ref[...] = mixed
    out_ref[...] = mixed.astype(BF)


def attend_backward(joined, q_ref, k_ref, v_ref, do_ref, exact_ref, lse_ref, qm_ref, km_ref, *refs):
    outs, (keys, turned_keys, grad_keys, grad_values) = refs[:-4], refs[-4:]
    lane = lax.broadcasted_iota(jnp.int32, (1, 2 * HD), 1) // HD
    pair, step = pl.program_id(0), pl.program_id(1)

    @pl.when(step == 0)
    def _():
        for h in range(2):
            keys[h] = jnp.where(lane == h, k_ref[...], km_ref[...])
        turned_keys[...] = turned(k_ref[...])
        grad_keys[...] = jnp.zeros_like(grad_keys)
        grad_values[...] = jnp.zeros_like(grad_values)

    query = q_ref[...] * jnp.asarray(SCALE, BF)
    grad = do_ref[...]
    spreads = (grad.astype(F32) * exact_ref[...]).T
    of_head = []
    for h in range(2):
        zero = jnp.zeros_like(query)
        of_head.append(
            (
                jnp.where(lane == h, query, qm_ref[...]),
                jnp.where(lane == h, query, zero),
                jnp.where(lane == h, grad, zero),
                jnp.sum(spreads[HD * h : HD * (h + 1)], 0, keepdims=True),
                lse_ref[0, h : h + 1, :],
            )
        )
    parts = []
    for h, (query_m, query_h, grad_h, spread, lse) in enumerate(of_head):
        shares = jnp.exp(dot_keys(keys[h], query_m) - lse)
        grad_raw = (shares * (dot_keys(v_ref[...], grad_h) - spread)).astype(BF)
        side = turned_keys[HD * h : HD * (h + 1), :]
        parts.append(jnp.dot(side, grad_raw, preferred_element_type=F32))
        grad_keys[...] += jnp.dot(grad_raw, query_h, preferred_element_type=F32)
        grad_values[...] += jnp.dot(shares.astype(BF), grad_h, preferred_element_type=F32)
    grad_query = (jnp.concatenate(parts, 0).T * SCALE).astype(BF)
    if joined:
        rows = grad_query.shape[0]
        down = pl.ds(pl.multiple_of(step * rows, rows), rows)
        outs[0][down, pl.ds(pl.multiple_of(pair * 128, 128), 128)] = grad_query
    else:
        outs[0][...] = grad_query

    @pl.when(step == pl.num_programs(1) - 1)
    def _():
        if joined:
            across = pl.num_programs(0)
            for n, total in enumerate((grad_keys, grad_values)):
                place = (pair + across * (n + 1)) * 128
                outs[0][:, pl.ds(pl.multiple_of(place, 128), 128)] = total[...].astype(BF)
        else:
            outs[1][...] = grad_keys[...]
            outs[2][...] = grad_values[...]


def queries_of(count):
    return 1024 if count % 1024 == 0 else tile_of(count)


def tile_of(count):
    return 256 if count % 256 == 0 else count


def mix_tokens(projected, around, mask_q, mask_k):
    nq, nk = projected.shape[0], around.shape[0]
    tile = queries_of(nq)
    rows = lambda part: pl.BlockSpec((tile, 128), lambda i, j: (j, part * PAIRS + i))
    tall = lambda part: pl.BlockSpec((nk, 128), lambda i, j: (0, part * PAIRS + i))
    return pl.pallas_call(
        attend_forward,
        grid=(PAIRS, nq // tile),
        in_specs=[
            rows(0),
            tall(1),
            tall(2),
            pl.BlockSpec((tile, 128), lambda i, j: (j, 0)),
            pl.BlockSpec((nk, 128), lambda i, j: (0, 0)),
        ],
        out_specs=[rows(0), rows(0), pl.BlockSpec((1, 2, tile), lambda i, j: (i, 0, j))],
        out_shape=[
            jax.ShapeDtypeStruct((nq, HALF), BF),
            jax.ShapeDtypeStruct((nq, HALF), F32),
            jax.ShapeDtypeStruct((PAIRS, 2, nq), F32),
        ],
        scratch_shapes=[
            pltpu.VMEM((2, nk, 128), BF),
            pltpu.VMEM((128, nk), BF),
            pltpu.VMEM((2, nk, tile), F32),
        ],
        cost_estimate=cost(nq * nk * HALF, nq * HALF),
        name="attend_forward",
    )(projected, around, around, mask_q, mask_k)


def mix_back(projected, around, grad, exact, lse, mask_q, mask_k):
    nq, nk = projected.shape[0], around.shape[0]
    tile, joined = queries_of(nq), nq == nk
    rows = lambda part: pl.BlockSpec((tile, 128), lambda i, j: (j, part * PAIRS + i))
    tall = lambda part: pl.BlockSpec((nk, 128), lambda i, j: (0, part * PAIRS + i))
    if joined:
        out_specs = [pl.BlockSpec((nq, 3 * HALF), lambda i, j: (0, 0))]
        out_shape = [jax.ShapeDtypeStruct((nq, 3 * HALF), BF)]
    else:
        out_specs = [rows(0), tall(0), tall(0)]
        out_shape = [jax.ShapeDtypeStruct((nq, HALF), BF)]
        out_shape += [jax.ShapeDtypeStruct((nk, HALF), F32)] * 2
    return pl.pallas_call(
        partial(attend_backward, joined),
        grid=(PAIRS, nq // tile),
        in_specs=[
            rows(0),
            tall(1),
            tall(2),
            rows(0),
            rows(0),
            pl.BlockSpec((1, 2, tile), lambda i, j: (i, 0, j)),
            pl.BlockSpec((tile, 128), lambda i, j: (j, 0)),
            pl.BlockSpec((nk, 128), lambda i, j: (0, 0)),
        ],
        out_specs=out_specs,
        out_shape=out_shape,
        scratch_shapes=[
            pltpu.VMEM((2, nk, 128), BF),
            pltpu.VMEM((128, nk), BF),
            pltpu.VMEM((nk, 128), F32),
            pltpu.VMEM((nk, 128), F32),
        ],
        cost_estimate=cost(nq * nk * HALF, nq * HALF),
        name="attend_backward",
    )(projected, around, around, grad, exact, lse, mask_q, mask_k)


def norm_parts(x):
    centre = x - jnp.mean(x, -1, keepdims=True)
    rate = lax.rsqrt(jnp.mean(centre * centre, -1, keepdims=True) + NORM_EPS)
    return (centre * rate, rate)


def layer_norm(x, gain, shift):
    return norm_parts(x)[0] * gain + shift


def norm_back(x, gain, grad):
    unit, rate = norm_parts(x)
    inner_grad = grad * gain
    back = rate * (
        inner_grad
        - jnp.mean(inner_grad, -1, keepdims=True)
        - unit * jnp.mean(inner_grad * unit, -1, keepdims=True)
    )
    return (back, jnp.sum(grad * unit, 0), jnp.sum(grad, 0))


def norm_back_body(x_ref, gain_ref, mine_ref, got_ref, more_ref, kind_ref, out_ref, low_ref, sum_ref):
    grad = mine_ref[...] + got_ref[...]
    back, _, _ = norm_back(x_ref[...], gain_ref[...], grad)
    unit, _ = norm_parts(x_ref[...])
    total = more_ref[...] + back
    out_ref[...] = total
    low_ref[...] = (total * kind_ref[:, :1]).astype(BF)

    @pl.when(pl.program_id(0) == 0)
    def _():
        sum_ref[...] = jnp.zeros_like(sum_ref)

    rows = (grad * unit, grad, total * kind_ref[:, 1:2], total * kind_ref[:, 2:3])
    for n, row in enumerate(rows):
        sum_ref[n : n + 1, :] += jnp.sum(row, 0, keepdims=True)


def norm_back_sum(x, gain, mine, got, more, kinds):
    count = x.shape[0]
    tile = tile_of(count)
    rows = pl.BlockSpec((tile, D), lambda i: (i, 0))
    return pl.pallas_call(
        norm_back_body,
        grid=(count // tile,),
        in_specs=[rows, pl.BlockSpec((1, D), lambda i: (0, 0)), rows, rows, rows]
        + [pl.BlockSpec((tile, 128), lambda i: (i, 0))],
        out_specs=[rows, rows, pl.BlockSpec((8, D), lambda i: (0, 0))],
        out_shape=[
            jax.ShapeDtypeStruct((count, D), F32),
            jax.ShapeDtypeStruct((count, D), BF),
            jax.ShapeDtypeStruct((8, D), F32),
        ],
        cost_estimate=cost(0, count * D),
        name="norm_back",
    )(x, gain[None, :], mine, got, more, kinds)


def matmul(left, right):
    return jnp.dot(left, right, preferred_element_type=F32)


def outer(left, right):
    return lax.dot_general(left, right, (((0,), (0,)), ((), ())), preferred_element_type=F32)


def inner(grad, weight):
    return lax.dot_general(grad, weight, (((1,), (1,)), ((), ())), preferred_element_type=F32)


def chip_bits():
    return [2 << b for b in range((lax.axis_size("seq") // 4 - 1).bit_length())]


def of_bit(value, bit):
    return exchange(value, lambda d, s: (d, s ^ bit))


def row_tokens(value):
    for bit in chip_bits():
        value = jnp.concatenate([value, of_bit(value, bit)], 0)
    return value


def row_return(value):
    for bit in reversed(chip_bits()):
        half = value.shape[0] // 2
        value = value[:half] + of_bit(value[half:].astype(BF), bit).astype(F32)
    return value


def row_sum(value):
    for bit in chip_bits():
        value = value + of_bit(value, bit)
    return value


def segment_lanes(segment, of_query):
    lane = jnp.arange(128, dtype=jnp.int32) % HD
    hit = segment[:, None] == lane[None, :]
    if of_query:
        return jnp.where(hit | (lane > IMGS)[None, :], 0.0, MASKED).astype(BF)
    return hit.astype(BF)


def adamw(weight, mean, square, grad, scale, decay):
    mean_next = BETA_ONE * mean + (1.0 - BETA_ONE) * grad
    square_next = BETA_TWO * square + (1.0 - BETA_TWO) * grad * grad
    mean_hat = mean_next / (1.0 - BETA_ONE**STEP_COUNT)
    square_hat = square_next / (1.0 - BETA_TWO**STEP_COUNT)
    weight_next = weight - BASE_RATE * scale * (
        mean_hat / (jnp.sqrt(square_hat) + ADAM_EPS) + decay * weight
    )
    return (weight_next, mean_next, square_next)


def moments(mean, square, grad):
    return (
        BETA_ONE * mean + (1.0 - BETA_ONE) * grad,
        BETA_TWO * square + (1.0 - BETA_TWO) * grad * grad,
    )


def on_device(
    pixels,
    lengths,
    labels,
    teacher,
    embedder,
    embedder_mean,
    embedder_square,
    attend,
    attend_mean,
    attend_square,
    merger,
    merger_mean,
    merger_square,
    expand,
    expand_mean,
    expand_square,
    shrink,
    shrink_mean,
    shrink_square,
    readout,
    readout_mean,
    readout_square,
    vectors,
    vectors_mean,
    vectors_square,
):
    seq_size, dp_size = lax.axis_size("seq"), lax.axis_size("dp")
    fast = seq_size == 4 and dp_size == 8 and embedder.shape[0] == 24
    seq, core = lax.axis_index("seq"), lax.axis_index("seq") % 2
    local, far = pixels.shape[1], seq_size // 2
    span = seq_size // 4
    classes = readout.shape[2]
    image_count = lengths.shape[0] * dp_size * IMGS

    gather = gather_weights if fast else gather_plain
    embed_w, attend_w, merger_half, expand_w, vector_w, first, cover, later_weights = gather(
        embedder, attend, merger, expand, shrink, readout, vectors
    )

    side = seq // far
    pixels = after(pixels, first)
    pixels_got = of_bit(at(pixels, 1 - side, 0), far)
    tokens = jnp.concatenate([at(pixels, side, 0), pixels_got], 0)
    all_pixels = both_tokens(tokens)
    row_lengths = at(lengths, side, 0)
    row_labels = at(labels, side, 0)
    row_teacher = at(teacher, side, 0)

    def places_of(where):
        step = jnp.arange(local, dtype=jnp.int32)
        return jnp.concatenate([where * local + step, (where ^ far) * local + step])

    places = places_of(seq)
    ends = jnp.cumsum(row_lengths)
    starts = ends - row_lengths

    def segment_of(spots):
        return jnp.sum((spots[:, None] >= ends[None, :]).astype(jnp.int32), 1)

    seg_q = segment_of(jnp.concatenate([places, places_of(seq ^ 1)]))
    order = [0]
    for bit in chip_bits():
        order = order + [o ^ bit for o in order]
    seg_k = segment_of(jnp.concatenate([places_of(seq ^ o ^ k) for o in order for k in range(2)]))
    mask_q, mask_k = segment_lanes(seg_q, True), segment_lanes(seg_k, False)
    marks = jnp.concatenate([starts, starts + 1])
    hits = (marks[:, None] == places[None, :]).astype(F32)
    token_hits = (places[:, None] == marks[None, :]).astype(F32)
    is_cls, is_dist = jnp.sum(hits[:IMGS], 0), jnp.sum(hits[IMGS:], 0)
    is_patch = (seg_q[: 2 * local] < IMGS).astype(F32) - is_cls - is_dist

    merger_w = in_core_order(core, merger_half, swap(merger_half), 1)
    vector_f = vector_w.astype(F32)

    patches = to_tokens(core, matmul(all_pixels, embed_w))
    x = (
        is_patch[:, None] * patches
        + is_cls[:, None] * vector_f[4 * L + 2]
        + is_dist[:, None] * vector_f[4 * L + 3]
    )
    a = both_tokens(layer_norm(x, vector_f[0], vector_f[1]).astype(BF))
    projected = matmul(a, attend_w).astype(BF)
    around = row_tokens(projected)
    mixed_half, exact, lse = mix_tokens(projected, around, mask_q, mask_k)
    mixed_half = after(mixed_half, *cover)
    shrink_w, readout_w, near = later_weights(mixed_half)
    other = swap(mixed_half)
    count = 2 * local
    other = jnp.concatenate([other[count:], other[:count]], 0)
    mixed = in_core_order(core, mixed_half, other, 1)
    x_mid = x + matmul(mixed[:count], merger_w)
    normed = both_tokens(layer_norm(x_mid, vector_f[2], vector_f[3]).astype(BF))
    hidden_in = matmul(after(normed, near), expand_w)
    cdf = 0.5 * (1.0 + lax.erf(hidden_in * (0.5**0.5)))
    hidden = (hidden_in * cdf).astype(BF)
    slope = cdf + hidden_in * jnp.exp(-0.5 * hidden_in * hidden_in) * ((0.5 / jnp.pi) ** 0.5)
    mine, got = with_other(matmul(hidden, shrink_w))
    x_last = x_mid + (mine[:count] + got)

    label_hot = (row_labels[:, None] == jnp.arange(classes, dtype=jnp.int32)).astype(F32)
    teach_log = jax.nn.log_softmax(row_teacher, -1)
    target = jnp.where(core == 0, label_hot, jnp.exp(teach_log))
    target_log = jnp.where(core == 0, 0.0, teach_log)
    gain, shift = vector_f[4 * L], vector_f[4 * L + 1]
    rows = row_sum(jnp.dot(hits, x_last, precision=HIGH)).reshape(2, IMGS, D)
    rows = at(rows, core, 0) + swap(at(rows, 1 - core, 0))
    unit, rate = norm_parts(rows)
    head_in = (unit * gain + shift).astype(BF)
    logits = matmul(head_in, readout_w)[:, :classes]
    log_share = jax.nn.log_softmax(logits, -1)
    loss_local = jnp.sum(0.5 * target * (target_log - log_share)) / span
    grad_logits = pad_lanes(
        0.5 * (jnp.exp(log_share) - target) / image_count, readout_w.shape[1]
    )
    grad_readout = lax.dot_general(
        head_in.astype(F32), grad_logits / span, (((0,), (0,)), ((), ())), precision=HIGH
    )
    grad_head = lax.dot_general(
        grad_logits, readout_w.astype(F32), (((1,), (1,)), ((), ())), precision=HIGH
    )
    head_back, gain_out, shift_out = norm_back(rows, gain, grad_head)
    back = in_core_order(core, head_back, swap(head_back), 0)

    grad_out = jnp.dot(token_hits, back, precision=HIGH)
    grad_branch = both_tokens(grad_out.astype(BF))
    grad_shrink = outer(hidden, grad_branch).astype(BF)
    grad_readout = grad_readout.astype(BF)
    if fast:
        parts = [blocks(grad_shrink), blocks(grad_readout)]
        unit_rows = parts[1].shape[3]
        first = scatter_give(parts, unit_rows)
    grad_pre = (inner(grad_branch, shrink_w) * slope).astype(BF)
    grad_expand = outer(normed, grad_pre).astype(BF)
    mine, got = with_other(inner(grad_pre, expand_w))
    kinds = jnp.stack([is_patch, is_cls, is_dist], 1)
    kinds = jnp.pad(kinds, ((0, 0), (0, 125)))
    every = jnp.ones_like(kinds)
    grad_mid, low_mid, sums_two = norm_back_sum(x_mid, vector_f[2], mine, got, grad_out, every)
    grad_attn = both_tokens(low_mid)
    attn_half = at(grad_attn.reshape(-1, 2, HALF), core, 1)
    grad_merger = outer(mixed, attn_half).astype(BF)
    if fast:
        second = scatter_give([blocks(grad_expand), blocks(grad_merger)], unit_rows)
    grad_mixed = inner(grad_attn, at(merger_w.reshape(2, HALF, D), core, 0)).astype(BF)
    if fast:
        first = scatter_near(first, second[3])
        grad_mixed = after(grad_mixed, first[0])
    grads = mix_back(projected, around, grad_mixed, exact, lse, mask_q, mask_k)
    if len(grads) == 1:
        grad_proj = grads[0]
    else:
        grad_proj = jnp.concatenate([grads[0]] + [row_return(g).astype(BF) for g in grads[1:]], 1)
    if fast:
        grad_proj = after(grad_proj, first[1], second[2])
    mine, got = with_other(inner(grad_proj, attend_w))
    grad_attend = outer(a, grad_proj).astype(BF)
    if fast:
        third = scatter_give([blocks(grad_attend)], unit_rows)
        first = scatter_column(first, third[3])
        second = scatter_near(second, first[0])
    _, grad_patch, sums_one = norm_back_sum(x, vector_f[0], mine, got, grad_mid, kinds)
    grad_embed = outer(all_pixels, to_columns(core, grad_patch)).astype(BF)
    grad_vectors = jnp.concatenate(
        [sums_one[:2], sums_two[:2], jnp.stack([gain_out, shift_out]) / span, sums_one[2:4]], 0
    )
    grad_vectors = grad_vectors + swap(grad_vectors)
    if fast:
        parts = [blocks(grad_embed)]
        fourth = scatter_give(parts + [vector_blocks(grad_vectors, parts[0])], unit_rows)
        third = scatter_near(third, grad_embed)
        second = scatter_column(second, grad_embed)
        fourth = scatter_near(fourth)
        first = scatter_pair(first, fourth[0])
        third = scatter_column(third)
        fourth = scatter_column(fourth)
        second = scatter_pair(second, fourth[0])
        third, fourth = scatter_pair(third), scatter_pair(fourth)
        units = [scatter_end(state) for state in (first, second, third, fourth)]
        tall, thin = vectors.shape
        sum_vectors = at(units[3][:tall, HALF : HALF + 2 * thin].reshape(tall, 2, thin), core, 1)
        squares_of = units[:3] + [units[3][:, :HALF], sum_vectors]
        sum_shrink, sum_readout = first_done(units[0], classes)
        sum_expand, sum_merger = second_done(units[1], grad_expand.shape[1])
        sum_embed, sum_attend = last_done(units[2], units[3])
    else:
        sum_embed, sum_attend, sum_merger, sum_expand, sum_shrink, sum_readout, sum_vectors = (
            scatter_plain(
                (grad_embed, grad_attend, grad_merger, grad_expand)
                + (grad_shrink, grad_readout, grad_vectors),
                classes,
            )
        )
        squares_of = [sum_embed, sum_attend, sum_merger, sum_expand, sum_shrink, sum_readout]
        squares_of.append(sum_vectors)
    reduced = (sum_embed, sum_attend, sum_merger, sum_expand, sum_shrink, sum_readout)
    square_sum = sum((jnp.sum(g * g) for g in squares_of))
    beside = [(sum_shrink, sum_readout), (sum_expand,), (sum_merger, sum_embed), (sum_attend,)]
    both = total_of(jnp.stack([square_sum, loss_local])[None, :], beside)
    grad_norm = jnp.sqrt(both[0, 0])
    factor = jnp.minimum(1.0, CLIP_AT / (grad_norm + 1e-06))

    masters = (embedder, attend, merger, expand, shrink, readout)
    means = (embedder_mean, attend_mean, merger_mean, expand_mean, shrink_mean, readout_mean)
    squares = (
        embedder_square,
        attend_square,
        merger_square,
        expand_square,
        shrink_square,
        readout_square,
    )
    outs = []
    for j in range(6):
        grad = reduced[j].reshape(masters[j].shape) * factor
        outs += adamw(masters[j], means[j], squares[j], grad, RATES[j], DECAY)
    outs += moments(vectors_mean, vectors_square, sum_vectors * factor)
    return tuple(outs) + (both[0, 1] / image_count, grad_norm)


def solution(mesh):
    return jax.shard_map(
        on_device,
        mesh=mesh,
        in_specs=(
            P("dp", "seq", None),
            P("dp", None),
            P("dp", None),
            P("dp", None, None),
            P(("dp", "seq"), None),
            P(("dp", "seq"), None),
            P(("dp", "seq"), None),
            P(None, ("dp", "seq"), None),
            P(None, ("dp", "seq"), None),
            P(None, ("dp", "seq"), None),
            P(None, ("dp", "seq"), None),
            P(None, ("dp", "seq"), None),
            P(None, ("dp", "seq"), None),
            P(None, ("dp", "seq"), None),
            P(None, ("dp", "seq"), None),
            P(None, ("dp", "seq"), None),
            P(None, ("dp", "seq"), None),
            P(None, ("dp", "seq"), None),
            P(None, ("dp", "seq"), None),
            P(None, ("dp", "seq"), None),
            P(None, ("dp", "seq"), None),
            P(None, ("dp", "seq"), None),
            P(None, ("dp", "seq")),
            P(None, ("dp", "seq")),
            P(None, ("dp", "seq")),
        ),
        out_specs=(
            P(("dp", "seq"), None),
            P(("dp", "seq"), None),
            P(("dp", "seq"), None),
            P(None, ("dp", "seq"), None),
            P(None, ("dp", "seq"), None),
            P(None, ("dp", "seq"), None),
            P(None, ("dp", "seq"), None),
            P(None, ("dp", "seq"), None),
            P(None, ("dp", "seq"), None),
            P(None, ("dp", "seq"), None),
            P(None, ("dp", "seq"), None),
            P(None, ("dp", "seq"), None),
            P(None, ("dp", "seq"), None),
            P(None, ("dp", "seq"), None),
            P(None, ("dp", "seq"), None),
            P(None, ("dp", "seq"), None),
            P(None, ("dp", "seq"), None),
            P(None, ("dp", "seq"), None),
            P(None, ("dp", "seq")),
            P(None, ("dp", "seq")),
            P(),
            P(),
        ),
        check_vma=False,
    )
```
